128 devices in a mesh: wide: 32 (over y_hi, z, x), four: 4 (over y_lo, core).
Axes of the slice: x: 4, y: 4 (y_hi: 2, y_lo: 2; y = y_hi * 2 + y_lo), z: 4, core: 2. Of those that a mesh axis runs over, the one named last changes fastest.
Arguments:
- voltage: float32 [512, 128, 128], P('wide', 'four'), may hold values from -4 to 4
- states: float32 [20, 512, 128, 128], P(None, 'wide', 'four'), may hold values from 0 to 1
- half_volt: float32 [20], replicated, may hold values from -1 to 1
- gate_slope: float32 [20], replicated, may hold values from 0.2 to 1
- retention: float32 [20], replicated, may hold values from 0.5 to 0.98
- conduct: float32 [20], replicated, may hold values from 0.02 to 0.3
- reversal: float32 [20], replicated, may hold values from -1.5 to 1.5
- tension_weights: float32 [20], replicated, may hold values from -2 to 2
- routes: int32 [131072, 1], P(('wide', 'four')), may hold values from 0 to 127; in each aligned block of 1024 rows (0 to 1023, 1024 to 2047, ...) at most 16 rows name the same one
- base_stiff: float32 [131072], P(('wide', 'four')), may hold values from 0.5 to 2
- elem_nodes: int32 [8, 262144], P(None, ('wide', 'four')), may hold values from 0 to 1023
- share_perm: int32 [128, 128], P(('wide', 'four')), may hold values from 0 to 127, each once within a row
- stiffness: float32 [24, 24], replicated, as said below
- force_map: float32 [24, 8], replicated, may hold values from -2 to 2
- strain_map: float32 [8, 24], replicated, may hold values from -3 to 3
Outputs:
- potential: float32 [512, 128, 128], P('wide', 'four')
- final_states: float32 [20, 512, 128, 128], P(None, 'wide', 'four')
- displacement: float32 [3, 131072], P(None, ('wide', 'four'))
The draws below stay inside these ranges and needn't reach their ends.
Inputs may be any that keep to these rules, and one draw needn't show every extreme that they name: routes[g, 0] is the device that owns block g's coarse element; among the 1024 blocks of one device at most 16 name the same owner. `elem_nodes`: node numbers on the device that holds the slot. `share_perm`: each row is a permutation; row 0 is not used. `stiffness`: symmetric.
All inputs are finite; a program needn't handle non-finite values.
Results may differ from the reference program's by a relative error of at most 0.0003.
Values sent between devices are 32-bit elements; how exact they have to be, the bound alone decides.
A program may use at most 128 MiB of HBM per device.

```python
import math
import jax
import jax.numpy as jnp
import numpy as np
from jax import lax

NSTATE = 20
CX = 16
CY = 32
CZ = 128
BE = 4
STEPS = 4
NX = 512
NY = 128
NZ = 128
NB = 1024
MOST = 16
SLOTS = 2048
NODE_DEV = 1024
SHARE = 128
N_WIDE = 32
N_FOUR = 4
DEVICES = 128


def draw_stiffness(key, part):
    first_key, second_key = jax.random.split(jax.random.fold_in(key, 7))
    noise = jax.random.normal(first_key, (24, 24), jnp.float32) * 0.08
    noise = (noise + noise.T) * (1.0 - jnp.eye(24, dtype=jnp.float32))
    center = jax.random.uniform(second_key, (24,), jnp.float32, 3.0, 4.0)
    return noise + jnp.diag(center)


def place_ends(result, stream_key, least, high):
    extent = result.shape
    spot = [jax.random.randint(jax.random.fold_in(stream_key, axis), (), 0, extent[axis]) for axis in range(len(extent))]
    result = result.at[tuple(spot)].set(least)
    longest = extent.index(max(extent))
    spot[longest] = (spot[longest] + 1) % extent[longest]
    return result.at[tuple(spot)].set(high)


def level_of(rng, shape, pieces, least, largest):
    loudness, own = 1.0, jax.random.fold_in(rng, 6)
    for dim, shards_of in pieces:
        draws = jnp.exp(jax.random.uniform(jax.random.fold_in(own, dim), (shards_of,), jnp.float32, least / len(pieces), largest / len(pieces)))
        loudness = loudness * jnp.repeat(draws, shape[dim] // shards_of).reshape([-1 if axis == dim else 1 for axis in range(len(shape))])
    return loudness


def shared_out(rng, own, number, rows, amount, top, most, slope):
    sequence = jax.random.permutation(rng, amount)
    packed, ordinary = load_shares(amount, rows * top, most, slope, True), load_shares(amount, rows * top, most, slope, False)
    places = jnp.arange(amount)

    def named(tallies, offset_by):
        used = int((tallies > 0).sum())
        fixed = max(1, used // 4)
        passed = fixed + (places - fixed + offset_by * (used - fixed)) % max(1, amount - fixed)
        return jnp.zeros((amount,), jnp.int32).at[sequence[jnp.where(places < fixed, places, passed)]].set(jnp.asarray(tallies, jnp.int32))

    tallies = jnp.where(number % 4 == 0, named(packed, number // 4), named(ordinary, number - number // 4 - 1))
    mixed = jax.random.permutation(jax.random.fold_in(own, 3), amount)
    source_of, receiver = mixed[0:amount // 2 * 2:2], mixed[1:amount // 2 * 2:2]
    slack = jnp.minimum(tallies[source_of] - 1, most - tallies[receiver]) // 2
    slack = jnp.where((source_of == sequence[0]) | (receiver == sequence[0]) | (tallies[receiver] == 0), 0, jnp.maximum(slack, 0))
    passed = jax.random.randint(jax.random.fold_in(own, 4), (amount // 2,), 0, 1 << 20) % (slack + 1)
    tallies = tallies.at[source_of].add(-passed).at[receiver].add(passed)
    members = jnp.searchsorted(jnp.cumsum(tallies), jnp.arange(rows * top), side="right").astype(jnp.int32)
    grid = members.reshape(top, rows).T
    grid = grid[jax.random.permutation(jax.random.fold_in(own, 1), rows)]
    offset_by = jax.random.randint(jax.random.fold_in(own, 2), (rows, 1), 0, top)
    return jnp.take_along_axis(grid, (jnp.arange(top)[None, :] + offset_by) % top, axis=1)


def load_shares(count, total, reach, skew, full):
    loads = [(1 << 20) // math.isqrt(grade ** skew) + 1 for grade in range(1, count + 1)]
    largest = reach if full else min(reach, max(-(-total // count), total * loads[0] // sum(loads)))
    least = 1 if total - largest >= count - 1 else 0
    given, rest = [largest] + [least] * (count - 1), total - largest - least * (count - 1)
    while rest > 0:
        free = [i for i in range(1, count) if given[i] < largest] or [i for i in range(1, count) if given[i] < reach]
        whole, budget = sum([loads[i] for i in free]), rest
        for i in free:
            extra = min(reach - given[i], max(1, budget * loads[i] // whole), rest)
            given[i] = given[i] + extra
            rest = rest - extra
    return np.array(given)


def normal_values(rng, dims, deviation, limit, shards=(), kind=jnp.bfloat16):
    array = deviation * jax.random.normal(rng, dims, jnp.float32)
    if shards:
        array = array * level_of(rng, dims, shards, -0.22, 0.18)
    return jnp.clip(array, -limit, limit).astype(kind)


def setup_inputs(seed: int = 0) -> dict:
    keys = jax.random.split(jax.random.key(seed), 16)
    voltage = normal_values(keys[0], (NX, NY, NZ), 1.0, 4.0, ((0, 32), (1, 4)), jnp.float32)
    states = jnp.clip(1.0 * jax.random.uniform(keys[1], (NSTATE, NX, NY, NZ), jnp.float32) ** level_of(keys[1], (NSTATE, NX, NY, NZ), ((1, 32), (2, 4)), -0.2, 0.2), 0.0, 1.0)
    half_volt = jnp.clip(jax.random.uniform(keys[2], (NSTATE,), jnp.float32, -1.0, 1.0), -1.0, 1.0)
    gate_slope = jnp.clip(jnp.exp(jax.random.uniform(keys[3], (NSTATE,), jnp.float32, math.log(0.2), math.log(1.0))), 0.2, 1.0)
    retention = jnp.clip(jnp.exp(jax.random.uniform(keys[4], (NSTATE,), jnp.float32, math.log(0.5), math.log(0.98))), 0.5, 0.98)
    conduct = jnp.clip(jnp.exp(jax.random.uniform(keys[5], (NSTATE,), jnp.float32, math.log(0.02), math.log(0.3))), 0.02, 0.3)
    reversal = jnp.clip(jax.random.uniform(keys[6], (NSTATE,), jnp.float32, -1.5, 1.5), -1.5, 1.5)
    tension_weights = normal_values(keys[7], (NSTATE,), 0.4, 2.0, (), jnp.float32)
    routes_keys = jax.random.split(jax.random.fold_in(keys[8], 1), (DEVICES * NB) // NB)
    routes_turns = jax.random.permutation(jax.random.fold_in(keys[8], 3), (DEVICES * NB) // NB)
    routes = jax.vmap(lambda own, number: shared_out(jax.random.fold_in(keys[8], 2), own, number, NB, DEVICES, 1, MOST, 2))(routes_keys, routes_turns).reshape((DEVICES * NB, 1))
    base_stiff = jnp.clip(jnp.exp(math.log(2.0) - 1.3862944 * jax.random.uniform(keys[9], (DEVICES * NB,), jnp.float32) ** level_of(keys[9], (DEVICES * NB,), ((0, 128),), -0.2, 0.2)), 0.5, 2.0)
    elem_nodes = place_ends(jax.random.randint(keys[10], (8, DEVICES * SLOTS), 0, NODE_DEV), jax.random.fold_in(keys[10], 1), 0, NODE_DEV - 1).astype(jnp.int32)
    share_perm = jax.vmap(lambda own: jax.random.permutation(own, SHARE))(jax.random.split(keys[11], DEVICES)).reshape((DEVICES, SHARE)).astype(jnp.int32)
    stiffness = draw_stiffness(jax.random.fold_in(keys[15], 71), 0)
    force_map = normal_values(keys[13], (24, 8), 8 ** -0.5, 2.0, (), jnp.float32)
    strain_map = normal_values(keys[14], (8, 24), 0.5, 3.0, (), jnp.float32)
    return dict(voltage=voltage, states=states, half_volt=half_volt, gate_slope=gate_slope, retention=retention, conduct=conduct, reversal=reversal, tension_weights=tension_weights, routes=routes, base_stiff=base_stiff, elem_nodes=elem_nodes, share_perm=share_perm, stiffness=stiffness, force_map=force_map, strain_map=strain_map)


TIME_STEP = 0.1
DIFFUSE_X = 1.5
DIFFUSE_Y = 1.0
DIFFUSE_Z = 0.6
STRETCH_GAIN = 2.0
STRETCH_REVERSAL = 0.5
SPRING = 1.0
RELAX = 0.7
PRECISE = lax.Precision.HIGHEST


def laplace(potential):
    padded = jnp.pad(potential, 1, mode="edge")
    center = padded[1:-1, 1:-1, 1:-1]
    along_x = padded[2:, 1:-1, 1:-1] + padded[:-2, 1:-1, 1:-1] - 2.0 * center
    along_y = padded[1:-1, 2:, 1:-1] + padded[1:-1, :-2, 1:-1] - 2.0 * center
    along_z = padded[1:-1, 1:-1, 2:] + padded[1:-1, 1:-1, :-2] - 2.0 * center
    return DIFFUSE_X * along_x + DIFFUSE_Y * along_y + DIFFUSE_Z * along_z


def advance(potential, states, excess, params):
    half_volt, gate_slope, retention, conduct, reversal = params
    current = STRETCH_GAIN * excess * (potential - STRETCH_REVERSAL)
    renewed = []
    for channel in range(states.shape[0]):
        gating = jax.nn.sigmoid((potential - half_volt[channel]) / gate_slope[channel])
        fresh = gating + (states[channel] - gating) * retention[channel]
        current = current + conduct[channel] * fresh * (potential - reversal[channel])
        renewed.append(fresh)
    potential = potential + TIME_STEP * (laplace(potential) - current)
    return potential, jnp.stack(renewed)


def corner_weights(edge):
    place = (jnp.arange(edge, dtype=jnp.float32) + 0.5) / edge
    return jnp.stack([1.0 - place, place], axis=1)


def to_blocks(field):
    shaped = field.reshape(N_WIDE, CX // BE, BE, N_FOUR, CY // BE, BE, CZ // BE, BE)
    shaped = shaped.transpose(0, 3, 1, 4, 6, 2, 5, 7)
    return shaped.reshape(N_WIDE * N_FOUR * NB, BE ** 3)


def from_blocks(rows_in):
    shaped = rows_in.reshape(N_WIDE, N_FOUR, CX // BE, CY // BE, CZ // BE, BE, BE, BE)
    shaped = shaped.transpose(0, 2, 5, 1, 3, 6, 4, 7)
    return shaped.reshape(NX, NY, NZ)


def slot_index(routes):
    target = routes[:, 0].reshape(DEVICES, NB)
    owners = jnp.arange(DEVICES, dtype=jnp.int32)
    onehot = (target[:, :, None] == owners[None, None, :]).astype(jnp.int32)
    before = (jnp.cumsum(onehot, axis=1, dtype=jnp.int32) - onehot).astype(jnp.int32)
    position = jnp.sum(before * onehot, axis=2, dtype=jnp.int32).astype(jnp.int32)
    source = jnp.arange(DEVICES, dtype=jnp.int32)[:, None]
    return (target * SLOTS + source * MOST + position).reshape(DEVICES * NB).astype(jnp.int32)


def collect(field, nodes):
    return field[:, nodes].reshape(24, nodes.shape[1])


def spread(values, nodes, count):
    return jnp.zeros((3, count), values.dtype).at[:, nodes].add(values.reshape(3, 8, nodes.shape[1]))


def assemble(local, share_perm):
    width = local.shape[0]
    shaped = local.reshape(width, DEVICES, NODE_DEV)
    leading = shaped[:, 1:, :SHARE]
    order = jnp.arange(DEVICES - 1, dtype=jnp.int32)[:, None]
    pairing = share_perm[1:].astype(jnp.int32)
    moved = jnp.zeros((width, DEVICES - 1, SHARE), local.dtype).at[:, order, pairing].set(leading)
    trailing = shaped[:, :-1, NODE_DEV - SHARE:] + moved
    shaped = shaped.at[:, :-1, NODE_DEV - SHARE:].set(trailing)
    picks = jnp.broadcast_to(pairing[None], (width, DEVICES - 1, SHARE))
    shaped = shaped.at[:, 1:, :SHARE].set(jnp.take_along_axis(trailing, picks, axis=2))
    return shaped.reshape(width, DEVICES * NODE_DEV)


def reference(voltage, states, half_volt, gate_slope, retention, conduct, reversal, tension_weights, routes, base_stiff, elem_nodes, share_perm, stiffness, force_map, strain_map):
    params = (half_volt, gate_slope, retention, conduct, reversal)
    potential = voltage
    for repeat in range(STEPS):
        potential, states = advance(potential, states, 0.0, params)
    tension = states[0] * tension_weights[0]
    for channel in range(1, states.shape[0]):
        tension = tension + states[channel] * tension_weights[channel]
    weights = corner_weights(BE)
    table = jnp.einsum("ix,jy,kz->ijkxyz", weights, weights, weights, precision=PRECISE).reshape(BE ** 3, 8)
    blocks = to_blocks(tension)
    corner = jnp.dot(table.T, blocks.T, precision=PRECISE) / (BE / 2.0) ** 3
    position = slot_index(routes)
    total_slots = DEVICES * SLOTS
    corner_slot = jnp.zeros((8, total_slots), corner.dtype).at[:, position].set(corner)
    base_slot = jnp.zeros((total_slots,), base_stiff.dtype).at[position].set(base_stiff)
    offset = (jnp.arange(total_slots, dtype=jnp.int32) // SLOTS) * NODE_DEV
    nodes = (elem_nodes + offset[None, :]).astype(jnp.int32)
    element_stiff = base_slot * (1.0 + 0.5 * jnp.tanh(jnp.mean(corner_slot, axis=0)))
    node_count = DEVICES * NODE_DEV
    forces = assemble(spread(jnp.dot(force_map, corner_slot, precision=PRECISE), nodes, node_count), share_perm)
    diag_terms = element_stiff[None, :] * jnp.diagonal(stiffness)[:, None]
    diagonal = SPRING + assemble(spread(diag_terms, nodes, node_count), share_perm)
    guess = RELAX * forces / diagonal
    pushed = element_stiff[None, :] * jnp.dot(stiffness, collect(guess, nodes), precision=PRECISE)
    applied = SPRING * guess + assemble(spread(pushed, nodes, node_count), share_perm)
    displacement = guess + RELAX * (forces - applied) / diagonal
    strain = jnp.dot(strain_map, collect(displacement, nodes), precision=PRECISE)
    picked = strain[:, position]
    excess = from_blocks(jnp.dot(table, picked, precision=PRECISE).T)
    for repeat in range(STEPS):
        potential, states = advance(potential, states, excess, params)
    return potential, states, displacement
```

```python
import functools

import jax
import jax.numpy as jnp
from jax import lax
from jax.experimental import pallas as pl
from jax.experimental.pallas import tpu as pltpu
from jax.sharding import PartitionSpec as P

BE = 4
NK = 20
PX, PY, PZ = 16, 32, 128
NROW = 8
LANES = 128
MOST = 16
F32, BF16 = jnp.float32, jnp.bfloat16
DT = 0.1
DX, DY, DZ = 1.5, 1.0, 0.6
GAIN, STRETCH_REV = 2.0, 0.5
SPRING, RELAX = 1.0, 0.7
GROUPS = 4
GP = PX // GROUPS
MESH = pl.DeviceIdType.MESH
NN = (((1,), (0,)), ((), ()))
NT = (((1,), (1,)), ((), ()))


def dot(a, b, dims=NN):
    return lax.dot_general(a, b, dims, preferred_element_type=F32)


def split2(x):
    high = x.astype(BF16)
    return high, (x - high.astype(F32)).astype(BF16)


def iota(shape, dim):
    return lax.broadcasted_iota(jnp.int32, shape, dim)


def corner_of(j):
    return 4 * ((j // 2) % 2) + 2 * (j % 2) + j // 4


def corner_weight(i, side):
    place = (i.astype(F32) + 0.5) * (1.0 / BE)
    return jnp.where(side == 1, place, 1.0 - place)


def kernel(
    n_wide,
    n_four,
    par,
    volt,
    states_in,
    routes,
    base,
    nodes,
    perm,
    stiff,
    fmap,
    smap,
    pot_out,
    states_out,
    disp_out,
    ust,
    vb,
    xh,
    yh,
    yf,
    ex,
    tens,
    tbuf,
    posb,
    lhi,
    llo,
    onehot,
    abuf,
    vsp,
    nlo,
    nhi,
    kf,
    ks,
    kt,
    dvec,
    wz,
    k8b,
    txb,
    vals,
    ndb,
    asm_s,
    asm_r,
    snd,
    rcv,
    dma_in,
    dma_out,
    hs,
    hr,
    a2s,
    a2r,
    ass,
    asr,
):
    count = n_wide * n_four
    wide = lax.axis_index("wide")
    four = lax.axis_index("four")
    me = wide * n_four + four
    barrier = pltpu.get_barrier_semaphore()

    def greet(i, c):
        t = lax.rem(me + i, count)
        pl.semaphore_signal(barrier, inc=1, device_id=(t // n_four, lax.rem(t, n_four)), device_id_type=MESH)
        return c

    lax.fori_loop(1, count, greet, 0)

    def load_group(g):
        part = pl.ds(g * GP, GP)
        return pltpu.make_async_copy(states_in.at[:, part], ust.at[:, part], dma_in.at[g])

    for g in range(GROUPS):
        load_group(g).start()

    tri = jnp.where((iota((LANES, 256), 0) < iota((LANES, 256), 1)), 1.0, 0.0).astype(BF16)
    carry = jnp.zeros((count, LANES), F32)
    for r in range(NROW):
        hot = jnp.broadcast_to(routes[r : r + 1, :], (count, LANES)) == iota((count, LANES), 0)
        hot_f = jnp.where(hot, 1.0, 0.0)
        hot_b = hot_f.astype(BF16)
        tbuf[:, r * LANES : (r + 1) * LANES] = hot_b
        run = dot(hot_b, tri)
        before = run[:, :LANES] + carry
        carry = carry + run[:, LANES:]
        posb[r : r + 1, :] = jnp.sum(before * hot_f, axis=0, keepdims=True).astype(jnp.int32)

    slot_row = lax.rem(iota((LANES, LANES), 0), MOST)

    def here(r):
        return jnp.broadcast_to(posb[r : r + 1, :], (LANES, LANES)) == slot_row

    def placed():
        return dot(tbuf[...], lhi[...], NT) + dot(tbuf[...], llo[...], NT)

    for r in range(NROW):
        row = jnp.broadcast_to(base[r : r + 1, :], (LANES, LANES))
        h, l = split2(jnp.where(here(r), row, 0.0))
        lhi[:, r * LANES : (r + 1) * LANES] = h
        llo[:, r * LANES : (r + 1) * LANES] = l
    snd[0] = placed().reshape(count, 1, LANES)

    has = (wide > 0, wide < n_wide - 1, four > 0, four < n_four - 1)
    opposite = (1, 0, 3, 2)
    peers = ((wide - 1, four), (wide + 1, four), (wide, four - 1), (wide, four + 1))

    def field(n):
        return volt if n == 0 else vb.at[n - 1]

    def halo(n, d):
        v = field(n)
        src = (v.at[0], v.at[PX - 1], yf.at[n, 0], yf.at[n, 1])[d]
        dst = (xh.at[n, 1], xh.at[n, 0], yh.at[n, 1], yh.at[n, 0])[d]
        return pltpu.make_async_remote_copy(
            src_ref=src,
            dst_ref=dst,
            send_sem=hs.at[n, d],
            recv_sem=hr.at[n, d],
            device_id=peers[d],
            device_id_type=MESH,
        )

    def start_halo(n):
        v = field(n)
        yf[n, 0] = v[:, 0, :]
        yf[n, 1] = v[:, PY - 1, :]
        for d in range(4):

            @pl.when(has[d])
            def _():
                halo(n, d).start()

    def finish_halo(n):
        v, w = field(n), vb.at[n]

        for d in range(4):

            @pl.when(has[opposite[d]])
            def _():
                halo(n, d).wait_recv()
                if d == 0:
                    w[PX - 1] = w[PX - 1] + (DT * DX) * (xh[n, 1] - v[PX - 1])
                elif d == 1:
                    w[0] = w[0] + (DT * DX) * (xh[n, 0] - v[0])
                elif d == 2:
                    w[:, PY - 1, :] = w[:, PY - 1, :] + (DT * DY) * (yh[n, 1] - v[:, PY - 1, :])
                else:
                    w[:, 0, :] = w[:, 0, :] + (DT * DY) * (yh[n, 0] - v[:, 0, :])

    def finish_sends(n):
        for d in range(4):

            @pl.when(has[d])
            def _():
                halo(n, d).wait_send()

    lane = iota((PY, PZ), 1)
    const_a, const_b, const_t = par[9, 0], par[9, 1], par[9, 2]

    def planes(n, first, last, with_excess=False, opening=False, tension=False, closing=False):
        v_ref, w_ref = field(n), vb.at[n]

        def body(i, c):
            v = v_ref[i]
            total_a = jnp.zeros((PY, PZ), F32)
            total_b = jnp.zeros((PY, PZ), F32)
            total_t = jnp.zeros((PY, PZ), F32)
            for k in range(NK):
                t = jnp.tanh(v * par[0, k] + par[1, k])
                if opening:
                    u = ust[k, i] * par[5, k] + (t * par[3, k] + par[6, k])
                else:
                    u = ust[k, i] * par[2, k] + t * par[3, k]
                ust[k, i] = u * par[7, k] + 0.5 if closing else u
                total_a = total_a + u
                total_b = total_b + u * par[4, k]
                if tension:
                    total_t = total_t + u * par[8, k]
            current = v * (total_a + const_a) - (total_b + const_b)
            if with_excess:
                current = current + GAIN * ex[i] * (v - STRETCH_REV)
            if tension:
                tens[i] = total_t + const_t
            near_x = v_ref[jnp.maximum(i - 1, 0)] + v_ref[jnp.minimum(i + 1, PX - 1)]
            near_y = jnp.concatenate([v[:1], v[:-1]], 0) + jnp.concatenate([v[1:], v[-1:]], 0)
            near_z = jnp.where(lane == 0, v, pltpu.roll(v, 1, 1)) + jnp.where(
                lane == PZ - 1, v, pltpu.roll(v, PZ - 1, 1)
            )
            lap = DX * near_x + DY * near_y + DZ * near_z - (2.0 * (DX + DY + DZ)) * v
            w_ref[i] = v + DT * (lap - current)
            return c

        lax.fori_loop(first, last, body, 0)

    def row_copy(s, t):
        return pltpu.make_async_remote_copy(
            src_ref=snd.at[s, t],
            dst_ref=rcv.at[s, me],
            send_sem=a2s.at[s],
            recv_sem=a2r.at[s],
            device_id=(t // n_four, lax.rem(t, n_four)),
            device_id_type=MESH,
        )

    def send_rows(s):
        def one(i, c):
            row_copy(s, lax.rem(me + i, count)).start()
            return c

        lax.fori_loop(1, count, one, 0)
        rcv[s, me] = snd[s, me]

    def wait_rows(s):
        part = rcv.at[s, pl.ds(0, count - 1)]
        pltpu.make_async_copy(part, part, a2r.at[s]).wait()

    def wait_sent(s):
        part = snd.at[s, pl.ds(0, count - 1)]
        pltpu.make_async_copy(part, part, a2s.at[s]).wait()

    def received(s):
        return rcv[s].reshape(count, LANES)

    for g in range(GROUPS):
        load_group(g).wait()
        planes(0, g * GP, (g + 1) * GP, opening=True)

    pl.semaphore_wait(barrier, count - 1)
    start_halo(0)
    send_rows(0)

    nlo[...] = lax.rem(nodes[...], LANES)
    nhi[...] = nodes[...] // LANES

    def hot_chunk(ch, c):
        for j in range(16):
            row = nlo[pl.ds(ch * 16 + j, 1), :]
            hit = jnp.broadcast_to(row, (LANES, LANES)) == iota((LANES, LANES), 0)
            onehot[ch, :, j * LANES : (j + 1) * LANES] = jnp.where(hit, 1.0, 0.0).astype(BF16)
        return c

    finish_halo(0)
    start_halo(1)
    planes(1, 0, PX)
    lax.fori_loop(0, 8, hot_chunk, 0)
    finish_halo(1)
    start_halo(2)
    planes(2, 0, PX)

    rd = jnp.where(iota((24, 384), 0) == iota((24, 384), 1) // MOST, 1.0, 0.0).astype(BF16)
    rdt = jnp.where(iota((384, 24), 1) == iota((384, 24), 0) // MOST, 1.0, 0.0).astype(BF16)
    rj = jnp.where(iota((LANES, 8), 1) == corner_of(iota((LANES, 8), 0) // MOST), 1.0, 0.0).astype(BF16)
    rjt = jnp.where(iota((8, LANES), 0) == corner_of(iota((8, LANES), 1) // MOST), 1.0, 0.0).astype(BF16)

    def kron(left, part, right, rows, cols):
        full = dot(dot(left, part, NT).astype(BF16), right)
        same = lax.rem(iota((rows, cols), 0), MOST) == lax.rem(iota((rows, cols), 1), MOST)
        return jnp.where(same, full, 0.0).astype(BF16)

    for s, part in enumerate(split2(fmap[...])):
        kf[s] = kron(rj, part, rd, LANES, 384)
    for s, part in enumerate(split2(stiff[...])):
        ks[s] = kron(rdt, part, rd, 384, 384)
    for s, part in enumerate(split2(smap[...])):
        kt[s] = kron(rdt, part, rjt, 384, LANES)
    eye = jnp.where(iota((24, 24), 0) == iota((24, 24), 1), stiff[...], 0.0)
    dh, dl = split2(jnp.broadcast_to(jnp.sum(eye, axis=0, keepdims=True), (8, 24)))
    dvec[...] = dot(dh, rd) + dot(dl, rd)
    zi, zj = iota((LANES, 256), 0), iota((LANES, 256), 1)
    wz[...] = jnp.where(
        zi // BE == lax.rem(zj, 32), corner_weight(lax.rem(zi, BE), zj // LANES), 0.0
    ).astype(BF16)
    pi, pj = iota((32, 64), 0), iota((32, 64), 1)
    wp = jnp.where(pi // 16 == pj // 32, corner_weight(lax.rem(pi, BE), (pj // 16) % 2), 0.0).astype(BF16)
    ti, tj = iota((64, 32), 0), iota((64, 32), 1)
    wpt = jnp.where(tj // 16 == ti // 32, corner_weight(lax.rem(tj, BE), (ti // 16) % 2), 0.0).astype(BF16)
    mean8 = jnp.where(
        lax.rem(iota((LANES, LANES), 0), MOST) == lax.rem(iota((LANES, LANES), 1), MOST), 0.125, 0.0
    ).astype(BF16)
    band = (iota((256, 256), 0) % 16) // BE == (iota((256, 256), 1) // 32) % BE
    pair = jnp.where(
        jnp.broadcast_to(perm[...], (LANES, LANES)) == iota((LANES, LANES), 0), 1.0, 0.0
    ).astype(BF16)
    back = dot(iota((8, LANES), 1).astype(F32).astype(BF16), pair, NT).astype(jnp.int32)

    finish_halo(2)
    start_halo(3)
    planes(3, 0, PX, tension=True)

    for r in range(NROW):
        a, bh = r // 2, r % 2
        for x in range(2):
            acc = None
            for i in range(BE):
                share = (i + 0.5) / BE
                term = tens[BE * a + i, bh * 16 : (bh + 1) * 16, :] * (
                    (share if x else 1.0 - share) / (BE / 2.0) ** 3
                )
                acc = term if acc is None else acc + term
            txb[r * 32 + x * 16 : r * 32 + (x + 1) * 16, :] = acc
    h, l = split2(txb[...])
    along = jnp.where(band, dot(h, wz[...]) + dot(l, wz[...]), 0.0)
    for r in range(NROW):
        h, l = split2(along[r * 32 : (r + 1) * 32])
        both = dot(wpt, h) + dot(wpt, l)
        full = jnp.concatenate([both[:, :LANES], both[:, LANES:]], axis=0)
        h, l = split2(jnp.where(here(r), full, 0.0))
        lhi[:, r * LANES : (r + 1) * LANES] = h
        llo[:, r * LANES : (r + 1) * LANES] = l
    snd[1] = placed().reshape(count, 1, LANES)
    send_rows(1)

    finish_halo(3)
    start_halo(4)
    wait_rows(0)

    def spread(comps):
        rows = 2 * comps * NROW
        for c in range(comps):
            h, l = split2(vals[c])
            vsp[0, c] = h.astype(F32)
            vsp[1, c] = l.astype(F32)

        def chunk(ch, acc):
            for j in range(16):
                p = ch * 16 + j
                hit = jnp.broadcast_to(nhi[pl.ds(p, 1), :], (NROW, LANES)) == iota((NROW, LANES), 0)
                column = []
                for s in range(2):
                    for c in range(comps):
                        row = jnp.broadcast_to(vsp[s, c, pl.ds(p, 1), :], (NROW, LANES))
                        column.append(jnp.where(hit, row, 0.0))
                abuf[0:rows, j * LANES : (j + 1) * LANES] = jnp.concatenate(column, axis=0).astype(BF16)
            return acc + dot(abuf[0:rows, :], onehot[ch], NT)

        acc = lax.fori_loop(0, 8, chunk, jnp.zeros((rows, LANES), F32))
        both = acc[: rows // 2] + acc[rows // 2 :]
        for c in range(comps):
            ndb[c] = both[c * NROW : (c + 1) * NROW]

    def shared(s, to):
        peer = me - 1 if to == 0 else me + 1
        return pltpu.make_async_remote_copy(
            src_ref=asm_s.at[s, to],
            dst_ref=asm_r.at[s, to],
            send_sem=ass.at[s, to],
            recv_sem=asr.at[s, to],
            device_id=(peer // n_four, lax.rem(peer, n_four)),
            device_id_type=MESH,
        )

    has_before, has_after = me > 0, me < count - 1

    def assemble(s, comps):
        lead = jnp.concatenate([ndb[c, 0:1, :] for c in range(comps)] + [jnp.zeros((NROW - comps, LANES), F32)], axis=0)
        trail = jnp.concatenate(
            [ndb[c, NROW - 1 :, :] for c in range(comps)] + [jnp.zeros((NROW - comps, LANES), F32)], axis=0
        )
        asm_s[s, 0] = jnp.take_along_axis(lead, back, axis=1)
        asm_s[s, 1] = trail

        @pl.when(has_before)
        def _():
            shared(s, 0).start()

        @pl.when(has_after)
        def _():
            shared(s, 1).start()

        @pl.when(has_after)
        def _():
            shared(s, 0).wait_recv()
            for c in range(comps):
                ndb[c, NROW - 1 :, :] = ndb[c, NROW - 1 :, :] + asm_r[s, 0, c : c + 1, :]

        @pl.when(has_before)
        def _():
            shared(s, 1).wait_recv()
            order = jnp.broadcast_to(perm[...], (NROW, LANES))
            got = jnp.take_along_axis(asm_r[s, 1], order, axis=1)
            for c in range(comps):
                ndb[c, 0:1, :] = ndb[c, 0:1, :] + got[c : c + 1]

        @pl.when(has_before)
        def _():
            shared(s, 0).wait_send()

        @pl.when(has_after)
        def _():
            shared(s, 1).wait_send()

    def collect(table):
        def tile(i, carry_in):
            rows = pl.ds(i * NROW, NROW)
            low, high = nlo[rows, :], nhi[rows, :]
            for c in range(3):
                out = jnp.zeros((NROW, LANES), F32)
                for hi in range(NROW):
                    line = jnp.broadcast_to(ndb[6 + c, hi : hi + 1, :], (NROW, LANES))
                    out = jnp.where(high == hi, jnp.take_along_axis(line, low, axis=1), out)
                vals[c, rows, :] = out
            return carry_in

        for c in range(3):
            ndb[6 + c] = table[c]
        lax.fori_loop(0, 16, tile, 0)
        return jnp.concatenate([vals[0], vals[1], vals[2]], axis=1)

    def times(x, table):
        h, l = split2(x)
        return dot(h, table[0]) + dot(l, table[0]) + dot(h, table[1])

    planes(4, 0, PX)

    wait_rows(1)
    arrived = received(1)
    h, l = split2(arrived)
    k8 = received(0) * (1.0 + 0.5 * jnp.tanh(dot(h, mean8) + dot(l, mean8)))
    k8b[...] = k8
    force = times(arrived, kf)
    for c in range(3):
        part = slice(c * LANES, (c + 1) * LANES)
        vals[c] = force[:, part]
        vals[3 + c] = k8 * dvec[0:1, part]
    spread(6)
    assemble(0, 6)
    forces = [ndb[c] for c in range(3)]
    diagonal = [SPRING + ndb[3 + c] for c in range(3)]
    guess = [RELAX * f / d for f, d in zip(forces, diagonal)]
    pushed = times(collect(guess), ks)
    for c in range(3):
        vals[c] = k8b[...] * pushed[:, c * LANES : (c + 1) * LANES]
    spread(3)
    assemble(1, 3)
    moved = []
    for c in range(3):
        applied = SPRING * guess[c] + ndb[c]
        moved.append(guess[c] + RELAX * (forces[c] - applied) / diagonal[c])
        disp_out[c] = moved[c]
    strain = times(collect(moved), kt)
    snd[2] = strain.reshape(count, 1, LANES)
    send_rows(2)
    finish_halo(4)
    wait_rows(2)

    h, l = split2(received(2).T)
    mine = dot(h, tbuf[...]) + dot(l, tbuf[...])
    for r in range(NROW):
        own = jnp.where(here(r), mine[:, r * LANES : (r + 1) * LANES], 0.0)
        h, l = split2(jnp.concatenate([own[:64], own[64:]], axis=1))
        along = jnp.where(band[:32], dot(wp, h) + dot(wp, l), 0.0)
        h, l = split2(along)
        fine = dot(h, wz[...], NT) + dot(l, wz[...], NT)
        a, bh = r // 2, r % 2
        for i in range(BE):
            share = (i + 0.5) / BE
            ex[BE * a + i, bh * 16 : (bh + 1) * 16, :] = (1.0 - share) * fine[:16] + share * fine[16:]

    def add_excess(i, c):
        vb[4, i] = vb[4, i] - (DT * GAIN) * ex[i] * (vb[3, i] - STRETCH_REV)
        return c

    lax.fori_loop(0, PX, add_excess, 0)
    start_halo(5)
    planes(5, 0, PX, with_excess=True)
    finish_halo(5)
    start_halo(6)
    planes(6, 0, PX, with_excess=True)
    finish_halo(6)
    start_halo(7)

    def store_group(g):
        part = pl.ds(g * GP, GP)
        return pltpu.make_async_copy(ust.at[:, part], states_out.at[:, part], dma_out.at[g])

    for g in range(GROUPS):
        planes(7, g * GP, (g + 1) * GP, with_excess=True, closing=True)
        store_group(g).start()
    finish_halo(7)
    pot_out[...] = vb[7]
    for n in range(8):
        finish_sends(n)
    for s in range(3):
        wait_sent(s)
    for g in range(GROUPS):
        store_group(g).wait()


def per_device(
    n_wide,
    n_four,
    voltage,
    states,
    half_volt,
    gate_slope,
    retention,
    conduct,
    reversal,
    tension_weights,
    routes,
    base_stiff,
    elem_nodes,
    share_perm,
    stiffness,
    force_map,
    strain_map,
):
    count = n_wide * n_four
    tw = tension_weights / conduct
    tail = jnp.zeros((NK,), F32)
    sums = (
        tail.at[0].set(0.5 * jnp.sum(conduct))
        .at[1].set(0.5 * jnp.sum(conduct * reversal))
        .at[2].set(0.5 * jnp.sum(tension_weights))
    )
    par = jnp.stack(
        [
            0.5 / gate_slope,
            -0.5 * half_volt / gate_slope,
            retention,
            0.5 * conduct * (1.0 - retention),
            reversal,
            retention * conduct,
            -0.5 * retention * conduct,
            1.0 / conduct,
            tw,
            sums,
        ]
    )
    nodes = elem_nodes.reshape(8, count, MOST).transpose(1, 0, 2).reshape(count, LANES)
    vmem = pl.BlockSpec(memory_space=pltpu.VMEM)
    anyspace = pl.BlockSpec(memory_space=pl.ANY)
    scratch = [
        pltpu.VMEM((NK, PX, PY, PZ), F32),
        pltpu.VMEM((8, PX, PY, PZ), F32),
        pltpu.VMEM((8, 2, PY, PZ), F32),
        pltpu.VMEM((8, 2, PX, PZ), F32),
        pltpu.VMEM((8, 2, PX, PZ), F32),
        pltpu.VMEM((PX, PY, PZ), F32),
        pltpu.VMEM((PX, PY, PZ), F32),
        pltpu.VMEM((count, 1024), BF16),
        pltpu.VMEM((NROW, LANES), jnp.int32),
        pltpu.VMEM((LANES, 1024), BF16),
        pltpu.VMEM((LANES, 1024), BF16),
        pltpu.VMEM((8, LANES, 2048), BF16),
        pltpu.VMEM((96, 2048), BF16),
        pltpu.VMEM((2, 6, count, LANES), F32),
        pltpu.VMEM((count, LANES), jnp.int32),
        pltpu.VMEM((count, LANES), jnp.int32),
        pltpu.VMEM((2, LANES, 384), BF16),
        pltpu.VMEM((2, 384, 384), BF16),
        pltpu.VMEM((2, 384, LANES), BF16),
        pltpu.VMEM((8, 384), F32),
        pltpu.VMEM((LANES, 256), BF16),
        pltpu.VMEM((count, LANES), F32),
        pltpu.VMEM((256, LANES), F32),
        pltpu.VMEM((6, count, LANES), F32),
        pltpu.VMEM((9, NROW, LANES), F32),
        pltpu.VMEM((2, 2, NROW, LANES), F32),
        pltpu.VMEM((2, 2, NROW, LANES), F32),
        pltpu.VMEM((3, count, 1, LANES), F32),
        pltpu.VMEM((3, count, 1, LANES), F32),
        pltpu.SemaphoreType.DMA((GROUPS,)),
        pltpu.SemaphoreType.DMA((GROUPS,)),
        pltpu.SemaphoreType.DMA((8, 4)),
        pltpu.SemaphoreType.DMA((8, 4)),
        pltpu.SemaphoreType.DMA((3,)),
        pltpu.SemaphoreType.DMA((3,)),
        pltpu.SemaphoreType.DMA((2, 2)),
        pltpu.SemaphoreType.DMA((2, 2)),
    ]
    pot, new_states, disp = pl.pallas_call(
        functools.partial(kernel, n_wide, n_four),
        out_shape=(
            jax.ShapeDtypeStruct((PX, PY, PZ), F32),
            jax.ShapeDtypeStruct((NK, PX, PY, PZ), F32),
            jax.ShapeDtypeStruct((3, NROW, LANES), F32),
        ),
        in_specs=[pl.BlockSpec(memory_space=pltpu.SMEM), vmem, anyspace] + [vmem] * 7,
        out_specs=(vmem, anyspace, vmem),
        scratch_shapes=scratch,
        compiler_params=pltpu.CompilerParams(
            collective_id=0, has_side_effects=True, vmem_limit_bytes=40 << 20
        ),
    )(
        par,
        voltage,
        states,
        routes.reshape(NROW, LANES),
        base_stiff.reshape(NROW, LANES),
        nodes,
        share_perm,
        stiffness,
        force_map,
        strain_map,
    )
    return pot, new_states, disp.reshape(3, NROW * LANES)


def solution(mesh):
    placed = (
        P("wide", "four", None),
        P(None, "wide", "four", None),
        P(),
        P(),
        P(),
        P(),
        P(),
        P(),
        P(("wide", "four"), None),
        P(("wide", "four")),
        P(None, ("wide", "four")),
        P(("wide", "four"), None),
        P(),
        P(),
        P(),
    )
    return jax.shard_map(
        functools.partial(per_device, mesh.shape["wide"], mesh.shape["four"]),
        mesh=mesh,
        in_specs=placed,
        out_specs=(
            P("wide", "four", None),
            P(None, "wide", "four", None),
            P(None, ("wide", "four")),
        ),
        check_vma=False,
    )
```

```python
import functools

import jax
import jax.numpy as jnp
from jax import lax
from jax.experimental import pallas as pl
from jax.experimental.pallas import tpu as pltpu
from jax.sharding import PartitionSpec as P

BE = 4
NK = 20
PX, PY, PZ = 16, 32, 128
NROW = 8
LANES = 128
MOST = 16
F32, BF16 = jnp.float32, jnp.bfloat16
DT = 0.1
DX, DY, DZ = 1.5, 1.0, 0.6
GAIN, STRETCH_REV = 2.0, 0.5
SPRING, RELAX = 1.0, 0.7
GROUPS = 4
TWO = 2
GP = PX // GROUPS
MESH = pl.DeviceIdType.MESH
NN = (((1,), (0,)), ((), ()))
NT = (((1,), (1,)), ((), ()))


def dot(a, b, dims=NN):
    return lax.dot_general(a, b, dims, preferred_element_type=F32)


def split2(x):
    high = x.astype(BF16)
    return high, (x - high.astype(F32)).astype(BF16)


def iota(shape, dim):
    return lax.broadcasted_iota(jnp.int32, shape, dim)


def corner_of(j):
    return 4 * ((j // 2) % 2) + 2 * (j % 2) + j // 4


def corner_weight(i, side):
    place = (i.astype(F32) + 0.5) * (1.0 / BE)
    return jnp.where(side == 1, place, 1.0 - place)


def kernel(
    n_wide,
    n_four,
    raw_in,
    volt_in,
    states_in,
    routes_in,
    base_in,
    nodes_in,
    perm_in,
    stiff_in,
    fmap_in,
    smap_in,
    pot_out,
    states_out,
    disp_out,
    raw,
    par,
    volt,
    routes,
    base,
    nodes,
    perm,
    stiff,
    fmap,
    smap,
    ust,
    vb,
    xh,
    yh,
    yf,
    ex,
    tens,
    tbuf,
    posb,
    lhi,
    llo,
    onehot,
    abuf,
    vsp,
    nlo,
    nhi,
    kf,
    ks,
    kt,
    dvec,
    wz,
    k8b,
    txb,
    vals,
    ndb,
    asm_s,
    asm_r,
    snd,
    rcv,
    dma_in,
    dma_small,
    hs,
    hr,
    a2s,
    a2r,
    ass,
    asr,
    rounds,
):
    count = n_wide * n_four
    wide = lax.axis_index("wide")
    four = lax.axis_index("four")
    me = wide * n_four + four
    barrier = pltpu.get_barrier_semaphore()

    ring = (wide // 16, (wide // 4) % 4, wide % 4, four)
    extent = (2, 4, 4, 4)

    def place(y, z, x, f):
        return {"wide": y * 16 + z * 4 + x, "four": f}

    def along(axis):
        for step in range(1, extent[axis]):
            spot = list(ring)
            spot[axis] = (spot[axis] + step) % extent[axis]
            yield place(*spot)

    def others(act):
        def some(g, c):
            a, b = g // 4, g % 4
            z = (ring[1] + 2 + 3 * a + 3 * ((a * a - a) // 2)) % 4
            x = (ring[2] + 2 + 3 * b + 3 * ((b * b - b) // 2)) % 4
            for dy in (1, 0):
                w = ((ring[0] + dy) % 2) * 16 + z * 4 + x
                for df in (2, 3, 1, 0):
                    f = (four + df) % 4

                    def go(w=w, f=f):
                        act(w * n_four + f, {"wide": w, "four": f})

                    if dy == 0 and df == 0:
                        pl.when(g < 15)(go)
                    else:
                        go()
            return c

        lax.fori_loop(0, 16, some, 0)

    small = [
        pltpu.make_async_copy(src, dst, dma_small.at[i])
        for i, (src, dst) in enumerate(
            [(raw_in[j], raw.at[j]) for j in range(6)]
            + [
                (routes_in, routes),
                (base_in, base),
                (volt_in, volt),
                (nodes_in, nodes),
                (perm_in, perm),
                (stiff_in, stiff),
                (fmap_in, fmap),
                (smap_in, smap),
            ]
        )
    ]
    for copy in small[:9]:
        copy.start()

    def load_group(g):
        part = pl.ds(g * GP, GP)
        return pltpu.make_async_copy(states_in.at[:, part], ust.at[:, part], dma_in.at[g])

    for g in range(GROUPS):
        load_group(g).start()
    for copy in small[9:]:
        copy.start()
    def greet(device):
        pl.semaphore_signal(barrier, inc=1, device_id=device, device_id_type=MESH)

    for axis in range(4):
        for device in along(axis):
            greet(device)
    at_x_end, at_x_start = wide % 4 == 3, wide % 4 == 0
    extra = (
        (at_x_end & (wide < n_wide - 1), {"wide": wide + 1, "four": four}),
        (at_x_start & (wide > 0), {"wide": wide - 1, "four": four}),
        ((four == n_four - 1) & (wide < n_wide - 1), {"wide": wide + 1, "four": 0 * four}),
        ((four == 0) & (wide > 0), {"wide": wide - 1, "four": 0 * four + n_four - 1}),
    )
    for cond, device in extra:
        pl.when(cond)(functools.partial(greet, device))
    pl.semaphore_wait(barrier, 10 + sum(cond.astype(jnp.int32) for cond, _ in extra))

    def meet(axis):
        for device in along(axis):
            pl.semaphore_signal(rounds.at[axis], inc=1, device_id=device, device_id_type=MESH)

    def met(axis):
        pl.semaphore_wait(rounds.at[axis], extent[axis] - 1)

    meet(0)
    has = (wide > 0, wide < n_wide - 1, four > 0, four < n_four - 1)
    opposite = (1, 0, 3, 2)
    peers = ((wide - 1, four), (wide + 1, four), (wide, four - 1), (wide, four + 1))

    def field(n):
        return volt if n == 0 else vb.at[n - 1]

    def halo(n, d):
        v = field(n)
        src = (v.at[0], v.at[PX - 1], yf.at[n, 0], yf.at[n, 1])[d]
        dst = (xh.at[n, 1], xh.at[n, 0], yh.at[n, 1], yh.at[n, 0])[d]
        return pltpu.make_async_remote_copy(
            src_ref=src,
            dst_ref=dst,
            send_sem=hs.at[n, d],
            recv_sem=hr.at[n, d],
            device_id=peers[d],
            device_id_type=MESH,
        )

    def start_halo(n):
        v = field(n)
        yf[n, 0] = v[:, 0, :]
        yf[n, 1] = v[:, PY - 1, :]
        for d in range(4):

            @pl.when(has[d])
            def _():
                halo(n, d).start()

    def finish_halo(n):
        v, w = field(n), vb.at[n]

        for d in range(4):

            @pl.when(has[opposite[d]])
            def _():
                halo(n, d).wait_recv()
                if d == 0:
                    w[PX - 1] = w[PX - 1] + (DT * DX) * (xh[n, 1] - v[PX - 1])
                elif d == 1:
                    w[0] = w[0] + (DT * DX) * (xh[n, 0] - v[0])
                elif d == 2:
                    w[:, PY - 1, :] = w[:, PY - 1, :] + (DT * DY) * (yh[n, 1] - v[:, PY - 1, :])
                else:
                    w[:, 0, :] = w[:, 0, :] + (DT * DY) * (yh[n, 0] - v[:, 0, :])

    def finish_sends(n):
        for d in range(4):

            @pl.when(has[d])
            def _():
                halo(n, d).wait_send()

    shape = (TWO, PY // NROW, NROW, LANES)
    lane = iota((PY, PZ), 1)

    def planes(n, first, last, with_excess=False, opening=False, tension=False, closing=False):
        v_ref, w_ref = field(n), vb.at[n]

        def body(g, c):
            i = g * TWO
            v = v_ref[pl.ds(i, TWO)].reshape(shape)
            total_a = jnp.broadcast_to(par[9, 0], shape)
            total_b = jnp.broadcast_to(par[9, 1], shape)
            total_t = jnp.broadcast_to(par[9, 2], shape)
            for k in range(NK):
                t = jnp.tanh(v * par[0, k] + par[1, k])
                old = ust[k, pl.ds(i, TWO)].reshape(shape)
                if opening:
                    u = old * par[5, k] + (t * par[3, k] + par[6, k])
                else:
                    u = old * par[2, k] + t * par[3, k]
                if closing:
                    states_out[k, pl.ds(i, TWO)] = (u * par[7, k] + 0.5).reshape(TWO, PY, PZ)
                else:
                    ust[k, pl.ds(i, TWO)] = u.reshape(TWO, PY, PZ)
                total_a = total_a + u
                total_b = total_b + u * par[4, k]
                if tension:
                    total_t = total_t + u * par[8, k]
            current = (v * total_a - total_b).reshape(TWO, PY, PZ)
            if tension:
                tens[pl.ds(i, TWO)] = total_t.reshape(TWO, PY, PZ)
            for h in range(TWO):
                j = i + h
                v = v_ref[j]
                flow = current[h]
                if with_excess:
                    flow = flow + GAIN * ex[j] * (v - STRETCH_REV)
                near_x = v_ref[jnp.maximum(j - 1, 0)] + v_ref[jnp.minimum(j + 1, PX - 1)]
                near_y = jnp.concatenate([v[:1], v[:-1]], 0) + jnp.concatenate([v[1:], v[-1:]], 0)
                near_z = jnp.where(lane == 0, v, pltpu.roll(v, 1, 1)) + jnp.where(
                    lane == PZ - 1, v, pltpu.roll(v, PZ - 1, 1)
                )
                lap = DX * near_x + DY * near_y + DZ * near_z - (2.0 * (DX + DY + DZ)) * v
                w_ref[j] = v + DT * (lap - flow)
            return c

        lax.fori_loop(first // TWO, last // TWO, body, 0)

    def send_rows(s):
        def one(t, device):
            pltpu.make_async_remote_copy(
                src_ref=snd.at[s, t],
                dst_ref=rcv.at[s, me],
                send_sem=a2s.at[s],
                recv_sem=a2r.at[s],
                device_id=device,
                device_id_type=MESH,
            ).start()

        others(one)
        rcv[s, me] = snd[s, me]

    def wait_rows(s):
        part = rcv.at[s, pl.ds(0, count - 1)]
        pltpu.make_async_copy(part, part, a2r.at[s]).wait()

    def wait_sent(s):
        part = snd.at[s, pl.ds(0, count - 1)]
        pltpu.make_async_copy(part, part, a2s.at[s]).wait()

    def received(s):
        return rcv[s].reshape(count, LANES)

    small[8].wait()
    start_halo(0)
    for copy in small[:8]:
        copy.wait()
    def spread_scalar(x):
        return jnp.full((NROW, LANES), x, F32)

    sums = [jnp.zeros((NROW, LANES), F32) for _ in range(3)]
    for k in range(NK):
        half, slope, keep, cond, rev, weight = [spread_scalar(raw[j, 0, k]) for j in range(6)]
        inv_slope, inv_cond = 0.5 / slope, 1.0 / cond
        entries = (
            inv_slope,
            -half * inv_slope,
            keep,
            0.5 * cond * (1.0 - keep),
            rev,
            keep * cond,
            -0.5 * keep * cond,
            inv_cond,
            weight * inv_cond,
        )
        for j, entry in enumerate(entries):
            par[j, k] = entry
        sums = [sums[0] + 0.5 * cond, sums[1] + 0.5 * cond * rev, sums[2] + 0.5 * weight]
    for j in range(3):
        par[9, j] = sums[j]

    met(0)
    meet(1)
    for g in range(GROUPS):
        load_group(g).wait()
        planes(0, g * GP, (g + 1) * GP, opening=True)

    met(1)
    meet(2)

    tri = jnp.where((iota((LANES, 256), 0) < iota((LANES, 256), 1)), 1.0, 0.0).astype(BF16)
    carry = jnp.zeros((count, LANES), F32)
    for r in range(NROW):
        hot = jnp.broadcast_to(routes[r : r + 1, :], (count, LANES)) == iota((count, LANES), 0)
        hot_f = jnp.where(hot, 1.0, 0.0)
        hot_b = hot_f.astype(BF16)
        tbuf[:, r * LANES : (r + 1) * LANES] = hot_b
        run = dot(hot_b, tri)
        before = run[:, :LANES] + carry
        carry = carry + run[:, LANES:]
        posb[r : r + 1, :] = jnp.sum(before * hot_f, axis=0, keepdims=True).astype(jnp.int32)

    slot_row = lax.rem(iota((LANES, LANES), 0), MOST)

    def here(r):
        return jnp.broadcast_to(posb[r : r + 1, :], (LANES, LANES)) == slot_row

    def placed():
        return dot(tbuf[...], lhi[...], NT) + dot(tbuf[...], llo[...], NT)

    for r in range(NROW):
        row = jnp.broadcast_to(base[r : r + 1, :], (LANES, LANES))
        h, l = split2(jnp.where(here(r), row, 0.0))
        lhi[:, r * LANES : (r + 1) * LANES] = h
        llo[:, r * LANES : (r + 1) * LANES] = l
    snd[0] = placed().reshape(count, 1, LANES)


    finish_halo(0)
    start_halo(1)
    planes(1, 0, PX)
    met(2)
    meet(3)

    for copy in small[9:]:
        copy.wait()
    row8, block = iota((NROW, LANES), 0), iota((NROW, LANES), 1) // MOST
    for t in range(count // NROW):
        x = nodes[:, t * LANES : (t + 1) * LANES]
        for bit in (1, 2, 4):
            up = pltpu.roll(pltpu.roll(x, NROW - bit, 0), MOST * bit, 1)
            down = pltpu.roll(pltpu.roll(x, bit, 0), LANES - MOST * bit, 1)
            row_bit, block_bit = (row8 // bit) % 2, (block // bit) % 2
            x = jnp.where(row_bit < block_bit, up, jnp.where(row_bit > block_bit, down, x))
        nlo[t * NROW : (t + 1) * NROW, :] = lax.rem(x, LANES)
        nhi[t * NROW : (t + 1) * NROW, :] = x // LANES

    def hot_chunk(ch, c):
        for j in range(16):
            row = nlo[pl.ds(ch * 16 + j, 1), :]
            hit = jnp.broadcast_to(row, (LANES, LANES)) == iota((LANES, LANES), 0)
            onehot[ch, :, j * LANES : (j + 1) * LANES] = jnp.where(hit, 1.0, 0.0).astype(BF16)
        return c

    lax.fori_loop(0, 8, hot_chunk, 0)
    finish_halo(1)
    start_halo(2)
    planes(2, 0, PX)

    rd = jnp.where(iota((24, 384), 0) == iota((24, 384), 1) // MOST, 1.0, 0.0).astype(BF16)
    rdt = jnp.where(iota((384, 24), 1) == iota((384, 24), 0) // MOST, 1.0, 0.0).astype(BF16)
    rj = jnp.where(iota((LANES, 8), 1) == corner_of(iota((LANES, 8), 0) // MOST), 1.0, 0.0).astype(BF16)
    rjt = jnp.where(iota((8, LANES), 0) == corner_of(iota((8, LANES), 1) // MOST), 1.0, 0.0).astype(BF16)

    def kron(left, part, right, rows, cols, dims=NT):
        full = dot(dot(left, part, dims).astype(BF16), right)
        same = lax.rem(iota((rows, cols), 0), MOST) == lax.rem(iota((rows, cols), 1), MOST)
        return jnp.where(same, full, 0.0).astype(BF16)

    for s, part in enumerate(split2(fmap[...])):
        kf[s] = kron(rj, part, rd, LANES, 384, NN)
    for s, part in enumerate(split2(stiff[...])):
        ks[s] = kron(rdt, part, rd, 384, 384)
    for s, part in enumerate(split2(smap[...])):
        kt[s] = kron(rdt, part, rjt, 384, LANES)
    eye = jnp.where(iota((24, 24), 0) == iota((24, 24), 1), stiff[...], 0.0)
    dh, dl = split2(jnp.broadcast_to(jnp.sum(eye, axis=0, keepdims=True), (8, 24)))
    dvec[...] = dot(dh, rd) + dot(dl, rd)
    zi, zj = iota((LANES, 256), 0), iota((LANES, 256), 1)
    wz[...] = jnp.where(
        zi // BE == lax.rem(zj, 32), corner_weight(lax.rem(zi, BE), zj // LANES), 0.0
    ).astype(BF16)
    pi, pj = iota((32, 64), 0), iota((32, 64), 1)
    wp = jnp.where(pi // 16 == pj // 32, corner_weight(lax.rem(pi, BE), (pj // 16) % 2), 0.0).astype(BF16)
    ti, tj = iota((64, 32), 0), iota((64, 32), 1)
    wpt = jnp.where(tj // 16 == ti // 32, corner_weight(lax.rem(tj, BE), (ti // 16) % 2), 0.0).astype(BF16)
    mean8 = jnp.where(
        lax.rem(iota((LANES, LANES), 0), MOST) == lax.rem(iota((LANES, LANES), 1), MOST), 0.125, 0.0
    ).astype(BF16)
    band = (iota((256, 256), 0) % 16) // BE == (iota((256, 256), 1) // 32) % BE
    pair = jnp.where(
        jnp.broadcast_to(perm[...], (LANES, LANES)) == iota((LANES, LANES), 0), 1.0, 0.0
    ).astype(BF16)
    back = dot(iota((8, LANES), 1).astype(F32).astype(BF16), pair, NT).astype(jnp.int32)

    met(3)
    send_rows(0)
    finish_halo(2)
    start_halo(3)
    planes(3, 0, PX, tension=True)

    for r in range(NROW):
        a, bh = r // 2, r % 2
        for x in range(2):
            acc = None
            for i in range(BE):
                share = (i + 0.5) / BE
                term = tens[BE * a + i, bh * 16 : (bh + 1) * 16, :] * (
                    (share if x else 1.0 - share) / (BE / 2.0) ** 3
                )
                acc = term if acc is None else acc + term
            txb[r * 32 + x * 16 : r * 32 + (x + 1) * 16, :] = acc
    h, l = split2(txb[...])
    along = jnp.where(band, dot(h, wz[...]) + dot(l, wz[...]), 0.0)
    for r in range(NROW):
        h, l = split2(along[r * 32 : (r + 1) * 32])
        both = dot(wpt, h) + dot(wpt, l)
        full = jnp.concatenate([both[:, :LANES], both[:, LANES:]], axis=0)
        h, l = split2(jnp.where(here(r), full, 0.0))
        lhi[:, r * LANES : (r + 1) * LANES] = h
        llo[:, r * LANES : (r + 1) * LANES] = l
    snd[1] = placed().reshape(count, 1, LANES)
    send_rows(1)

    finish_halo(3)
    start_halo(4)
    wait_rows(0)

    def spread(comps):
        rows = 2 * comps * NROW
        for c in range(comps):
            h, l = split2(vals[c])
            vsp[0, c] = h.astype(F32)
            vsp[1, c] = l.astype(F32)

        def chunk(ch, acc):
            for j in range(16):
                p = ch * 16 + j
                hit = jnp.broadcast_to(nhi[pl.ds(p, 1), :], (NROW, LANES)) == iota((NROW, LANES), 0)
                column = []
                for s in range(2):
                    for c in range(comps):
                        row = jnp.broadcast_to(vsp[s, c, pl.ds(p, 1), :], (NROW, LANES))
                        column.append(jnp.where(hit, row, 0.0))
                abuf[0:rows, j * LANES : (j + 1) * LANES] = jnp.concatenate(column, axis=0).astype(BF16)
            return acc + dot(abuf[0:rows, :], onehot[ch], NT)

        acc = lax.fori_loop(0, 8, chunk, jnp.zeros((rows, LANES), F32))
        both = acc[: rows // 2] + acc[rows // 2 :]
        for c in range(comps):
            ndb[c] = both[c * NROW : (c + 1) * NROW]

    def shared(s, to):
        peer = me - 1 if to == 0 else me + 1
        return pltpu.make_async_remote_copy(
            src_ref=asm_s.at[s, to],
            dst_ref=asm_r.at[s, to],
            send_sem=ass.at[s, to],
            recv_sem=asr.at[s, to],
            device_id=(peer // n_four, lax.rem(peer, n_four)),
            device_id_type=MESH,
        )

    has_before, has_after = me > 0, me < count - 1

    def assemble(s, comps):
        lead = jnp.concatenate([ndb[c, 0:1, :] for c in range(comps)] + [jnp.zeros((NROW - comps, LANES), F32)], axis=0)
        trail = jnp.concatenate(
            [ndb[c, NROW - 1 :, :] for c in range(comps)] + [jnp.zeros((NROW - comps, LANES), F32)], axis=0
        )
        asm_s[s, 0] = jnp.take_along_axis(lead, back, axis=1)
        asm_s[s, 1] = trail

        @pl.when(has_before)
        def _():
            shared(s, 0).start()

        @pl.when(has_after)
        def _():
            shared(s, 1).start()

        @pl.when(has_after)
        def _():
            shared(s, 0).wait_recv()
            for c in range(comps):
                ndb[c, NROW - 1 :, :] = ndb[c, NROW - 1 :, :] + asm_r[s, 0, c : c + 1, :]

        @pl.when(has_before)
        def _():
            shared(s, 1).wait_recv()
            order = jnp.broadcast_to(perm[...], (NROW, LANES))
            got = jnp.take_along_axis(asm_r[s, 1], order, axis=1)
            for c in range(comps):
                ndb[c, 0:1, :] = ndb[c, 0:1, :] + got[c : c + 1]

        @pl.when(has_before)
        def _():
            shared(s, 0).wait_send()

        @pl.when(has_after)
        def _():
            shared(s, 1).wait_send()

    def collect(table):
        def tiles(g, carry_in):
            for j in range(4):
                rows = pl.ds(g * 32 + j * NROW, NROW)
                low, high = nlo[rows, :], nhi[rows, :]
                masks = [high == hi for hi in range(NROW)]
                for c in range(3):
                    out = jnp.zeros((NROW, LANES), F32)
                    for hi in range(NROW):
                        line = jnp.broadcast_to(ndb[6 + c, hi : hi + 1, :], (NROW, LANES))
                        out = jnp.where(masks[hi], jnp.take_along_axis(line, low, axis=1), out)
                    vals[c, rows, :] = out
            return carry_in

        for c in range(3):
            ndb[6 + c] = table[c]
        lax.fori_loop(0, 4, tiles, 0)
        return jnp.concatenate([vals[0], vals[1], vals[2]], axis=1)

    def times(x, table):
        h, l = split2(x)
        return dot(h, table[0]) + dot(l, table[0]) + dot(h, table[1])

    planes(4, 0, PX)

    wait_rows(1)
    arrived = received(1)
    h, l = split2(arrived)
    k8 = received(0) * (1.0 + 0.5 * jnp.tanh(dot(h, mean8) + dot(l, mean8)))
    k8b[...] = k8
    force = times(arrived, kf)
    for c in range(3):
        part = slice(c * LANES, (c + 1) * LANES)
        vals[c] = force[:, part]
        vals[3 + c] = k8 * dvec[0:1, part]
    spread(6)
    assemble(0, 6)
    forces = [ndb[c] for c in range(3)]
    diagonal = [SPRING + ndb[3 + c] for c in range(3)]
    guess = [RELAX * f / d for f, d in zip(forces, diagonal)]
    pushed = times(collect(guess), ks)
    for c in range(3):
        vals[c] = k8b[...] * pushed[:, c * LANES : (c + 1) * LANES]
    spread(3)
    assemble(1, 3)
    moved = []
    for c in range(3):
        applied = SPRING * guess[c] + ndb[c]
        moved.append(guess[c] + RELAX * (forces[c] - applied) / diagonal[c])
        for hi in range(NROW):
            disp_out[c : c + 1, hi * LANES : (hi + 1) * LANES] = moved[c][hi : hi + 1]
    strain = times(collect(moved), kt)
    snd[2] = strain.reshape(count, 1, LANES)
    send_rows(2)
    finish_halo(4)
    wait_rows(2)

    h, l = split2(received(2).T)
    mine = dot(h, tbuf[...]) + dot(l, tbuf[...])
    for r in range(NROW):
        own = jnp.where(here(r), mine[:, r * LANES : (r + 1) * LANES], 0.0)
        h, l = split2(jnp.concatenate([own[:64], own[64:]], axis=1))
        along = jnp.where(band[:32], dot(wp, h) + dot(wp, l), 0.0)
        h, l = split2(along)
        fine = dot(h, wz[...], NT) + dot(l, wz[...], NT)
        a, bh = r // 2, r % 2
        for i in range(BE):
            share = (i + 0.5) / BE
            ex[BE * a + i, bh * 16 : (bh + 1) * 16, :] = (1.0 - share) * fine[:16] + share * fine[16:]

    def add_excess(i, c):
        vb[4, i] = vb[4, i] - (DT * GAIN) * ex[i] * (vb[3, i] - STRETCH_REV)
        return c

    lax.fori_loop(0, PX, add_excess, 0)
    start_halo(5)
    planes(5, 0, PX, with_excess=True)
    finish_halo(5)
    start_halo(6)
    planes(6, 0, PX, with_excess=True)
    finish_halo(6)
    start_halo(7)

    planes(7, 0, PX, with_excess=True, closing=True)
    finish_halo(7)
    pot_out[...] = vb[7]
    for n in range(8):
        finish_sends(n)
    for s in range(3):
        wait_sent(s)


def put_out(pot, states, disp, pot_out, states_out, disp_out, sem):
    copies = [
        pltpu.make_async_copy(src, dst, sem.at[i])
        for i, (src, dst) in enumerate(((states, states_out), (pot, pot_out), (disp, disp_out)))
    ]
    for copy in copies:
        copy.start()
    for copy in copies:
        copy.wait()


def in_hbm(x):
    return pltpu.with_memory_space_constraint(x, pltpu.HBM)


def per_device(
    n_wide,
    n_four,
    voltage,
    states,
    half_volt,
    gate_slope,
    retention,
    conduct,
    reversal,
    tension_weights,
    routes,
    base_stiff,
    elem_nodes,
    share_perm,
    stiffness,
    force_map,
    strain_map,
):
    count = n_wide * n_four
    vmem = pl.BlockSpec(memory_space=pltpu.VMEM)
    hbm = pl.BlockSpec(memory_space=pltpu.HBM)
    scratch = [
        pltpu.SMEM((6, 1, NK), F32),
        pltpu.VMEM((10, NK, NROW, LANES), F32),
        pltpu.VMEM((PX, PY, PZ), F32),
        pltpu.VMEM((NROW, LANES), jnp.int32),
        pltpu.VMEM((NROW, LANES), F32),
        pltpu.VMEM((8, count * MOST), jnp.int32),
        pltpu.VMEM((1, LANES), jnp.int32),
        pltpu.VMEM((24, 24), F32),
        pltpu.VMEM((8, 24), F32),
        pltpu.VMEM((8, 24), F32),
        pltpu.VMEM((NK, PX, PY, PZ), F32),
        pltpu.VMEM((8, PX, PY, PZ), F32),
        pltpu.VMEM((8, 2, PY, PZ), F32),
        pltpu.VMEM((8, 2, PX, PZ), F32),
        pltpu.VMEM((8, 2, PX, PZ), F32),
        pltpu.VMEM((PX, PY, PZ), F32),
        pltpu.VMEM((PX, PY, PZ), F32),
        pltpu.VMEM((count, 1024), BF16),
        pltpu.VMEM((NROW, LANES), jnp.int32),
        pltpu.VMEM((LANES, 1024), BF16),
        pltpu.VMEM((LANES, 1024), BF16),
        pltpu.VMEM((8, LANES, 2048), BF16),
        pltpu.VMEM((96, 2048), BF16),
        pltpu.VMEM((2, 6, count, LANES), F32),
        pltpu.VMEM((count, LANES), jnp.int32),
        pltpu.VMEM((count, LANES), jnp.int32),
        pltpu.VMEM((2, LANES, 384), BF16),
        pltpu.VMEM((2, 384, 384), BF16),
        pltpu.VMEM((2, 384, LANES), BF16),
        pltpu.VMEM((8, 384), F32),
        pltpu.VMEM((LANES, 256), BF16),
        pltpu.VMEM((count, LANES), F32),
        pltpu.VMEM((256, LANES), F32),
        pltpu.VMEM((6, count, LANES), F32),
        pltpu.VMEM((9, NROW, LANES), F32),
        pltpu.VMEM((2, 2, NROW, LANES), F32),
        pltpu.VMEM((2, 2, NROW, LANES), F32),
        pltpu.VMEM((3, count, 1, LANES), F32),
        pltpu.VMEM((3, count, 1, LANES), F32),
        pltpu.SemaphoreType.DMA((GROUPS,)),
        pltpu.SemaphoreType.DMA((14,)),
        pltpu.SemaphoreType.DMA((8, 4)),
        pltpu.SemaphoreType.DMA((8, 4)),
        pltpu.SemaphoreType.DMA((3,)),
        pltpu.SemaphoreType.DMA((3,)),
        pltpu.SemaphoreType.DMA((2, 2)),
        pltpu.SemaphoreType.DMA((2, 2)),
        pltpu.SemaphoreType.REGULAR((4,)),
    ]
    made = pl.pallas_call(
        functools.partial(kernel, n_wide, n_four),
        out_shape=(
            jax.ShapeDtypeStruct((PX, PY, PZ), F32),
            jax.ShapeDtypeStruct((NK, PX, PY, PZ), F32),
            jax.ShapeDtypeStruct((3, NROW * LANES), F32),
        ),
        in_specs=[[hbm] * 6] + [hbm] * 9,
        out_specs=(vmem, vmem, vmem),
        scratch_shapes=scratch,
        compiler_params=pltpu.CompilerParams(
            collective_id=0, has_side_effects=True, vmem_limit_bytes=40 << 20
        ),
    )(
        [
            in_hbm(x.reshape(1, NK))
            for x in (half_volt, gate_slope, retention, conduct, reversal, tension_weights)
        ],
        in_hbm(voltage),
        in_hbm(states),
        in_hbm(routes.reshape(NROW, LANES)),
        in_hbm(base_stiff.reshape(NROW, LANES)),
        in_hbm(elem_nodes),
        in_hbm(share_perm),
        in_hbm(stiffness),
        in_hbm(force_map.T),
        in_hbm(strain_map),
    )
    return pl.pallas_call(
        put_out,
        out_shape=[jax.ShapeDtypeStruct(x.shape, x.dtype) for x in made],
        in_specs=[vmem] * 3,
        out_specs=[hbm] * 3,
        scratch_shapes=[pltpu.SemaphoreType.DMA((3,))],
        compiler_params=pltpu.CompilerParams(vmem_limit_bytes=1 << 20),
    )(*made)


def solution(mesh):
    placed = (
        P("wide", "four", None),
        P(None, "wide", "four", None),
        P(),
        P(),
        P(),
        P(),
        P(),
        P(),
        P(("wide", "four"), None),
        P(("wide", "four")),
        P(None, ("wide", "four")),
        P(("wide", "four"), None),
        P(),
        P(),
        P(),
    )
    return jax.shard_map(
        functools.partial(per_device, mesh.shape["wide"], mesh.shape["four"]),
        mesh=mesh,
        in_specs=placed,
        out_specs=(
            P("wide", "four", None),
            P(None, "wide", "four", None),
            P(None, ("wide", "four")),
        ),
        check_vma=False,
    )
```

```python
import functools

import jax
import jax.numpy as jnp
from jax import lax
from jax.experimental import pallas as pl
from jax.experimental.pallas import tpu as pltpu
from jax.sharding import PartitionSpec as P

BE = 4
NK = 20
PX, PY, PZ = 16, 32, 128
NROW = 8
LANES = 128
MOST = 16
F32, BF16 = jnp.float32, jnp.bfloat16
DT = 0.1
DX, DY, DZ = 1.5, 1.0, 0.6
GAIN, STRETCH_REV = 2.0, 0.5
SPRING, RELAX = 1.0, 0.7
GROUPS = 4
TWO = 2
SKIPPED = (2, 6)
GP = PX // GROUPS
MESH = pl.DeviceIdType.MESH
NN = (((1,), (0,)), ((), ()))
NT = (((1,), (1,)), ((), ()))


def dot(a, b, dims=NN):
    return lax.dot_general(a, b, dims, preferred_element_type=F32)


def split2(x):
    high = x.astype(BF16)
    return high, (x - high.astype(F32)).astype(BF16)


def iota(shape, dim):
    return lax.broadcasted_iota(jnp.int32, shape, dim)


def corner_of(j):
    return 4 * ((j // 2) % 2) + 2 * (j % 2) + j // 4


def corner_weight(i, side):
    place = (i.astype(F32) + 0.5) * (1.0 / BE)
    return jnp.where(side == 1, place, 1.0 - place)


def kernel(
    n_wide,
    n_four,
    raw_in,
    volt_in,
    states_in,
    routes_in,
    base_in,
    nodes_in,
    perm_in,
    stiff_in,
    fmap_in,
    smap_in,
    pot_out,
    states_out,
    disp_out,
    raw,
    par,
    volt,
    routes,
    base,
    nodes,
    perm,
    stiff,
    fmap,
    smap,
    ust,
    vb,
    xh,
    yh,
    yf,
    ex,
    tens,
    tbuf,
    posb,
    lhi,
    llo,
    onehot,
    abuf,
    vsp,
    nlo,
    nhi,
    kf,
    ks,
    kt,
    dvec,
    wz,
    k8b,
    txb,
    vals,
    ndb,
    asm_s,
    asm_r,
    snd2,
    rcv2,
    snd1,
    rcv1,
    dma_in,
    dma_small,
    hs,
    hr,
    a2s,
    a2r,
    ass,
    asr,
    rounds,
    gu,
    gplane,
    grow_s,
    grow_r,
    os,
    orv,
    gs,
    gr,
):
    count = n_wide * n_four
    wide = lax.axis_index("wide")
    four = lax.axis_index("four")
    me = wide * n_four + four
    barrier = pltpu.get_barrier_semaphore()

    ring = (wide // 16, (wide // 4) % 4, wide % 4, four)
    extent = (2, 4, 4, 4)

    def place(y, z, x, f):
        return {"wide": y * 16 + z * 4 + x, "four": f}

    def along(axis):
        for step in range(1, extent[axis]):
            spot = list(ring)
            spot[axis] = (spot[axis] + step) % extent[axis]
            yield place(*spot)

    def others(act):
        def some(g, c):
            a, b = g // 4, g % 4
            z = (ring[1] + 2 + 3 * a + 3 * ((a * a - a) // 2)) % 4
            x = (ring[2] + 2 + 3 * b + 3 * ((b * b - b) // 2)) % 4
            for dy in (1, 0):
                w = ((ring[0] + dy) % 2) * 16 + z * 4 + x
                for df in (2, 3, 1, 0):
                    f = (four + df) % 4

                    def go(w=w, f=f):
                        act(w * n_four + f, {"wide": w, "four": f})

                    if dy == 0 and df == 0:
                        pl.when(g < 15)(go)
                    else:
                        go()
            return c

        lax.fori_loop(0, 16, some, 0)

    small = [
        pltpu.make_async_copy(src, dst, dma_small.at[i])
        for i, (src, dst) in enumerate(
            [(raw_in[j], raw.at[j]) for j in range(6)]
            + [
                (routes_in, routes),
                (base_in, base),
                (volt_in, volt),
                (nodes_in, nodes),
                (perm_in, perm),
                (stiff_in, stiff),
                (fmap_in, fmap),
                (smap_in, smap),
            ]
        )
    ]
    for copy in small[:9]:
        copy.start()

    def load_group(g):
        part = pl.ds(g * GP, GP)
        return pltpu.make_async_copy(states_in.at[:, part], ust.at[:, part], dma_in.at[g])

    for g in range(GROUPS):
        load_group(g).start()
    for copy in small[9:]:
        copy.start()
    def greet(device):
        pl.semaphore_signal(barrier, inc=1, device_id=device, device_id_type=MESH)

    for axis in range(4):
        for device in along(axis):
            greet(device)
    at_x_end, at_x_start = wide % 4 == 3, wide % 4 == 0
    extra = (
        (at_x_end & (wide < n_wide - 1), {"wide": wide + 1, "four": four}),
        (at_x_start & (wide > 0), {"wide": wide - 1, "four": four}),
        ((four == n_four - 1) & (wide < n_wide - 1), {"wide": wide + 1, "four": 0 * four}),
        ((four == 0) & (wide > 0), {"wide": wide - 1, "four": 0 * four + n_four - 1}),
    )
    for cond, device in extra:
        pl.when(cond)(functools.partial(greet, device))
    pl.semaphore_wait(barrier, 10 + sum(cond.astype(jnp.int32) for cond, _ in extra))

    def meet(axis):
        for device in along(axis):
            pl.semaphore_signal(rounds.at[axis], inc=1, device_id=device, device_id_type=MESH)

    def met(axis):
        pl.semaphore_wait(rounds.at[axis], extent[axis] - 1)

    meet(0)
    has = (wide > 0, wide < n_wide - 1, four > 0, four < n_four - 1)
    opposite = (1, 0, 3, 2)
    peers = ((wide - 1, four), (wide + 1, four), (wide, four - 1), (wide, four + 1))

    def field(n):
        return volt if n == 0 else vb.at[n - 1]

    half = n_wide // 2
    slow_low, slow_high = wide == half - 1, wide == half
    slow = slow_low | slow_high
    across = {"wide": jnp.where(slow_low, half, half - 1), "four": four}
    edge = jnp.where(slow_low, PX - 1, 0)
    second = jnp.where(slow_low, PX - 2, 1)
    shut = (slow_high, slow_low, False, False)

    def talks(n, d):
        return has[d] & ~shut[d] if n in SKIPPED and d < 2 else has[d]

    def over(i):
        src, dst = (
            (states_in.at[:, edge], gu),
            (vb.at[0, second], gplane.at[0]),
            (vb.at[4, second], gplane.at[1]),
            (ex.at[edge], gplane.at[2]),
        )[i]
        return pltpu.make_async_remote_copy(
            src_ref=src, dst_ref=dst, send_sem=os.at[i], recv_sem=orv.at[i], device_id=across, device_id_type=MESH
        )

    def rows_copy(m, d):
        return pltpu.make_async_remote_copy(
            src_ref=grow_s.at[m, d],
            dst_ref=grow_r.at[m, 1 - d],
            send_sem=gs.at[m, d],
            recv_sem=gr.at[m, d],
            device_id=peers[2 + d],
            device_id_type=MESH,
        )

    def halo(n, d):
        v = field(n)
        src = (v.at[0], v.at[PX - 1], yf.at[n, 0], yf.at[n, 1])[d]
        dst = (xh.at[n, 1], xh.at[n, 0], yh.at[n, 1], yh.at[n, 0])[d]
        return pltpu.make_async_remote_copy(
            src_ref=src,
            dst_ref=dst,
            send_sem=hs.at[n, d],
            recv_sem=hr.at[n, d],
            device_id=peers[d],
            device_id_type=MESH,
        )

    def start_halo(n):
        v = field(n)
        yf[n, 0] = v[:, 0, :]
        yf[n, 1] = v[:, PY - 1, :]
        for d in range(4):

            @pl.when(talks(n, d))
            def _():
                halo(n, d).start()

    def finish_halo(n):
        v, w = field(n), vb.at[n]

        for d in range(4):

            @pl.when(talks(n, opposite[d]))
            def _():
                halo(n, d).wait_recv()

            @pl.when(has[opposite[d]])
            def _():
                if d == 0:
                    w[PX - 1] = w[PX - 1] + (DT * DX) * (xh[n, 1] - v[PX - 1])
                elif d == 1:
                    w[0] = w[0] + (DT * DX) * (xh[n, 0] - v[0])
                elif d == 2:
                    w[:, PY - 1, :] = w[:, PY - 1, :] + (DT * DY) * (yh[n, 1] - v[:, PY - 1, :])
                else:
                    w[:, 0, :] = w[:, 0, :] + (DT * DY) * (yh[n, 0] - v[:, 0, :])

    def finish_sends(n):
        for d in range(4):

            @pl.when(talks(n, d))
            def _():
                halo(n, d).wait_send()

    shape = (TWO, PY // NROW, NROW, LANES)
    lane = iota((PY, PZ), 1)

    def planes(n, first, last, with_excess=False, opening=False, tension=False, flow_only=False, closing=False):
        v_ref, w_ref = field(n), vb.at[n]

        def body(g, c):
            i = g * TWO
            v = v_ref[pl.ds(i, TWO)].reshape(shape)
            total_a = jnp.broadcast_to(par[9, 0], shape)
            total_b = jnp.broadcast_to(par[9, 1], shape)
            total_t = jnp.broadcast_to(par[9, 2], shape)
            for k in range(NK):
                old = ust[k, pl.ds(i, TWO)].reshape(shape)
                if flow_only:
                    total_a = total_a + old
                    total_b = total_b + old * par[4, k]
                    continue
                t = jnp.tanh(v * par[0, k] + par[1, k])
                if opening:
                    u = old * par[5, k] + (t * par[3, k] + par[6, k])
                else:
                    u = old * par[2, k] + t * par[3, k]
                if closing:
                    states_out[k, pl.ds(i, TWO)] = (u * par[7, k] + 0.5).reshape(TWO, PY, PZ)
                else:
                    ust[k, pl.ds(i, TWO)] = u.reshape(TWO, PY, PZ)
                if tension:
                    total_t = total_t + u * par[8, k]
                else:
                    total_a = total_a + u
                    total_b = total_b + u * par[4, k]
            if tension:
                tens[pl.ds(i, TWO)] = total_t.reshape(TWO, PY, PZ)
                return c
            current = (v * total_a - total_b).reshape(TWO, PY, PZ)
            for h in range(TWO):
                j = i + h
                v = v_ref[j]
                flow = current[h]
                if with_excess:
                    flow = flow + GAIN * ex[j] * (v - STRETCH_REV)
                near_x = v_ref[jnp.maximum(j - 1, 0)] + v_ref[jnp.minimum(j + 1, PX - 1)]
                near_y = jnp.concatenate([v[:1], v[:-1]], 0) + jnp.concatenate([v[1:], v[-1:]], 0)
                near_z = jnp.where(lane == 0, v, pltpu.roll(v, 1, 1)) + jnp.where(
                    lane == PZ - 1, v, pltpu.roll(v, PZ - 1, 1)
                )
                lap = DX * near_x + DY * near_y + DZ * near_z - (2.0 * (DX + DY + DZ)) * v
                w_ref[j] = v + DT * (lap - flow)
            return c

        lax.fori_loop(first // TWO, last // TWO, body, 0)

    def ghost_plane(n):
        return jnp.where(slow_low, xh[n, 1], xh[n, 0])

    def ghost_states(n, opening=False):
        v = ghost_plane(n).reshape(shape[1:])
        total_a = jnp.broadcast_to(par[9, 0], shape[1:])
        total_b = jnp.broadcast_to(par[9, 1], shape[1:])
        for k in range(NK):
            t = jnp.tanh(v * par[0, k] + par[1, k])
            old = gu[k].reshape(shape[1:])
            if opening:
                u = old * par[5, k] + (t * par[3, k] + par[6, k])
            else:
                u = old * par[2, k] + t * par[3, k]
            gu[k] = u.reshape(PY, PZ)
            total_a = total_a + u
            total_b = total_b + u * par[4, k]
        return (v * total_a - total_b).reshape(PY, PZ)

    def on_slow(act):
        pl.when(slow)(act)

    def ghost_opening():
        @on_slow
        def _():
            over(0).wait_recv()
            ghost_states(0, opening=True)

    def ghost_later(n):
        @on_slow
        def _():
            ghost_states(n)

    def ghost_rows(m, n):
        @on_slow
        def _():
            over(1 + m).wait_recv()
            v = ghost_plane(n)
            grow_s[m, 0] = v[0:1]
            grow_s[m, 1] = v[PY - 1 :]
            for d in range(2):
                pl.when(has[2 + d])(lambda d=d: rows_copy(m, d).start())

    def ghost_step(m, n, with_excess):
        @on_slow
        def _():
            flow = ghost_states(n)
            v = ghost_plane(n)
            if with_excess:
                over(3).wait_recv()
                flow = flow + GAIN * gplane[2] * (v - STRETCH_REV)
            grow_r[m, 2] = v[0:1]
            grow_r[m, 3] = v[PY - 1 :]
            for d in range(2):

                @pl.when(has[2 + 1 - d])
                def _():
                    rows_copy(m, d).wait_recv()
                    grow_r[m, 2 + 1 - d] = grow_r[m, 1 - d]

            below, above = grow_r[m, 2], grow_r[m, 3]
            near_x = field(n)[edge] + gplane[m]
            near_y = jnp.concatenate([below, v[:-1]], 0) + jnp.concatenate([v[1:], above], 0)
            near_z = jnp.where(lane == 0, v, pltpu.roll(v, 1, 1)) + jnp.where(
                lane == PZ - 1, v, pltpu.roll(v, PZ - 1, 1)
            )
            lap = DX * near_x + DY * near_y + DZ * near_z - (2.0 * (DX + DY + DZ)) * v
            fresh = v + DT * (lap - flow)

            @pl.when(slow_low)
            def _():
                xh[n + 1, 1] = fresh

            @pl.when(slow_high)
            def _():
                xh[n + 1, 0] = fresh

    def ghost_sent():
        @on_slow
        def _():
            for i in range(4):
                over(i).wait_send()
            for m in range(2):
                for d in range(2):
                    pl.when(has[2 + d])(lambda m=m, d=d: rows_copy(m, d).wait_send())

    sent, got = (snd2, snd1), (rcv2, rcv1)

    def send_rows(s):
        def one(t, device):
            pltpu.make_async_remote_copy(
                src_ref=sent[s].at[t],
                dst_ref=got[s].at[me],
                send_sem=a2s.at[s],
                recv_sem=a2r.at[s],
                device_id=device,
                device_id_type=MESH,
            ).start()

        others(one)
        got[s][me] = sent[s][me]

    def wait_rows(s):
        part = got[s].at[pl.ds(0, count - 1)]
        pltpu.make_async_copy(part, part, a2r.at[s]).wait()

    def wait_sent(s):
        part = sent[s].at[pl.ds(0, count - 1)]
        pltpu.make_async_copy(part, part, a2s.at[s]).wait()

    small[8].wait()
    start_halo(0)
    on_slow(lambda: over(0).start())
    for copy in small[:8]:
        copy.wait()
    def spread_scalar(x):
        return jnp.full((NROW, LANES), x, F32)

    sums = [jnp.zeros((NROW, LANES), F32) for _ in range(3)]
    for k in range(NK):
        half, slope, keep, cond, rev, weight = [spread_scalar(raw[j, 0, k]) for j in range(6)]
        inv_slope, inv_cond = 0.5 / slope, 1.0 / cond
        entries = (
            inv_slope,
            -half * inv_slope,
            keep,
            0.5 * cond * (1.0 - keep),
            rev,
            keep * cond,
            -0.5 * keep * cond,
            inv_cond,
            weight * inv_cond,
        )
        for j, entry in enumerate(entries):
            par[j, k] = entry
        sums = [sums[0] + 0.5 * cond, sums[1] + 0.5 * cond * rev, sums[2] + 0.5 * weight]
    for j in range(3):
        par[9, j] = sums[j]

    met(0)
    meet(1)
    for g in range(GROUPS):
        load_group(g).wait()
        planes(0, g * GP, (g + 1) * GP, opening=True)

    met(1)
    meet(2)

    tri = jnp.where((iota((LANES, 256), 0) < iota((LANES, 256), 1)), 1.0, 0.0).astype(BF16)
    carry = jnp.zeros((count, LANES), F32)
    for r in range(NROW):
        hot = jnp.broadcast_to(routes[r : r + 1, :], (count, LANES)) == iota((count, LANES), 0)
        hot_f = jnp.where(hot, 1.0, 0.0)
        hot_b = hot_f.astype(BF16)
        tbuf[:, r * LANES : (r + 1) * LANES] = hot_b
        run = dot(hot_b, tri)
        before = run[:, :LANES] + carry
        carry = carry + run[:, LANES:]
        posb[r : r + 1, :] = jnp.sum(before * hot_f, axis=0, keepdims=True).astype(jnp.int32)

    slot_row = lax.rem(iota((LANES, LANES), 0), MOST)

    def here(r):
        return jnp.broadcast_to(posb[r : r + 1, :], (LANES, LANES)) == slot_row

    def placed():
        return dot(tbuf[...], lhi[...], NT) + dot(tbuf[...], llo[...], NT)

    for r in range(NROW):
        row = jnp.broadcast_to(base[r : r + 1, :], (LANES, LANES))
        h, l = split2(jnp.where(here(r), row, 0.0))
        lhi[:, r * LANES : (r + 1) * LANES] = h
        llo[:, r * LANES : (r + 1) * LANES] = l
    snd2[:, 1, :] = placed()


    finish_halo(0)
    start_halo(1)
    on_slow(lambda: over(1).start())
    planes(1, 0, PX)
    met(2)
    meet(3)

    for copy in small[9:]:
        copy.wait()
    row8, block = iota((NROW, LANES), 0), iota((NROW, LANES), 1) // MOST
    for t in range(count // NROW):
        x = nodes[:, t * LANES : (t + 1) * LANES]
        for bit in (1, 2, 4):
            up = pltpu.roll(pltpu.roll(x, NROW - bit, 0), MOST * bit, 1)
            down = pltpu.roll(pltpu.roll(x, bit, 0), LANES - MOST * bit, 1)
            row_bit, block_bit = (row8 // bit) % 2, (block // bit) % 2
            x = jnp.where(row_bit < block_bit, up, jnp.where(row_bit > block_bit, down, x))
        nlo[t * NROW : (t + 1) * NROW, :] = lax.rem(x, LANES)
        nhi[t * NROW : (t + 1) * NROW, :] = x // LANES

    def hot_chunk(ch, c):
        for j in range(16):
            row = nlo[pl.ds(ch * 16 + j, 1), :]
            hit = jnp.broadcast_to(row, (LANES, LANES)) == iota((LANES, LANES), 0)
            onehot[ch, :, j * LANES : (j + 1) * LANES] = jnp.where(hit, 1.0, 0.0).astype(BF16)
        return c

    lax.fori_loop(0, 8, hot_chunk, 0)
    ghost_opening()
    finish_halo(1)
    ghost_rows(0, 1)
    start_halo(2)
    planes(2, 0, PX)

    zi, zj = iota((LANES, 256), 0), iota((LANES, 256), 1)
    wz[...] = jnp.where(
        zi // BE == lax.rem(zj, 32), corner_weight(lax.rem(zi, BE), zj // LANES), 0.0
    ).astype(BF16)
    pi, pj = iota((32, 64), 0), iota((32, 64), 1)
    wp = jnp.where(pi // 16 == pj // 32, corner_weight(lax.rem(pi, BE), (pj // 16) % 2), 0.0).astype(BF16)
    ti, tj = iota((64, 32), 0), iota((64, 32), 1)
    wpt = jnp.where(tj // 16 == ti // 32, corner_weight(lax.rem(tj, BE), (ti // 16) % 2), 0.0).astype(BF16)
    band = (iota((256, 256), 0) % 16) // BE == (iota((256, 256), 1) // 32) % BE
    met(3)
    ghost_step(0, 1, False)
    finish_halo(2)
    start_halo(3)
    planes(3, 0, PX, tension=True)

    for r in range(NROW):
        a, bh = r // 2, r % 2
        for x in range(2):
            acc = None
            for i in range(BE):
                share = (i + 0.5) / BE
                term = tens[BE * a + i, bh * 16 : (bh + 1) * 16, :] * (
                    (share if x else 1.0 - share) / (BE / 2.0) ** 3
                )
                acc = term if acc is None else acc + term
            txb[r * 32 + x * 16 : r * 32 + (x + 1) * 16, :] = acc
    h, l = split2(txb[...])
    along = jnp.where(band, dot(h, wz[...]) + dot(l, wz[...]), 0.0)
    for r in range(NROW):
        h, l = split2(along[r * 32 : (r + 1) * 32])
        both = dot(wpt, h) + dot(wpt, l)
        full = jnp.concatenate([both[:, :LANES], both[:, LANES:]], axis=0)
        h, l = split2(jnp.where(here(r), full, 0.0))
        lhi[:, r * LANES : (r + 1) * LANES] = h
        llo[:, r * LANES : (r + 1) * LANES] = l
    snd2[:, 0, :] = placed()
    send_rows(0)

    planes(3, 0, PX, flow_only=True)
    finish_halo(3)
    start_halo(4)

    rd = jnp.where(iota((24, 384), 0) == iota((24, 384), 1) // MOST, 1.0, 0.0).astype(BF16)
    rdt = jnp.where(iota((384, 24), 1) == iota((384, 24), 0) // MOST, 1.0, 0.0).astype(BF16)
    rj = jnp.where(iota((LANES, 8), 1) == corner_of(iota((LANES, 8), 0) // MOST), 1.0, 0.0).astype(BF16)
    rjt = jnp.where(iota((8, LANES), 0) == corner_of(iota((8, LANES), 1) // MOST), 1.0, 0.0).astype(BF16)

    def kron(left, part, right, rows, cols, dims=NT):
        full = dot(dot(left, part, dims).astype(BF16), right)
        same = lax.rem(iota((rows, cols), 0), MOST) == lax.rem(iota((rows, cols), 1), MOST)
        return jnp.where(same, full, 0.0).astype(BF16)

    for s, part in enumerate(split2(fmap[...])):
        kf[s] = kron(rj, part, rd, LANES, 384, NN)
    for s, part in enumerate(split2(stiff[...])):
        ks[s] = kron(rdt, part, rd, 384, 384)
    for s, part in enumerate(split2(smap[...])):
        kt[s] = kron(rdt, part, rjt, 384, LANES)
    eye = jnp.where(iota((24, 24), 0) == iota((24, 24), 1), stiff[...], 0.0)
    dh, dl = split2(jnp.broadcast_to(jnp.sum(eye, axis=0, keepdims=True), (8, 24)))
    dvec[...] = dot(dh, rd) + dot(dl, rd)
    mean8 = jnp.where(
        lax.rem(iota((LANES, LANES), 0), MOST) == lax.rem(iota((LANES, LANES), 1), MOST), 0.125, 0.0
    ).astype(BF16)
    pair = jnp.where(
        jnp.broadcast_to(perm[...], (LANES, LANES)) == iota((LANES, LANES), 0), 1.0, 0.0
    ).astype(BF16)
    back = dot(iota((8, LANES), 1).astype(F32).astype(BF16), pair, NT).astype(jnp.int32)


    def spread(comps):
        rows = 2 * comps * NROW
        for c in range(comps):
            h, l = split2(vals[c])
            vsp[0, c] = h.astype(F32)
            vsp[1, c] = l.astype(F32)

        def chunk(ch, acc):
            for j in range(16):
                p = ch * 16 + j
                hit = jnp.broadcast_to(nhi[pl.ds(p, 1), :], (NROW, LANES)) == iota((NROW, LANES), 0)
                column = []
                for s in range(2):
                    for c in range(comps):
                        row = jnp.broadcast_to(vsp[s, c, pl.ds(p, 1), :], (NROW, LANES))
                        column.append(jnp.where(hit, row, 0.0))
                abuf[0:rows, j * LANES : (j + 1) * LANES] = jnp.concatenate(column, axis=0).astype(BF16)
            return acc + dot(abuf[0:rows, :], onehot[ch], NT)

        acc = lax.fori_loop(0, 8, chunk, jnp.zeros((rows, LANES), F32))
        both = acc[: rows // 2] + acc[rows // 2 :]
        for c in range(comps):
            ndb[c] = both[c * NROW : (c + 1) * NROW]

    def shared(s, to):
        peer = me - 1 if to == 0 else me + 1
        return pltpu.make_async_remote_copy(
            src_ref=asm_s.at[s, to],
            dst_ref=asm_r.at[s, to],
            send_sem=ass.at[s, to],
            recv_sem=asr.at[s, to],
            device_id=(peer // n_four, lax.rem(peer, n_four)),
            device_id_type=MESH,
        )

    has_before, has_after = me > 0, me < count - 1

    def assemble(s, comps):
        lead = jnp.concatenate([ndb[c, 0:1, :] for c in range(comps)] + [jnp.zeros((NROW - comps, LANES), F32)], axis=0)
        trail = jnp.concatenate(
            [ndb[c, NROW - 1 :, :] for c in range(comps)] + [jnp.zeros((NROW - comps, LANES), F32)], axis=0
        )
        asm_s[s, 0] = jnp.take_along_axis(lead, back, axis=1)
        asm_s[s, 1] = trail

        @pl.when(has_before)
        def _():
            shared(s, 0).start()

        @pl.when(has_after)
        def _():
            shared(s, 1).start()

        @pl.when(has_after)
        def _():
            shared(s, 0).wait_recv()
            for c in range(comps):
                ndb[c, NROW - 1 :, :] = ndb[c, NROW - 1 :, :] + asm_r[s, 0, c : c + 1, :]

        @pl.when(has_before)
        def _():
            shared(s, 1).wait_recv()
            order = jnp.broadcast_to(perm[...], (NROW, LANES))
            got = jnp.take_along_axis(asm_r[s, 1], order, axis=1)
            for c in range(comps):
                ndb[c, 0:1, :] = ndb[c, 0:1, :] + got[c : c + 1]

        @pl.when(has_before)
        def _():
            shared(s, 0).wait_send()

        @pl.when(has_after)
        def _():
            shared(s, 1).wait_send()

    def collect(table):
        def tiles(g, carry_in):
            for j in range(4):
                rows = pl.ds(g * 32 + j * NROW, NROW)
                low, high = nlo[rows, :], nhi[rows, :]
                masks = [high == hi for hi in range(NROW)]
                for c in range(3):
                    out = jnp.zeros((NROW, LANES), F32)
                    for hi in range(NROW):
                        line = jnp.broadcast_to(ndb[6 + c, hi : hi + 1, :], (NROW, LANES))
                        out = jnp.where(masks[hi], jnp.take_along_axis(line, low, axis=1), out)
                    vals[c, rows, :] = out
            return carry_in

        for c in range(3):
            ndb[6 + c] = table[c]
        lax.fori_loop(0, 4, tiles, 0)
        return jnp.concatenate([vals[0], vals[1], vals[2]], axis=1)

    def times(x, table):
        h, l = split2(x)
        return dot(h, table[0]) + dot(l, table[0]) + dot(h, table[1])

    planes(4, 0, PX)

    wait_rows(0)
    arrived = rcv2[:, 0, :]
    h, l = split2(arrived)
    k8 = rcv2[:, 1, :] * (1.0 + 0.5 * jnp.tanh(dot(h, mean8) + dot(l, mean8)))
    k8b[...] = k8
    force = times(arrived, kf)
    for c in range(3):
        part = slice(c * LANES, (c + 1) * LANES)
        vals[c] = force[:, part]
        vals[3 + c] = k8 * dvec[0:1, part]
    spread(6)
    assemble(0, 6)
    forces = [ndb[c] for c in range(3)]
    diagonal = [SPRING + ndb[3 + c] for c in range(3)]
    guess = [RELAX * f / d for f, d in zip(forces, diagonal)]
    pushed = times(collect(guess), ks)
    for c in range(3):
        vals[c] = k8b[...] * pushed[:, c * LANES : (c + 1) * LANES]
    spread(3)
    assemble(1, 3)
    moved = []
    for c in range(3):
        applied = SPRING * guess[c] + ndb[c]
        moved.append(guess[c] + RELAX * (forces[c] - applied) / diagonal[c])
        for hi in range(NROW):
            disp_out[c : c + 1, hi * LANES : (hi + 1) * LANES] = moved[c][hi : hi + 1]
    strain = times(collect(moved), kt)
    snd1[...] = strain.reshape(count, 1, LANES)
    send_rows(1)
    finish_halo(4)
    for n in (2, 3, 4):
        ghost_later(n)
    wait_rows(1)

    h, l = split2(rcv1[...].reshape(count, LANES).T)
    mine = dot(h, tbuf[...]) + dot(l, tbuf[...])
    for r in range(NROW):
        own = jnp.where(here(r), mine[:, r * LANES : (r + 1) * LANES], 0.0)
        h, l = split2(jnp.concatenate([own[:64], own[64:]], axis=1))
        along = jnp.where(band[:32], dot(wp, h) + dot(wp, l), 0.0)
        h, l = split2(along)
        fine = dot(h, wz[...], NT) + dot(l, wz[...], NT)
        a, bh = r // 2, r % 2
        for i in range(BE):
            share = (i + 0.5) / BE
            ex[BE * a + i, bh * 16 : (bh + 1) * 16, :] = (1.0 - share) * fine[:16] + share * fine[16:]

    def add_excess(i, c):
        vb[4, i] = vb[4, i] - (DT * GAIN) * ex[i] * (vb[3, i] - STRETCH_REV)
        return c

    lax.fori_loop(0, PX, add_excess, 0)
    start_halo(5)
    on_slow(lambda: over(2).start())
    on_slow(lambda: over(3).start())
    planes(5, 0, PX, with_excess=True)
    finish_halo(5)
    ghost_rows(1, 5)
    start_halo(6)
    planes(6, 0, PX, with_excess=True)
    ghost_step(1, 5, True)
    finish_halo(6)
    start_halo(7)

    planes(7, 0, PX, with_excess=True, closing=True)
    finish_halo(7)
    pot_out[...] = vb[7]
    for n in range(8):
        finish_sends(n)
    ghost_sent()
    for s in range(2):
        wait_sent(s)


def put_out(pot, states, disp, pot_out, states_out, disp_out, sem):
    copies = [
        pltpu.make_async_copy(src, dst, sem.at[i])
        for i, (src, dst) in enumerate(((states, states_out), (pot, pot_out), (disp, disp_out)))
    ]
    for copy in copies:
        copy.start()
    for copy in copies:
        copy.wait()


def in_hbm(x):
    return pltpu.with_memory_space_constraint(x, pltpu.HBM)


def per_device(
    n_wide,
    n_four,
    voltage,
    states,
    half_volt,
    gate_slope,
    retention,
    conduct,
    reversal,
    tension_weights,
    routes,
    base_stiff,
    elem_nodes,
    share_perm,
    stiffness,
    force_map,
    strain_map,
):
    count = n_wide * n_four
    vmem = pl.BlockSpec(memory_space=pltpu.VMEM)
    hbm = pl.BlockSpec(memory_space=pltpu.HBM)
    scratch = [
        pltpu.SMEM((6, 1, NK), F32),
        pltpu.VMEM((10, NK, NROW, LANES), F32),
        pltpu.VMEM((PX, PY, PZ), F32),
        pltpu.VMEM((NROW, LANES), jnp.int32),
        pltpu.VMEM((NROW, LANES), F32),
        pltpu.VMEM((8, count * MOST), jnp.int32),
        pltpu.VMEM((1, LANES), jnp.int32),
        pltpu.VMEM((24, 24), F32),
        pltpu.VMEM((8, 24), F32),
        pltpu.VMEM((8, 24), F32),
        pltpu.VMEM((NK, PX, PY, PZ), F32),
        pltpu.VMEM((8, PX, PY, PZ), F32),
        pltpu.VMEM((8, 2, PY, PZ), F32),
        pltpu.VMEM((8, 2, PX, PZ), F32),
        pltpu.VMEM((8, 2, PX, PZ), F32),
        pltpu.VMEM((PX, PY, PZ), F32),
        pltpu.VMEM((PX, PY, PZ), F32),
        pltpu.VMEM((count, 1024), BF16),
        pltpu.VMEM((NROW, LANES), jnp.int32),
        pltpu.VMEM((LANES, 1024), BF16),
        pltpu.VMEM((LANES, 1024), BF16),
        pltpu.VMEM((8, LANES, 2048), BF16),
        pltpu.VMEM((96, 2048), BF16),
        pltpu.VMEM((2, 6, count, LANES), F32),
        pltpu.VMEM((count, LANES), jnp.int32),
        pltpu.VMEM((count, LANES), jnp.int32),
        pltpu.VMEM((2, LANES, 384), BF16),
        pltpu.VMEM((2, 384, 384), BF16),
        pltpu.VMEM((2, 384, LANES), BF16),
        pltpu.VMEM((8, 384), F32),
        pltpu.VMEM((LANES, 256), BF16),
        pltpu.VMEM((count, LANES), F32),
        pltpu.VMEM((256, LANES), F32),
        pltpu.VMEM((6, count, LANES), F32),
        pltpu.VMEM((9, NROW, LANES), F32),
        pltpu.VMEM((2, 2, NROW, LANES), F32),
        pltpu.VMEM((2, 2, NROW, LANES), F32),
        pltpu.VMEM((count, 2, LANES), F32),
        pltpu.VMEM((count, 2, LANES), F32),
        pltpu.VMEM((count, 1, LANES), F32),
        pltpu.VMEM((count, 1, LANES), F32),
        pltpu.SemaphoreType.DMA((GROUPS,)),
        pltpu.SemaphoreType.DMA((14,)),
        pltpu.SemaphoreType.DMA((8, 4)),
        pltpu.SemaphoreType.DMA((8, 4)),
        pltpu.SemaphoreType.DMA((2,)),
        pltpu.SemaphoreType.DMA((2,)),
        pltpu.SemaphoreType.DMA((2, 2)),
        pltpu.SemaphoreType.DMA((2, 2)),
        pltpu.SemaphoreType.REGULAR((4,)),
        pltpu.VMEM((NK, PY, PZ), F32),
        pltpu.VMEM((3, PY, PZ), F32),
        pltpu.VMEM((2, 2, 1, LANES), F32),
        pltpu.VMEM((2, 4, 1, LANES), F32),
        pltpu.SemaphoreType.DMA((4,)),
        pltpu.SemaphoreType.DMA((4,)),
        pltpu.SemaphoreType.DMA((2, 2)),
        pltpu.SemaphoreType.DMA((2, 2)),
    ]
    made = pl.pallas_call(
        functools.partial(kernel, n_wide, n_four),
        out_shape=(
            jax.ShapeDtypeStruct((PX, PY, PZ), F32),
            jax.ShapeDtypeStruct((NK, PX, PY, PZ), F32),
            jax.ShapeDtypeStruct((3, NROW * LANES), F32),
        ),
        in_specs=[[hbm] * 6] + [hbm] * 9,
        out_specs=(vmem, vmem, vmem),
        scratch_shapes=scratch,
        compiler_params=pltpu.CompilerParams(
            collective_id=0, has_side_effects=True, vmem_limit_bytes=40 << 20
        ),
    )(
        [
            in_hbm(x.reshape(1, NK))
            for x in (half_volt, gate_slope, retention, conduct, reversal, tension_weights)
        ],
        in_hbm(voltage),
        in_hbm(states),
        in_hbm(routes.reshape(NROW, LANES)),
        in_hbm(base_stiff.reshape(NROW, LANES)),
        in_hbm(elem_nodes),
        in_hbm(share_perm),
        in_hbm(stiffness),
        in_hbm(force_map.T),
        in_hbm(strain_map),
    )
    return pl.pallas_call(
        put_out,
        out_shape=[jax.ShapeDtypeStruct(x.shape, x.dtype) for x in made],
        in_specs=[vmem] * 3,
        out_specs=[hbm] * 3,
        scratch_shapes=[pltpu.SemaphoreType.DMA((3,))],
        compiler_params=pltpu.CompilerParams(vmem_limit_bytes=1 << 20),
    )(*made)


def solution(mesh):
    placed = (
        P("wide", "four", None),
        P(None, "wide", "four", None),
        P(),
        P(),
        P(),
        P(),
        P(),
        P(),
        P(("wide", "four"), None),
        P(("wide", "four")),
        P(None, ("wide", "four")),
        P(("wide", "four"), None),
        P(),
        P(),
        P(),
    )
    return jax.shard_map(
        functools.partial(per_device, mesh.shape["wide"], mesh.shape["four"]),
        mesh=mesh,
        in_specs=placed,
        out_specs=(
            P("wide", "four", None),
            P(None, "wide", "four", None),
            P(None, ("wide", "four")),
        ),
        check_vma=False,
    )
```

```python
import functools

import jax
import jax.numpy as jnp
from jax import lax
from jax.experimental import pallas as pl
from jax.experimental.pallas import tpu as pltpu
from jax.sharding import PartitionSpec as P

BE = 4
NK = 20
PX, PY, PZ = 16, 32, 128
NROW = 8
LANES = 128
MOST = 16
F32, BF16 = jnp.float32, jnp.bfloat16
DT = 0.1
DX, DY, DZ = 1.5, 1.0, 0.6
GAIN, STRETCH_REV = 2.0, 0.5
SPRING, RELAX = 1.0, 0.7
GROUPS = 4
TWO = 2
SKIPPED = (2, 6, 7)
GP = PX // GROUPS
MESH = pl.DeviceIdType.MESH
NN = (((1,), (0,)), ((), ()))
NT = (((1,), (1,)), ((), ()))


def dot(a, b, dims=NN):
    return lax.dot_general(a, b, dims, preferred_element_type=F32)


def split2(x):
    high = x.astype(BF16)
    return high, (x - high.astype(F32)).astype(BF16)


def iota(shape, dim):
    return lax.broadcasted_iota(jnp.int32, shape, dim)


def corner_of(j):
    return 4 * ((j // 2) % 2) + 2 * (j % 2) + j // 4


def corner_weight(i, side):
    place = (i.astype(F32) + 0.5) * (1.0 / BE)
    return jnp.where(side == 1, place, 1.0 - place)


def kernel(
    n_wide,
    n_four,
    raw_in,
    volt_in,
    states_in,
    routes_in,
    base_in,
    nodes_in,
    perm_in,
    stiff_in,
    fmap_in,
    smap_in,
    pot_out,
    states_out,
    disp_out,
    raw,
    par,
    volt,
    routes,
    base,
    nodes,
    perm,
    stiff,
    fmap,
    smap,
    ust,
    vb,
    xh,
    yh,
    yf,
    ex,
    tens,
    tbuf,
    posb,
    lhi,
    llo,
    onehot,
    abuf,
    vsp,
    nlo,
    nhi,
    kf,
    ks,
    kt,
    dvec,
    wz,
    k8b,
    txb,
    vals,
    ndb,
    asm_s,
    asm_r,
    snd2,
    rcv2,
    snd1,
    rcv1,
    dma_in,
    dma_small,
    hs,
    hr,
    a2s,
    a2r,
    ass,
    asr,
    rounds,
    gu,
    stage,
    gplane,
    grow_s,
    grow_r,
    os,
    orv,
    gs,
    gr,
):
    count = n_wide * n_four
    wide = lax.axis_index("wide")
    four = lax.axis_index("four")
    me = wide * n_four + four
    barrier = pltpu.get_barrier_semaphore()

    ring = (wide // 16, (wide // 4) % 4, wide % 4, four)
    extent = (2, 4, 4, 4)

    def place(y, z, x, f):
        return {"wide": y * 16 + z * 4 + x, "four": f}

    def along(axis):
        for step in range(1, extent[axis]):
            spot = list(ring)
            spot[axis] = (spot[axis] + step) % extent[axis]
            yield place(*spot)

    def others(act):
        def some(g, c):
            a, b = g // 4, g % 4
            z = (ring[1] + 2 + 3 * a + 3 * ((a * a - a) // 2)) % 4
            x = (ring[2] + 2 + 3 * b + 3 * ((b * b - b) // 2)) % 4
            for dy in (1, 0):
                w = ((ring[0] + dy) % 2) * 16 + z * 4 + x
                for df in (2, 3, 1, 0):
                    f = (four + df) % 4

                    def go(w=w, f=f):
                        act(w * n_four + f, {"wide": w, "four": f})

                    if dy == 0 and df == 0:
                        pl.when(g < 15)(go)
                    else:
                        go()
            return c

        lax.fori_loop(0, 16, some, 0)

    def greet(device):
        pl.semaphore_signal(barrier, inc=1, device_id=device, device_id_type=MESH)

    for axis in range(4):
        for device in along(axis):
            greet(device)
    at_x_end, at_x_start = wide % 4 == 3, wide % 4 == 0
    extra = (
        (at_x_end & (wide < n_wide - 1), {"wide": wide + 1, "four": four}),
        (at_x_start & (wide > 0), {"wide": wide - 1, "four": four}),
        ((four == n_four - 1) & (wide < n_wide - 1), {"wide": wide + 1, "four": 0 * four}),
        ((four == 0) & (wide > 0), {"wide": wide - 1, "four": 0 * four + n_four - 1}),
    )
    for cond, device in extra:
        pl.when(cond)(functools.partial(greet, device))
    small = [
        pltpu.make_async_copy(src, dst, dma_small.at[i])
        for i, (src, dst) in enumerate(
            [(raw_in[j], raw.at[j]) for j in range(6)]
            + [
                (routes_in, routes),
                (base_in, base),
                (volt_in, volt),
                (nodes_in, nodes),
                (perm_in, perm),
                (stiff_in, stiff),
                (fmap_in, fmap),
                (smap_in, smap),
            ]
        )
    ]
    for copy in small[:9]:
        copy.start()

    def load_group(g):
        part = pl.ds(g * GP, GP)
        return pltpu.make_async_copy(states_in.at[:, part], ust.at[:, part], dma_in.at[g])

    for g in range(GROUPS):
        load_group(g).start()
    for copy in small[9:]:
        copy.start()
    pl.semaphore_wait(barrier, 10 + sum(cond.astype(jnp.int32) for cond, _ in extra))

    def meet(axis):
        for device in along(axis):
            pl.semaphore_signal(rounds.at[axis], inc=1, device_id=device, device_id_type=MESH)

    def met(axis):
        pl.semaphore_wait(rounds.at[axis], extent[axis] - 1)

    meet(0)
    has = (wide > 0, wide < n_wide - 1, four > 0, four < n_four - 1)
    opposite = (1, 0, 3, 2)
    peers = ((wide - 1, four), (wide + 1, four), (wide, four - 1), (wide, four + 1))

    def field(n):
        return volt if n == 0 else vb.at[n - 1]

    def after(n):
        return pot_out if n == 7 else vb.at[n]

    half = n_wide // 2
    slow_low, slow_high = wide == half - 1, wide == half
    slow = slow_low | slow_high
    across = {"wide": jnp.where(slow_low, half, half - 1), "four": four}
    edge = jnp.where(slow_low, PX - 1, 0)
    second = jnp.where(slow_low, PX - 2, 1)
    third = jnp.where(slow_low, PX - 3, 2)
    shut = (slow_high, slow_low, False, False)

    def talks(n, d):
        return has[d] & ~shut[d] if n in SKIPPED and d < 2 else has[d]

    def over(i):
        src, dst = (
            (states_in.at[:, edge], gu.at[0]),
            (vb.at[0, second], gplane.at[0]),
            (vb.at[4, second], gplane.at[1]),
            (ex.at[edge], gplane.at[2]),
            (stage, gu.at[1]),
            (vb.at[3, second], gplane.at[3]),
            (vb.at[4, third], gplane.at[4]),
            (ex.at[second], gplane.at[5]),
        )[i]
        return pltpu.make_async_remote_copy(
            src_ref=src, dst_ref=dst, send_sem=os.at[i], recv_sem=orv.at[i], device_id=across, device_id_type=MESH
        )

    def rows_copy(m, d):
        return pltpu.make_async_remote_copy(
            src_ref=grow_s.at[m, d],
            dst_ref=grow_r.at[m, 1 - d],
            send_sem=gs.at[m, d],
            recv_sem=gr.at[m, d],
            device_id=peers[2 + d],
            device_id_type=MESH,
        )

    def halo(n, d):
        v = field(n)
        src = (v.at[0], v.at[PX - 1], yf.at[n, 0], yf.at[n, 1])[d]
        dst = (xh.at[n, 1], xh.at[n, 0], yh.at[n, 1], yh.at[n, 0])[d]
        return pltpu.make_async_remote_copy(
            src_ref=src,
            dst_ref=dst,
            send_sem=hs.at[n, d],
            recv_sem=hr.at[n, d],
            device_id=peers[d],
            device_id_type=MESH,
        )

    def start_halo(n):
        v = field(n)
        yf[n, 0] = v[:, 0, :]
        yf[n, 1] = v[:, PY - 1, :]
        for d in range(4):

            @pl.when(talks(n, d))
            def _():
                halo(n, d).start()

    def finish_halo(n):
        v, w = field(n), after(n)

        for d in range(4):

            @pl.when(talks(n, opposite[d]))
            def _():
                halo(n, d).wait_recv()

            @pl.when(has[opposite[d]])
            def _():
                if d == 0:
                    w[PX - 1] = w[PX - 1] + (DT * DX) * (xh[n, 1] - v[PX - 1])
                elif d == 1:
                    w[0] = w[0] + (DT * DX) * (xh[n, 0] - v[0])
                elif d == 2:
                    w[:, PY - 1, :] = w[:, PY - 1, :] + (DT * DY) * (yh[n, 1] - v[:, PY - 1, :])
                else:
                    w[:, 0, :] = w[:, 0, :] + (DT * DY) * (yh[n, 0] - v[:, 0, :])

    def finish_sends(n):
        for d in range(4):

            @pl.when(talks(n, d))
            def _():
                halo(n, d).wait_send()

    shape = (TWO, PY // NROW, NROW, LANES)
    lane = iota((PY, PZ), 1)

    def planes(n, first, last, with_excess=False, opening=False, tension=False, flow_only=False, closing=False):
        v_ref, w_ref = field(n), after(n)

        def body(g, c):
            i = g * TWO
            v = v_ref[pl.ds(i, TWO)].reshape(shape)
            total_a = jnp.broadcast_to(par[9, 0], shape)
            total_b = jnp.broadcast_to(par[9, 1], shape)
            total_t = jnp.broadcast_to(par[9, 2], shape)
            for k in range(NK):
                old = ust[k, pl.ds(i, TWO)].reshape(shape)
                if flow_only:
                    total_a = total_a + old
                    total_b = total_b + old * par[4, k]
                    continue
                t = jnp.tanh(v * par[0, k] + par[1, k])
                if opening:
                    u = old * par[5, k] + (t * par[3, k] + par[6, k])
                else:
                    u = old * par[2, k] + t * par[3, k]
                if closing:
                    states_out[k, pl.ds(i, TWO)] = (u * par[7, k] + 0.5).reshape(TWO, PY, PZ)
                else:
                    ust[k, pl.ds(i, TWO)] = u.reshape(TWO, PY, PZ)
                if tension:
                    total_t = total_t + u * par[8, k]
                else:
                    total_a = total_a + u
                    total_b = total_b + u * par[4, k]
            if tension:
                tens[pl.ds(i, TWO)] = total_t.reshape(TWO, PY, PZ)
                return c
            current = (v * total_a - total_b).reshape(TWO, PY, PZ)
            for h in range(TWO):
                j = i + h
                v = v_ref[j]
                flow = current[h]
                if with_excess:
                    flow = flow + GAIN * ex[j] * (v - STRETCH_REV)
                near_x = v_ref[jnp.maximum(j - 1, 0)] + v_ref[jnp.minimum(j + 1, PX - 1)]
                near_y = jnp.concatenate([v[:1], v[:-1]], 0) + jnp.concatenate([v[1:], v[-1:]], 0)
                near_z = jnp.where(lane == 0, v, pltpu.roll(v, 1, 1)) + jnp.where(
                    lane == PZ - 1, v, pltpu.roll(v, PZ - 1, 1)
                )
                lap = DX * near_x + DY * near_y + DZ * near_z - (2.0 * (DX + DY + DZ)) * v
                w_ref[j] = v + DT * (lap - flow)
            return c

        lax.fori_loop(first // TWO, last // TWO, body, 0)

    def ghost_plane(n):
        return jnp.where(slow_low, xh[n, 1], xh[n, 0])

    def ghost_states(which, plane, opening=False):
        v = plane.reshape(shape[1:])
        total_a = jnp.broadcast_to(par[9, 0], shape[1:])
        total_b = jnp.broadcast_to(par[9, 1], shape[1:])
        for k in range(NK):
            t = jnp.tanh(v * par[0, k] + par[1, k])
            old = gu[which, k].reshape(shape[1:])
            if opening:
                u = old * par[5, k] + (t * par[3, k] + par[6, k])
            else:
                u = old * par[2, k] + t * par[3, k]
            gu[which, k] = u.reshape(PY, PZ)
            total_a = total_a + u
            total_b = total_b + u * par[4, k]
        return (v * total_a - total_b).reshape(PY, PZ)

    def on_slow(act):
        pl.when(slow)(act)

    def cross(*items):
        @on_slow
        def _():
            for i in items:
                over(i).start()

    def ghost_opening():
        @on_slow
        def _():
            over(0).wait_recv()
            ghost_states(0, ghost_plane(0), opening=True)

    def ghost_later():
        @on_slow
        def _():
            for n in (2, 3, 4):
                ghost_states(0, ghost_plane(n))
            over(4).wait_recv()
            over(5).wait_recv()
            ghost_states(1, gplane[3])

    def ghost_rows(m, plane):
        grow_s[m, 0] = plane[0:1]
        grow_s[m, 1] = plane[PY - 1 :]
        for d in range(2):
            pl.when(has[2 + d])(lambda d=d: rows_copy(m, d).start())

    def ghost_fresh(m, v, near_x, flow):
        grow_r[m, 2] = v[0:1]
        grow_r[m, 3] = v[PY - 1 :]
        for d in range(2):

            @pl.when(has[2 + 1 - d])
            def _():
                rows_copy(m, d).wait_recv()
                grow_r[m, 2 + 1 - d] = grow_r[m, 1 - d]

        below, above = grow_r[m, 2], grow_r[m, 3]
        near_y = jnp.concatenate([below, v[:-1]], 0) + jnp.concatenate([v[1:], above], 0)
        near_z = jnp.where(lane == 0, v, pltpu.roll(v, 1, 1)) + jnp.where(
            lane == PZ - 1, v, pltpu.roll(v, PZ - 1, 1)
        )
        lap = DX * near_x + DY * near_y + DZ * near_z - (2.0 * (DX + DY + DZ)) * v
        return v + DT * (lap - flow)

    def ghost_put(n, plane):
        @pl.when(slow_low)
        def _():
            xh[n, 1] = plane

        @pl.when(slow_high)
        def _():
            xh[n, 0] = plane

    def stretch(plane, v):
        return GAIN * plane * (v - STRETCH_REV)

    def ghost_first_rows():
        @on_slow
        def _():
            ghost_rows(0, ghost_plane(1))

    def ghost_first():
        @on_slow
        def _():
            v = ghost_plane(1)
            flow = ghost_states(0, v)
            over(1).wait_recv()
            ghost_put(2, ghost_fresh(0, v, vb[0, edge] + gplane[0], flow))

    def ghost_second_rows():
        @on_slow
        def _():
            ghost_rows(1, ghost_plane(5))
            over(2).wait_recv()
            ghost_rows(2, gplane[1])

    def ghost_second():
        @on_slow
        def _():
            near, far = ghost_plane(5), gplane[1]
            flow = ghost_states(0, near)
            over(3).wait_recv()
            fresh = ghost_fresh(1, near, vb[4, edge] + far, flow + stretch(gplane[2], near))
            ghost_put(6, fresh)
            ghost_rows(3, fresh)
            flow = ghost_states(1, far)
            over(6).wait_recv()
            over(7).wait_recv()
            gplane[0] = ghost_fresh(2, far, near + gplane[4], flow + stretch(gplane[5], far))

    def ghost_third():
        @on_slow
        def _():
            v = ghost_plane(6)
            flow = ghost_states(0, v) + stretch(gplane[2], v)
            ghost_put(7, ghost_fresh(3, v, vb[5, edge] + gplane[0], flow))

    def ghost_sent():
        @on_slow
        def _():
            for i in range(8):
                over(i).wait_send()
            for m in range(4):
                for d in range(2):
                    pl.when(has[2 + d])(lambda m=m, d=d: rows_copy(m, d).wait_send())

    sent, got = (snd2, snd1), (rcv2, rcv1)

    def send_rows(s):
        def one(t, device):
            pltpu.make_async_remote_copy(
                src_ref=sent[s].at[t],
                dst_ref=got[s].at[me],
                send_sem=a2s.at[s],
                recv_sem=a2r.at[s],
                device_id=device,
                device_id_type=MESH,
            ).start()

        others(one)
        got[s][me] = sent[s][me]

    def wait_rows(s):
        part = got[s].at[pl.ds(0, count - 1)]
        pltpu.make_async_copy(part, part, a2r.at[s]).wait()

    def wait_sent(s):
        part = sent[s].at[pl.ds(0, count - 1)]
        pltpu.make_async_copy(part, part, a2s.at[s]).wait()

    small[8].wait()
    start_halo(0)
    cross(0)
    for copy in small[:8]:
        copy.wait()
    def spread_scalar(x):
        return jnp.full((NROW, LANES), x, F32)

    sums = [jnp.zeros((NROW, LANES), F32) for _ in range(3)]
    for k in range(NK):
        half, slope, keep, cond, rev, weight = [spread_scalar(raw[j, 0, k]) for j in range(6)]
        inv_slope, inv_cond = 0.5 / slope, 1.0 / cond
        entries = (
            inv_slope,
            -half * inv_slope,
            keep,
            0.5 * cond * (1.0 - keep),
            rev,
            keep * cond,
            -0.5 * keep * cond,
            inv_cond,
            weight * inv_cond,
        )
        for j, entry in enumerate(entries):
            par[j, k] = entry
        sums = [sums[0] + 0.5 * cond, sums[1] + 0.5 * cond * rev, sums[2] + 0.5 * weight]
    for j in range(3):
        par[9, j] = sums[j]

    for g in range(GROUPS):
        load_group(g).wait()
        planes(0, g * GP, (g + 1) * GP, opening=True)

    tri = jnp.where((iota((LANES, 256), 0) < iota((LANES, 256), 1)), 1.0, 0.0).astype(BF16)
    carry = jnp.zeros((count, LANES), F32)
    for r in range(NROW):
        hot = jnp.broadcast_to(routes[r : r + 1, :], (count, LANES)) == iota((count, LANES), 0)
        hot_f = jnp.where(hot, 1.0, 0.0)
        hot_b = hot_f.astype(BF16)
        tbuf[:, r * LANES : (r + 1) * LANES] = hot_b
        run = dot(hot_b, tri)
        before = run[:, :LANES] + carry
        carry = carry + run[:, LANES:]
        posb[r : r + 1, :] = jnp.sum(before * hot_f, axis=0, keepdims=True).astype(jnp.int32)

    slot_row = lax.rem(iota((LANES, LANES), 0), MOST)

    def here(r):
        return jnp.broadcast_to(posb[r : r + 1, :], (LANES, LANES)) == slot_row

    def placed():
        return dot(tbuf[...], lhi[...], NT) + dot(tbuf[...], llo[...], NT)

    for r in range(NROW):
        row = jnp.broadcast_to(base[r : r + 1, :], (LANES, LANES))
        h, l = split2(jnp.where(here(r), row, 0.0))
        lhi[:, r * LANES : (r + 1) * LANES] = h
        llo[:, r * LANES : (r + 1) * LANES] = l
    snd2[:, 1, :] = placed()


    met(0)
    meet(1)
    finish_halo(0)
    start_halo(1)
    cross(1)
    planes(1, 0, PX)
    met(1)
    meet(2)

    for copy in small[9:]:
        copy.wait()
    row8, block = iota((NROW, LANES), 0), iota((NROW, LANES), 1) // MOST
    for t in range(count // NROW):
        x = nodes[:, t * LANES : (t + 1) * LANES]
        for bit in (1, 2, 4):
            up = pltpu.roll(pltpu.roll(x, NROW - bit, 0), MOST * bit, 1)
            down = pltpu.roll(pltpu.roll(x, bit, 0), LANES - MOST * bit, 1)
            row_bit, block_bit = (row8 // bit) % 2, (block // bit) % 2
            x = jnp.where(row_bit < block_bit, up, jnp.where(row_bit > block_bit, down, x))
        nlo[t * NROW : (t + 1) * NROW, :] = lax.rem(x, LANES)
        nhi[t * NROW : (t + 1) * NROW, :] = x // LANES

    def hot_chunk(ch, c):
        for j in range(16):
            row = nlo[pl.ds(ch * 16 + j, 1), :]
            hit = jnp.broadcast_to(row, (LANES, LANES)) == iota((LANES, LANES), 0)
            onehot[ch, :, j * LANES : (j + 1) * LANES] = jnp.where(hit, 1.0, 0.0).astype(BF16)
        return c

    lax.fori_loop(0, 8, hot_chunk, 0)
    ghost_opening()
    finish_halo(1)
    ghost_first_rows()
    start_halo(2)
    planes(2, 0, PX)
    met(2)
    meet(3)

    zi, zj = iota((LANES, 256), 0), iota((LANES, 256), 1)
    wz[...] = jnp.where(
        zi // BE == lax.rem(zj, 32), corner_weight(lax.rem(zi, BE), zj // LANES), 0.0
    ).astype(BF16)
    pi, pj = iota((32, 64), 0), iota((32, 64), 1)
    wp = jnp.where(pi // 16 == pj // 32, corner_weight(lax.rem(pi, BE), (pj // 16) % 2), 0.0).astype(BF16)
    ti, tj = iota((64, 32), 0), iota((64, 32), 1)
    wpt = jnp.where(tj // 16 == ti // 32, corner_weight(lax.rem(tj, BE), (ti // 16) % 2), 0.0).astype(BF16)
    band = (iota((256, 256), 0) % 16) // BE == (iota((256, 256), 1) // 32) % BE
    ghost_first()
    finish_halo(2)
    start_halo(3)
    planes(3, 0, PX, tension=True)

    for r in range(NROW):
        a, bh = r // 2, r % 2
        for x in range(2):
            acc = None
            for i in range(BE):
                share = (i + 0.5) / BE
                term = tens[BE * a + i, bh * 16 : (bh + 1) * 16, :] * (
                    (share if x else 1.0 - share) / (BE / 2.0) ** 3
                )
                acc = term if acc is None else acc + term
            txb[r * 32 + x * 16 : r * 32 + (x + 1) * 16, :] = acc
    h, l = split2(txb[...])
    along = jnp.where(band, dot(h, wz[...]) + dot(l, wz[...]), 0.0)
    for r in range(NROW):
        h, l = split2(along[r * 32 : (r + 1) * 32])
        both = dot(wpt, h) + dot(wpt, l)
        full = jnp.concatenate([both[:, :LANES], both[:, LANES:]], axis=0)
        h, l = split2(jnp.where(here(r), full, 0.0))
        lhi[:, r * LANES : (r + 1) * LANES] = h
        llo[:, r * LANES : (r + 1) * LANES] = l
    snd2[:, 0, :] = placed()
    met(3)
    send_rows(0)

    @on_slow
    def _():
        stage[...] = ust[:, pl.ds(second, 1)].reshape(NK, PY, PZ)
        over(4).start()

    planes(3, 0, PX, flow_only=True)
    finish_halo(3)
    start_halo(4)
    cross(5)

    rd = jnp.where(iota((24, 384), 0) == iota((24, 384), 1) // MOST, 1.0, 0.0).astype(BF16)
    rdt = jnp.where(iota((384, 24), 1) == iota((384, 24), 0) // MOST, 1.0, 0.0).astype(BF16)
    rj = jnp.where(iota((LANES, 8), 1) == corner_of(iota((LANES, 8), 0) // MOST), 1.0, 0.0).astype(BF16)
    rjt = jnp.where(iota((8, LANES), 0) == corner_of(iota((8, LANES), 1) // MOST), 1.0, 0.0).astype(BF16)

    def kron(left, part, right, rows, cols, dims=NT):
        full = dot(dot(left, part, dims).astype(BF16), right)
        same = lax.rem(iota((rows, cols), 0), MOST) == lax.rem(iota((rows, cols), 1), MOST)
        return jnp.where(same, full, 0.0).astype(BF16)

    for s, part in enumerate(split2(fmap[...])):
        kf[s] = kron(rj, part, rd, LANES, 384, NN)
    for s, part in enumerate(split2(stiff[...])):
        ks[s] = kron(rdt, part, rd, 384, 384)
    for s, part in enumerate(split2(smap[...])):
        kt[s] = kron(rdt, part, rjt, 384, LANES)
    eye = jnp.where(iota((24, 24), 0) == iota((24, 24), 1), stiff[...], 0.0)
    dh, dl = split2(jnp.broadcast_to(jnp.sum(eye, axis=0, keepdims=True), (8, 24)))
    dvec[...] = dot(dh, rd) + dot(dl, rd)
    mean8 = jnp.where(
        lax.rem(iota((LANES, LANES), 0), MOST) == lax.rem(iota((LANES, LANES), 1), MOST), 0.125, 0.0
    ).astype(BF16)
    pair = jnp.where(
        jnp.broadcast_to(perm[...], (LANES, LANES)) == iota((LANES, LANES), 0), 1.0, 0.0
    ).astype(BF16)
    back = dot(iota((8, LANES), 1).astype(F32).astype(BF16), pair, NT).astype(jnp.int32)


    def spread(comps):
        rows = 2 * comps * NROW
        for c in range(comps):
            h, l = split2(vals[c])
            vsp[0, c] = h.astype(F32)
            vsp[1, c] = l.astype(F32)

        def chunk(ch, acc):
            for j in range(16):
                p = ch * 16 + j
                hit = jnp.broadcast_to(nhi[pl.ds(p, 1), :], (NROW, LANES)) == iota((NROW, LANES), 0)
                column = []
                for s in range(2):
                    for c in range(comps):
                        row = jnp.broadcast_to(vsp[s, c, pl.ds(p, 1), :], (NROW, LANES))
                        column.append(jnp.where(hit, row, 0.0))
                abuf[0:rows, j * LANES : (j + 1) * LANES] = jnp.concatenate(column, axis=0).astype(BF16)
            return acc + dot(abuf[0:rows, :], onehot[ch], NT)

        acc = lax.fori_loop(0, 8, chunk, jnp.zeros((rows, LANES), F32))
        both = acc[: rows // 2] + acc[rows // 2 :]
        for c in range(comps):
            ndb[c] = both[c * NROW : (c + 1) * NROW]

    def shared(s, to):
        peer = me - 1 if to == 0 else me + 1
        return pltpu.make_async_remote_copy(
            src_ref=asm_s.at[s, to],
            dst_ref=asm_r.at[s, to],
            send_sem=ass.at[s, to],
            recv_sem=asr.at[s, to],
            device_id=(peer // n_four, lax.rem(peer, n_four)),
            device_id_type=MESH,
        )

    has_before, has_after = me > 0, me < count - 1

    def assemble(s, comps):
        lead = jnp.concatenate([ndb[c, 0:1, :] for c in range(comps)] + [jnp.zeros((NROW - comps, LANES), F32)], axis=0)
        trail = jnp.concatenate(
            [ndb[c, NROW - 1 :, :] for c in range(comps)] + [jnp.zeros((NROW - comps, LANES), F32)], axis=0
        )
        asm_s[s, 0] = jnp.take_along_axis(lead, back, axis=1)
        asm_s[s, 1] = trail

        @pl.when(has_before)
        def _():
            shared(s, 0).start()

        @pl.when(has_after)
        def _():
            shared(s, 1).start()

        @pl.when(has_after)
        def _():
            shared(s, 0).wait_recv()
            for c in range(comps):
                ndb[c, NROW - 1 :, :] = ndb[c, NROW - 1 :, :] + asm_r[s, 0, c : c + 1, :]

        @pl.when(has_before)
        def _():
            shared(s, 1).wait_recv()
            order = jnp.broadcast_to(perm[...], (NROW, LANES))
            got = jnp.take_along_axis(asm_r[s, 1], order, axis=1)
            for c in range(comps):
                ndb[c, 0:1, :] = ndb[c, 0:1, :] + got[c : c + 1]

        @pl.when(has_before)
        def _():
            shared(s, 0).wait_send()

        @pl.when(has_after)
        def _():
            shared(s, 1).wait_send()

    def collect(table):
        def tiles(g, carry_in):
            for j in range(4):
                rows = pl.ds(g * 32 + j * NROW, NROW)
                low, high = nlo[rows, :], nhi[rows, :]
                masks = [high == hi for hi in range(NROW)]
                for c in range(3):
                    out = jnp.zeros((NROW, LANES), F32)
                    for hi in range(NROW):
                        line = jnp.broadcast_to(ndb[6 + c, hi : hi + 1, :], (NROW, LANES))
                        out = jnp.where(masks[hi], jnp.take_along_axis(line, low, axis=1), out)
                    vals[c, rows, :] = out
            return carry_in

        for c in range(3):
            ndb[6 + c] = table[c]
        lax.fori_loop(0, 4, tiles, 0)
        return jnp.concatenate([vals[0], vals[1], vals[2]], axis=1)

    def times(x, table):
        h, l = split2(x)
        return dot(h, table[0]) + dot(l, table[0]) + dot(h, table[1])

    planes(4, 0, PX)

    wait_rows(0)
    arrived = rcv2[:, 0, :]
    h, l = split2(arrived)
    k8 = rcv2[:, 1, :] * (1.0 + 0.5 * jnp.tanh(dot(h, mean8) + dot(l, mean8)))
    k8b[...] = k8
    force = times(arrived, kf)
    for c in range(3):
        part = slice(c * LANES, (c + 1) * LANES)
        vals[c] = force[:, part]
        vals[3 + c] = k8 * dvec[0:1, part]
    spread(6)
    assemble(0, 6)
    forces = [ndb[c] for c in range(3)]
    diagonal = [SPRING + ndb[3 + c] for c in range(3)]
    guess = [RELAX * f / d for f, d in zip(forces, diagonal)]
    pushed = times(collect(guess), ks)
    for c in range(3):
        vals[c] = k8b[...] * pushed[:, c * LANES : (c + 1) * LANES]
    spread(3)
    assemble(1, 3)
    moved = []
    for c in range(3):
        applied = SPRING * guess[c] + ndb[c]
        moved.append(guess[c] + RELAX * (forces[c] - applied) / diagonal[c])
        for hi in range(NROW):
            disp_out[c : c + 1, hi * LANES : (hi + 1) * LANES] = moved[c][hi : hi + 1]
    strain = times(collect(moved), kt)
    snd1[...] = strain.reshape(count, 1, LANES)
    send_rows(1)
    finish_halo(4)
    ghost_later()
    wait_rows(1)

    h, l = split2(rcv1[...].reshape(count, LANES).T)
    mine = dot(h, tbuf[...]) + dot(l, tbuf[...])
    for r in range(NROW):
        own = jnp.where(here(r), mine[:, r * LANES : (r + 1) * LANES], 0.0)
        h, l = split2(jnp.concatenate([own[:64], own[64:]], axis=1))
        along = jnp.where(band[:32], dot(wp, h) + dot(wp, l), 0.0)
        h, l = split2(along)
        fine = dot(h, wz[...], NT) + dot(l, wz[...], NT)
        a, bh = r // 2, r % 2
        for i in range(BE):
            share = (i + 0.5) / BE
            ex[BE * a + i, bh * 16 : (bh + 1) * 16, :] = (1.0 - share) * fine[:16] + share * fine[16:]

    def add_excess(i, c):
        vb[4, i] = vb[4, i] - (DT * GAIN) * ex[i] * (vb[3, i] - STRETCH_REV)
        return c

    lax.fori_loop(0, PX, add_excess, 0)
    start_halo(5)
    cross(2, 3, 6, 7)
    planes(5, 0, PX, with_excess=True)
    finish_halo(5)
    ghost_second_rows()
    start_halo(6)
    planes(6, 0, PX, with_excess=True)
    ghost_second()
    finish_halo(6)
    start_halo(7)

    planes(7, 0, PX, with_excess=True, closing=True)
    ghost_third()
    for n in range(7):
        finish_sends(n)
    ghost_sent()
    for s in range(2):
        wait_sent(s)
    finish_halo(7)
    finish_sends(7)


def put_out(pot, states, disp, pot_out, states_out, disp_out, sem):
    copies = [
        pltpu.make_async_copy(src, dst, sem.at[i])
        for i, (src, dst) in enumerate(((states, states_out), (pot, pot_out), (disp, disp_out)))
    ]
    for copy in copies:
        copy.start()
    for copy in copies:
        copy.wait()


def in_hbm(x):
    return pltpu.with_memory_space_constraint(x, pltpu.HBM)


def per_device(
    n_wide,
    n_four,
    voltage,
    states,
    half_volt,
    gate_slope,
    retention,
    conduct,
    reversal,
    tension_weights,
    routes,
    base_stiff,
    elem_nodes,
    share_perm,
    stiffness,
    force_map,
    strain_map,
):
    count = n_wide * n_four
    vmem = pl.BlockSpec(memory_space=pltpu.VMEM)
    hbm = pl.BlockSpec(memory_space=pltpu.HBM)
    scratch = [
        pltpu.SMEM((6, 1, NK), F32),
        pltpu.VMEM((10, NK, NROW, LANES), F32),
        pltpu.VMEM((PX, PY, PZ), F32),
        pltpu.VMEM((NROW, LANES), jnp.int32),
        pltpu.VMEM((NROW, LANES), F32),
        pltpu.VMEM((8, count * MOST), jnp.int32),
        pltpu.VMEM((1, LANES), jnp.int32),
        pltpu.VMEM((24, 24), F32),
        pltpu.VMEM((8, 24), F32),
        pltpu.VMEM((8, 24), F32),
        pltpu.VMEM((NK, PX, PY, PZ), F32),
        pltpu.VMEM((7, PX, PY, PZ), F32),
        pltpu.VMEM((8, 2, PY, PZ), F32),
        pltpu.VMEM((8, 2, PX, PZ), F32),
        pltpu.VMEM((8, 2, PX, PZ), F32),
        pltpu.VMEM((PX, PY, PZ), F32),
        pltpu.VMEM((PX, PY, PZ), F32),
        pltpu.VMEM((count, 1024), BF16),
        pltpu.VMEM((NROW, LANES), jnp.int32),
        pltpu.VMEM((LANES, 1024), BF16),
        pltpu.VMEM((LANES, 1024), BF16),
        pltpu.VMEM((8, LANES, 2048), BF16),
        pltpu.VMEM((96, 2048), BF16),
        pltpu.VMEM((2, 6, count, LANES), F32),
        pltpu.VMEM((count, LANES), jnp.int32),
        pltpu.VMEM((count, LANES), jnp.int32),
        pltpu.VMEM((2, LANES, 384), BF16),
        pltpu.VMEM((2, 384, 384), BF16),
        pltpu.VMEM((2, 384, LANES), BF16),
        pltpu.VMEM((8, 384), F32),
        pltpu.VMEM((LANES, 256), BF16),
        pltpu.VMEM((count, LANES), F32),
        pltpu.VMEM((256, LANES), F32),
        pltpu.VMEM((6, count, LANES), F32),
        pltpu.VMEM((9, NROW, LANES), F32),
        pltpu.VMEM((2, 2, NROW, LANES), F32),
        pltpu.VMEM((2, 2, NROW, LANES), F32),
        pltpu.VMEM((count, 2, LANES), F32),
        pltpu.VMEM((count, 2, LANES), F32),
        pltpu.VMEM((count, 1, LANES), F32),
        pltpu.VMEM((count, 1, LANES), F32),
        pltpu.SemaphoreType.DMA((GROUPS,)),
        pltpu.SemaphoreType.DMA((14,)),
        pltpu.SemaphoreType.DMA((8, 4)),
        pltpu.SemaphoreType.DMA((8, 4)),
        pltpu.SemaphoreType.DMA((2,)),
        pltpu.SemaphoreType.DMA((2,)),
        pltpu.SemaphoreType.DMA((2, 2)),
        pltpu.SemaphoreType.DMA((2, 2)),
        pltpu.SemaphoreType.REGULAR((4,)),
        pltpu.VMEM((2, NK, PY, PZ), F32),
        pltpu.VMEM((NK, PY, PZ), F32),
        pltpu.VMEM((6, PY, PZ), F32),
        pltpu.VMEM((4, 2, 1, LANES), F32),
        pltpu.VMEM((4, 4, 1, LANES), F32),
        pltpu.SemaphoreType.DMA((8,)),
        pltpu.SemaphoreType.DMA((8,)),
        pltpu.SemaphoreType.DMA((4, 2)),
        pltpu.SemaphoreType.DMA((4, 2)),
    ]
    made = pl.pallas_call(
        functools.partial(kernel, n_wide, n_four),
        out_shape=(
            jax.ShapeDtypeStruct((PX, PY, PZ), F32),
            jax.ShapeDtypeStruct((NK, PX, PY, PZ), F32),
            jax.ShapeDtypeStruct((3, NROW * LANES), F32),
        ),
        in_specs=[[hbm] * 6] + [hbm] * 9,
        out_specs=(vmem, vmem, vmem),
        scratch_shapes=scratch,
        compiler_params=pltpu.CompilerParams(
            collective_id=0, has_side_effects=True, vmem_limit_bytes=40 << 20
        ),
    )(
        [
            in_hbm(x.reshape(1, NK))
            for x in (half_volt, gate_slope, retention, conduct, reversal, tension_weights)
        ],
        in_hbm(voltage),
        in_hbm(states),
        in_hbm(routes.reshape(NROW, LANES)),
        in_hbm(base_stiff.reshape(NROW, LANES)),
        in_hbm(elem_nodes),
        in_hbm(share_perm),
        in_hbm(stiffness),
        in_hbm(force_map.T),
        in_hbm(strain_map),
    )
    return pl.pallas_call(
        put_out,
        out_shape=[jax.ShapeDtypeStruct(x.shape, x.dtype) for x in made],
        in_specs=[vmem] * 3,
        out_specs=[hbm] * 3,
        scratch_shapes=[pltpu.SemaphoreType.DMA((3,))],
        compiler_params=pltpu.CompilerParams(vmem_limit_bytes=1 << 20),
    )(*made)


def solution(mesh):
    placed = (
        P("wide", "four", None),
        P(None, "wide", "four", None),
        P(),
        P(),
        P(),
        P(),
        P(),
        P(),
        P(("wide", "four"), None),
        P(("wide", "four")),
        P(None, ("wide", "four")),
        P(("wide", "four"), None),
        P(),
        P(),
        P(),
    )
    return jax.shard_map(
        functools.partial(per_device, mesh.shape["wide"], mesh.shape["four"]),
        mesh=mesh,
        in_specs=placed,
        out_specs=(
            P("wide", "four", None),
            P(None, "wide", "four", None),
            P(None, ("wide", "four")),
        ),
        check_vma=False,
    )
```

```python
import functools

import jax
import jax.numpy as jnp
from jax import lax
from jax.experimental import pallas as pl
from jax.experimental.pallas import tpu as pltpu
from jax.sharding import PartitionSpec as P

BE = 4
NK = 20
PX, PY, PZ = 16, 32, 128
NROW = 8
LANES = 128
MOST = 16
F32, BF16 = jnp.float32, jnp.bfloat16
DT = 0.1
DX, DY, DZ = 1.5, 1.0, 0.6
GAIN, STRETCH_REV = 2.0, 0.5
SPRING, RELAX = 1.0, 0.7
GROUPS = 4
TWO = 2
SKIPPED = (1, 2, 6, 7)
BASES = (0, 5)
GP = PX // GROUPS
MESH = pl.DeviceIdType.MESH
NN = (((1,), (0,)), ((), ()))
NT = (((1,), (1,)), ((), ()))


def dot(a, b, dims=NN):
    return lax.dot_general(a, b, dims, preferred_element_type=F32)


def split2(x):
    high = x.astype(BF16)
    return high, (x - high.astype(F32)).astype(BF16)


def iota(shape, dim):
    return lax.broadcasted_iota(jnp.int32, shape, dim)


def corner_of(j):
    return 4 * ((j // 2) % 2) + 2 * (j % 2) + j // 4


def corner_weight(i, side):
    place = (i.astype(F32) + 0.5) * (1.0 / BE)
    return jnp.where(side == 1, place, 1.0 - place)


def kernel(
    n_wide,
    n_four,
    raw_in,
    volt_in,
    states_in,
    routes_in,
    base_in,
    nodes_in,
    perm_in,
    stiff_in,
    fmap_in,
    smap_in,
    pot_out,
    states_out,
    disp_out,
    raw,
    par,
    volt,
    routes,
    base,
    nodes,
    perm,
    stiff,
    fmap,
    smap,
    ust,
    vb,
    xh,
    yh,
    yf,
    ex,
    tens,
    tbuf,
    posb,
    lhi,
    llo,
    onehot,
    abuf,
    vsp,
    nlo,
    nhi,
    kf,
    ks,
    kt,
    dvec,
    wz,
    k8b,
    txb,
    vals,
    ndb,
    asm_s,
    asm_r,
    snd2,
    rcv2,
    snd1,
    rcv1,
    dma_in,
    dma_small,
    hs,
    hr,
    a2s,
    a2r,
    ass,
    asr,
    rounds,
    graw,
    dma_raw,
    mom_s,
    mom_r,
    gpl,
    gex,
    gkeep,
    grow_s,
    grow_r,
    os,
    orv,
    gs,
    gr,
):
    count = n_wide * n_four
    wide = lax.axis_index("wide")
    four = lax.axis_index("four")
    me = wide * n_four + four
    barrier = pltpu.get_barrier_semaphore()

    ring = (wide // 16, (wide // 4) % 4, wide % 4, four)
    extent = (2, 4, 4, 4)

    def place(y, z, x, f):
        return {"wide": y * 16 + z * 4 + x, "four": f}

    def along(axis):
        for step in range(1, extent[axis]):
            spot = list(ring)
            spot[axis] = (spot[axis] + step) % extent[axis]
            yield place(*spot)

    def others(act):
        def some(g, c):
            a, b = g // 4, g % 4
            z = (ring[1] + 2 + 3 * a + 3 * ((a * a - a) // 2)) % 4
            x = (ring[2] + 2 + 3 * b + 3 * ((b * b - b) // 2)) % 4
            for dy in (1, 0):
                w = ((ring[0] + dy) % 2) * 16 + z * 4 + x
                for df in (2, 3, 1, 0):
                    f = (four + df) % 4

                    def go(w=w, f=f):
                        act(w * n_four + f, {"wide": w, "four": f})

                    if dy == 0 and df == 0:
                        pl.when(g < 15)(go)
                    else:
                        go()
            return c

        lax.fori_loop(0, 16, some, 0)

    def greet(device):
        pl.semaphore_signal(barrier, inc=1, device_id=device, device_id_type=MESH)

    for axis in range(4):
        for device in along(axis):
            greet(device)
    at_x_end, at_x_start = wide % 4 == 3, wide % 4 == 0
    extra = (
        (at_x_end & (wide < n_wide - 1), {"wide": wide + 1, "four": four}),
        (at_x_start & (wide > 0), {"wide": wide - 1, "four": four}),
        ((four == n_four - 1) & (wide < n_wide - 1), {"wide": wide + 1, "four": 0 * four}),
        ((four == 0) & (wide > 0), {"wide": wide - 1, "four": 0 * four + n_four - 1}),
    )
    for cond, device in extra:
        pl.when(cond)(functools.partial(greet, device))
    small = [
        pltpu.make_async_copy(src, dst, dma_small.at[i])
        for i, (src, dst) in enumerate(
            [(raw_in[j], raw.at[j]) for j in range(6)]
            + [
                (routes_in, routes),
                (base_in, base),
                (volt_in, volt),
                (nodes_in, nodes),
                (perm_in, perm),
                (stiff_in, stiff),
                (fmap_in, fmap),
                (smap_in, smap),
            ]
        )
    ]
    for copy in small[:9]:
        copy.start()

    def load_group(g):
        part = pl.ds(g * GP, GP)
        return pltpu.make_async_copy(states_in.at[:, part], ust.at[:, part], dma_in.at[g])

    for g in range(GROUPS):
        load_group(g).start()
    for copy in small[9:]:
        copy.start()
    pl.semaphore_wait(barrier, 10 + sum(cond.astype(jnp.int32) for cond, _ in extra))

    def meet(axis):
        for device in along(axis):
            pl.semaphore_signal(rounds.at[axis], inc=1, device_id=device, device_id_type=MESH)

    def met(axis):
        pl.semaphore_wait(rounds.at[axis], extent[axis] - 1)

    meet(0)
    has = (wide > 0, wide < n_wide - 1, four > 0, four < n_four - 1)
    opposite = (1, 0, 3, 2)
    peers = ((wide - 1, four), (wide + 1, four), (wide, four - 1), (wide, four + 1))

    def field(n):
        return volt if n == 0 else vb.at[n - 1]

    def after(n):
        return pot_out if n == 7 else vb.at[n]

    half = n_wide // 2
    slow_low, slow_high = wide == half - 1, wide == half
    slow = slow_low | slow_high
    across = {"wide": jnp.where(slow_low, half, half - 1), "four": four}
    edge = jnp.where(slow_low, PX - 1, 0)
    second = jnp.where(slow_low, PX - 2, 1)
    third = jnp.where(slow_low, PX - 3, 2)
    shut = (slow_high, slow_low, False, False)

    def talks(n, d):
        return has[d] & ~shut[d] if n in SKIPPED and d < 2 else has[d]

    def over(p, i):
        src, dst = (
            (field(BASES[p]).at[second], gpl.at[p, 0]),
            (field(BASES[p]).at[third], gpl.at[p, 1]),
            (mom_s.at[p], mom_r.at[p]),
            (ex.at[edge], gex.at[0]),
            (ex.at[second], gex.at[1]),
        )[i]
        return pltpu.make_async_remote_copy(
            src_ref=src,
            dst_ref=dst,
            send_sem=os.at[p, i],
            recv_sem=orv.at[p, i],
            device_id=across,
            device_id_type=MESH,
        )

    def rows_copy(m, d):
        return pltpu.make_async_remote_copy(
            src_ref=grow_s.at[m, d],
            dst_ref=grow_r.at[m, 1 - d],
            send_sem=gs.at[m, d],
            recv_sem=gr.at[m, d],
            device_id=peers[2 + d],
            device_id_type=MESH,
        )

    def halo(n, d):
        v = field(n)
        src = (v.at[0], v.at[PX - 1], yf.at[n, 0], yf.at[n, 1])[d]
        dst = (xh.at[n, 1], xh.at[n, 0], yh.at[n, 1], yh.at[n, 0])[d]
        return pltpu.make_async_remote_copy(
            src_ref=src,
            dst_ref=dst,
            send_sem=hs.at[n, d],
            recv_sem=hr.at[n, d],
            device_id=peers[d],
            device_id_type=MESH,
        )

    def start_halo(n):
        v = field(n)
        yf[n, 0] = v[:, 0, :]
        yf[n, 1] = v[:, PY - 1, :]
        for d in range(4):

            @pl.when(talks(n, d))
            def _():
                halo(n, d).start()

    def finish_halo(n):
        v, w = field(n), after(n)

        for d in range(4):

            @pl.when(talks(n, opposite[d]))
            def _():
                halo(n, d).wait_recv()

            @pl.when(has[opposite[d]])
            def _():
                if d == 0:
                    w[PX - 1] = w[PX - 1] + (DT * DX) * (xh[n, 1] - v[PX - 1])
                elif d == 1:
                    w[0] = w[0] + (DT * DX) * (xh[n, 0] - v[0])
                elif d == 2:
                    w[:, PY - 1, :] = w[:, PY - 1, :] + (DT * DY) * (yh[n, 1] - v[:, PY - 1, :])
                else:
                    w[:, 0, :] = w[:, 0, :] + (DT * DY) * (yh[n, 0] - v[:, 0, :])

    def finish_sends(n):
        for d in range(4):

            @pl.when(talks(n, d))
            def _():
                halo(n, d).wait_send()

    shape = (TWO, PY // NROW, NROW, LANES)
    lane = iota((PY, PZ), 1)

    def planes(n, first, last, with_excess=False, opening=False, tension=False, flow_only=False, closing=False):
        v_ref, w_ref = field(n), after(n)

        def body(g, c):
            i = g * TWO
            v = v_ref[pl.ds(i, TWO)].reshape(shape)
            total_a = jnp.broadcast_to(par[9, 0], shape)
            total_b = jnp.broadcast_to(par[9, 1], shape)
            total_t = jnp.broadcast_to(par[9, 2], shape)
            for k in range(NK):
                old = ust[k, pl.ds(i, TWO)].reshape(shape)
                if flow_only:
                    total_a = total_a + old
                    total_b = total_b + old * par[4, k]
                    continue
                t = jnp.tanh(v * par[0, k] + par[1, k])
                if opening:
                    u = old * par[5, k] + (t * par[3, k] + par[6, k])
                else:
                    u = old * par[2, k] + t * par[3, k]
                if closing:
                    states_out[k, pl.ds(i, TWO)] = (u * par[7, k] + 0.5).reshape(TWO, PY, PZ)
                else:
                    ust[k, pl.ds(i, TWO)] = u.reshape(TWO, PY, PZ)
                if tension:
                    total_t = total_t + u * par[8, k]
                else:
                    total_a = total_a + u
                    total_b = total_b + u * par[4, k]
            if tension:
                tens[pl.ds(i, TWO)] = total_t.reshape(TWO, PY, PZ)
                return c
            current = (v * total_a - total_b).reshape(TWO, PY, PZ)
            for h in range(TWO):
                j = i + h
                v = v_ref[j]
                flow = current[h]
                if with_excess:
                    flow = flow + GAIN * ex[j] * (v - STRETCH_REV)
                near_x = v_ref[jnp.maximum(j - 1, 0)] + v_ref[jnp.minimum(j + 1, PX - 1)]
                near_y = jnp.concatenate([v[:1], v[:-1]], 0) + jnp.concatenate([v[1:], v[-1:]], 0)
                near_z = jnp.where(lane == 0, v, pltpu.roll(v, 1, 1)) + jnp.where(
                    lane == PZ - 1, v, pltpu.roll(v, PZ - 1, 1)
                )
                lap = DX * near_x + DY * near_y + DZ * near_z - (2.0 * (DX + DY + DZ)) * v
                w_ref[j] = v + DT * (lap - flow)
            return c

        lax.fori_loop(first // TWO, last // TWO, body, 0)

    def ghost_plane(n):
        return jnp.where(slow_low, xh[n, 1], xh[n, 0])

    def gate_sums(plane, later=False):
        v = plane.reshape(shape[1:])
        a0 = jnp.broadcast_to(par[9, 0], shape[1:])
        b0 = jnp.broadcast_to(par[9, 1], shape[1:])
        a1 = b1 = jnp.zeros(shape[1:], F32)
        for k in range(NK):
            t = jnp.tanh(v * par[0, k] + par[1, k]) * par[3, k]
            a0, b0 = a0 + t, b0 + t * par[4, k]
            if later:
                t = t * par[2, k]
                a1, b1 = a1 + t, b1 + t * par[4, k]
        return [x.reshape(PY, PZ) for x in (a0, b0, a1, b1)]

    def moments(p, kept):
        for which, powers in ((0, 2), (1, 1)):
            sums = [jnp.zeros(shape[1:], F32) for _ in range(4)]
            for k in range(NK):
                u = kept(k, which).reshape(shape[1:])
                sums[0], sums[1] = sums[0] + u, sums[1] + u * par[4, k]
                if powers == 2:
                    u = u * par[2, k]
                    sums[2], sums[3] = sums[2] + u, sums[3] + u * par[4, k]
            for j in range(2 * powers):
                mom_s[p, 4 * which + j] = sums[j].reshape(PY, PZ)

    def on_slow(act):
        pl.when(slow)(act)

    def cross(p, *items):
        @on_slow
        def _():
            for i in items:
                over(p, i).start()

    first_two = pltpu.make_async_copy(
        states_in.at[:, pl.ds(jnp.where(slow_low, PX - 2, 0), 2)], graw, dma_raw
    )

    def moments_opening():
        @on_slow
        def _():
            first_two.wait()
            spot = (jnp.where(slow_low, 1, 0), jnp.where(slow_low, 0, 1))

            def kept(k, which):
                x = graw[k, spot[which]].reshape(shape[1:])
                return x * par[5, k] + par[6, k]

            moments(0, kept)
            over(0, 2).start()

    def moments_later():
        @on_slow
        def _():
            moments(1, lambda k, which: ust[k, (edge, second)[which]].reshape(shape[1:]) * par[2, k])
            over(1, 2).start()

    def ghost_rows(m, plane):
        grow_s[m, 0] = plane[0:1]
        grow_s[m, 1] = plane[PY - 1 :]
        for d in range(2):
            pl.when(has[2 + d])(lambda d=d: rows_copy(m, d).start())

    def ghost_fresh(m, v, near_x, flow):
        grow_r[m, 2] = v[0:1]
        grow_r[m, 3] = v[PY - 1 :]
        for d in range(2):

            @pl.when(has[2 + 1 - d])
            def _():
                rows_copy(m, d).wait_recv()
                grow_r[m, 2 + 1 - d] = grow_r[m, 1 - d]

        below, above = grow_r[m, 2], grow_r[m, 3]
        near_y = jnp.concatenate([below, v[:-1]], 0) + jnp.concatenate([v[1:], above], 0)
        near_z = jnp.where(lane == 0, v, pltpu.roll(v, 1, 1)) + jnp.where(
            lane == PZ - 1, v, pltpu.roll(v, PZ - 1, 1)
        )
        lap = DX * near_x + DY * near_y + DZ * near_z - (2.0 * (DX + DY + DZ)) * v
        return v + DT * (lap - flow)

    def ghost_put(n, plane):
        @pl.when(slow_low)
        def _():
            xh[n, 1] = plane

        @pl.when(slow_high)
        def _():
            xh[n, 0] = plane

    def ghost_flow(p, which, v, total_a, total_b):
        flow = v * total_a - total_b
        return flow + GAIN * gex[which] * (v - STRETCH_REV) if p else flow

    def ghost_a_rows(p):
        @on_slow
        def _():
            ghost_rows(3 * p, ghost_plane(BASES[p]))
            over(p, 0).wait_recv()
            ghost_rows(3 * p + 1, gpl[p, 0])

    def ghost_a(p):
        @on_slow
        def _():
            n = BASES[p]
            near, far = ghost_plane(n), gpl[p, 0]
            a0, b0, a1, b1 = gate_sums(near, True)
            over(p, 2).wait_recv()
            if p:
                over(p, 3).wait_recv()
            flow = ghost_flow(p, 0, near, a0 + mom_r[p, 0], b0 + mom_r[p, 1])
            gkeep[0] = a1 + mom_r[p, 2]
            gkeep[1] = b1 + mom_r[p, 3]
            fresh = ghost_fresh(3 * p, near, field(n)[edge] + far, flow)
            ghost_put(n + 1, fresh)
            ghost_rows(3 * p + 2, fresh)
            a0, b0, _, _ = gate_sums(far)
            over(p, 1).wait_recv()
            if p:
                over(p, 4).wait_recv()
            flow = ghost_flow(p, 1, far, a0 + mom_r[p, 4], b0 + mom_r[p, 5])
            gkeep[2] = ghost_fresh(3 * p + 1, far, near + gpl[p, 1], flow)

    def ghost_b(p):
        @on_slow
        def _():
            n = BASES[p] + 1
            v = ghost_plane(n)
            a0, b0, _, _ = gate_sums(v)
            flow = ghost_flow(p, 0, v, a0 + gkeep[0], b0 + gkeep[1])
            ghost_put(n + 1, ghost_fresh(3 * p + 2, v, field(n)[edge] + gkeep[2], flow))

    def ghost_sent():
        @on_slow
        def _():
            for p in range(2):
                for i in range(5 if p else 3):
                    over(p, i).wait_send()
                for m in range(3):
                    for d in range(2):
                        pl.when(has[2 + d])(lambda m=3 * p + m, d=d: rows_copy(m, d).wait_send())

    sent, got = (snd2, snd1), (rcv2, rcv1)

    def send_rows(s):
        def one(t, device):
            pltpu.make_async_remote_copy(
                src_ref=sent[s].at[t],
                dst_ref=got[s].at[me],
                send_sem=a2s.at[s],
                recv_sem=a2r.at[s],
                device_id=device,
                device_id_type=MESH,
            ).start()

        others(one)
        got[s][me] = sent[s][me]

    def wait_rows(s):
        part = got[s].at[pl.ds(0, count - 1)]
        pltpu.make_async_copy(part, part, a2r.at[s]).wait()

    def wait_sent(s):
        part = sent[s].at[pl.ds(0, count - 1)]
        pltpu.make_async_copy(part, part, a2s.at[s]).wait()

    on_slow(lambda: first_two.start())
    small[8].wait()
    start_halo(0)
    cross(0, 0, 1)
    for copy in small[:8]:
        copy.wait()
    def spread_scalar(x):
        return jnp.full((NROW, LANES), x, F32)

    sums = [jnp.zeros((NROW, LANES), F32) for _ in range(3)]
    for k in range(NK):
        half, slope, keep, cond, rev, weight = [spread_scalar(raw[j, 0, k]) for j in range(6)]
        inv_slope, inv_cond = 0.5 / slope, 1.0 / cond
        entries = (
            inv_slope,
            -half * inv_slope,
            keep,
            0.5 * cond * (1.0 - keep),
            rev,
            keep * cond,
            -0.5 * keep * cond,
            inv_cond,
            weight * inv_cond,
        )
        for j, entry in enumerate(entries):
            par[j, k] = entry
        sums = [sums[0] + 0.5 * cond, sums[1] + 0.5 * cond * rev, sums[2] + 0.5 * weight]
    for j in range(3):
        par[9, j] = sums[j]

    moments_opening()
    for g in range(GROUPS):
        load_group(g).wait()
        planes(0, g * GP, (g + 1) * GP, opening=True)

    tri = jnp.where((iota((LANES, 256), 0) < iota((LANES, 256), 1)), 1.0, 0.0).astype(BF16)
    carry = jnp.zeros((count, LANES), F32)
    for r in range(NROW):
        hot = jnp.broadcast_to(routes[r : r + 1, :], (count, LANES)) == iota((count, LANES), 0)
        hot_f = jnp.where(hot, 1.0, 0.0)
        hot_b = hot_f.astype(BF16)
        tbuf[:, r * LANES : (r + 1) * LANES] = hot_b
        run = dot(hot_b, tri)
        before = run[:, :LANES] + carry
        carry = carry + run[:, LANES:]
        posb[r : r + 1, :] = jnp.sum(before * hot_f, axis=0, keepdims=True).astype(jnp.int32)

    slot_row = lax.rem(iota((LANES, LANES), 0), MOST)

    def here(r):
        return jnp.broadcast_to(posb[r : r + 1, :], (LANES, LANES)) == slot_row

    def placed():
        return dot(tbuf[...], lhi[...], NT) + dot(tbuf[...], llo[...], NT)

    for r in range(NROW):
        row = jnp.broadcast_to(base[r : r + 1, :], (LANES, LANES))
        h, l = split2(jnp.where(here(r), row, 0.0))
        lhi[:, r * LANES : (r + 1) * LANES] = h
        llo[:, r * LANES : (r + 1) * LANES] = l
    snd2[:, 1, :] = placed()


    for copy in small[9:]:
        copy.wait()
    row8, block = iota((NROW, LANES), 0), iota((NROW, LANES), 1) // MOST
    for t in range(count // NROW):
        x = nodes[:, t * LANES : (t + 1) * LANES]
        for bit in (1, 2, 4):
            up = pltpu.roll(pltpu.roll(x, NROW - bit, 0), MOST * bit, 1)
            down = pltpu.roll(pltpu.roll(x, bit, 0), LANES - MOST * bit, 1)
            row_bit, block_bit = (row8 // bit) % 2, (block // bit) % 2
            x = jnp.where(row_bit < block_bit, up, jnp.where(row_bit > block_bit, down, x))
        nlo[t * NROW : (t + 1) * NROW, :] = lax.rem(x, LANES)
        nhi[t * NROW : (t + 1) * NROW, :] = x // LANES

    def hot_chunk(ch, c):
        for j in range(16):
            row = nlo[pl.ds(ch * 16 + j, 1), :]
            hit = jnp.broadcast_to(row, (LANES, LANES)) == iota((LANES, LANES), 0)
            onehot[ch, :, j * LANES : (j + 1) * LANES] = jnp.where(hit, 1.0, 0.0).astype(BF16)
        return c

    lax.fori_loop(0, 8, hot_chunk, 0)
    met(0)
    meet(1)
    finish_halo(0)
    ghost_a_rows(0)
    start_halo(1)
    planes(1, 0, PX)
    met(1)
    meet(2)

    ghost_a(0)
    finish_halo(1)
    start_halo(2)
    planes(2, 0, PX)
    met(2)
    meet(3)

    zi, zj = iota((LANES, 256), 0), iota((LANES, 256), 1)
    wz[...] = jnp.where(
        zi // BE == lax.rem(zj, 32), corner_weight(lax.rem(zi, BE), zj // LANES), 0.0
    ).astype(BF16)
    pi, pj = iota((32, 64), 0), iota((32, 64), 1)
    wp = jnp.where(pi // 16 == pj // 32, corner_weight(lax.rem(pi, BE), (pj // 16) % 2), 0.0).astype(BF16)
    ti, tj = iota((64, 32), 0), iota((64, 32), 1)
    wpt = jnp.where(tj // 16 == ti // 32, corner_weight(lax.rem(tj, BE), (ti // 16) % 2), 0.0).astype(BF16)
    band = (iota((256, 256), 0) % 16) // BE == (iota((256, 256), 1) // 32) % BE
    ghost_b(0)
    finish_halo(2)
    start_halo(3)
    planes(3, 0, PX, tension=True)

    for r in range(NROW):
        a, bh = r // 2, r % 2
        for x in range(2):
            acc = None
            for i in range(BE):
                share = (i + 0.5) / BE
                term = tens[BE * a + i, bh * 16 : (bh + 1) * 16, :] * (
                    (share if x else 1.0 - share) / (BE / 2.0) ** 3
                )
                acc = term if acc is None else acc + term
            txb[r * 32 + x * 16 : r * 32 + (x + 1) * 16, :] = acc
    h, l = split2(txb[...])
    along = jnp.where(band, dot(h, wz[...]) + dot(l, wz[...]), 0.0)
    for r in range(NROW):
        h, l = split2(along[r * 32 : (r + 1) * 32])
        both = dot(wpt, h) + dot(wpt, l)
        full = jnp.concatenate([both[:, :LANES], both[:, LANES:]], axis=0)
        h, l = split2(jnp.where(here(r), full, 0.0))
        lhi[:, r * LANES : (r + 1) * LANES] = h
        llo[:, r * LANES : (r + 1) * LANES] = l
    snd2[:, 0, :] = placed()
    met(3)
    send_rows(0)

    planes(3, 0, PX, flow_only=True)
    finish_halo(3)
    start_halo(4)

    rd = jnp.where(iota((24, 384), 0) == iota((24, 384), 1) // MOST, 1.0, 0.0).astype(BF16)
    rdt = jnp.where(iota((384, 24), 1) == iota((384, 24), 0) // MOST, 1.0, 0.0).astype(BF16)
    rj = jnp.where(iota((LANES, 8), 1) == corner_of(iota((LANES, 8), 0) // MOST), 1.0, 0.0).astype(BF16)
    rjt = jnp.where(iota((8, LANES), 0) == corner_of(iota((8, LANES), 1) // MOST), 1.0, 0.0).astype(BF16)

    def kron(left, part, right, rows, cols, dims=NT):
        full = dot(dot(left, part, dims).astype(BF16), right)
        same = lax.rem(iota((rows, cols), 0), MOST) == lax.rem(iota((rows, cols), 1), MOST)
        return jnp.where(same, full, 0.0).astype(BF16)

    for s, part in enumerate(split2(fmap[...])):
        kf[s] = kron(rj, part, rd, LANES, 384, NN)
    for s, part in enumerate(split2(stiff[...])):
        ks[s] = kron(rdt, part, rd, 384, 384)
    for s, part in enumerate(split2(smap[...])):
        kt[s] = kron(rdt, part, rjt, 384, LANES)
    eye = jnp.where(iota((24, 24), 0) == iota((24, 24), 1), stiff[...], 0.0)
    dh, dl = split2(jnp.broadcast_to(jnp.sum(eye, axis=0, keepdims=True), (8, 24)))
    dvec[...] = dot(dh, rd) + dot(dl, rd)
    mean8 = jnp.where(
        lax.rem(iota((LANES, LANES), 0), MOST) == lax.rem(iota((LANES, LANES), 1), MOST), 0.125, 0.0
    ).astype(BF16)
    pair = jnp.where(
        jnp.broadcast_to(perm[...], (LANES, LANES)) == iota((LANES, LANES), 0), 1.0, 0.0
    ).astype(BF16)
    back = dot(iota((8, LANES), 1).astype(F32).astype(BF16), pair, NT).astype(jnp.int32)


    def spread(comps):
        rows = 2 * comps * NROW
        for c in range(comps):
            h, l = split2(vals[c])
            vsp[0, c] = h.astype(F32)
            vsp[1, c] = l.astype(F32)

        def chunk(ch, acc):
            for j in range(16):
                p = ch * 16 + j
                hit = jnp.broadcast_to(nhi[pl.ds(p, 1), :], (NROW, LANES)) == iota((NROW, LANES), 0)
                column = []
                for s in range(2):
                    for c in range(comps):
                        row = jnp.broadcast_to(vsp[s, c, pl.ds(p, 1), :], (NROW, LANES))
                        column.append(jnp.where(hit, row, 0.0))
                abuf[0:rows, j * LANES : (j + 1) * LANES] = jnp.concatenate(column, axis=0).astype(BF16)
            return acc + dot(abuf[0:rows, :], onehot[ch], NT)

        acc = lax.fori_loop(0, 8, chunk, jnp.zeros((rows, LANES), F32))
        both = acc[: rows // 2] + acc[rows // 2 :]
        for c in range(comps):
            ndb[c] = both[c * NROW : (c + 1) * NROW]

    def shared(s, to):
        peer = me - 1 if to == 0 else me + 1
        return pltpu.make_async_remote_copy(
            src_ref=asm_s.at[s, to],
            dst_ref=asm_r.at[s, to],
            send_sem=ass.at[s, to],
            recv_sem=asr.at[s, to],
            device_id=(peer // n_four, lax.rem(peer, n_four)),
            device_id_type=MESH,
        )

    has_before, has_after = me > 0, me < count - 1

    def assemble(s, comps):
        lead = jnp.concatenate([ndb[c, 0:1, :] for c in range(comps)] + [jnp.zeros((NROW - comps, LANES), F32)], axis=0)
        trail = jnp.concatenate(
            [ndb[c, NROW - 1 :, :] for c in range(comps)] + [jnp.zeros((NROW - comps, LANES), F32)], axis=0
        )
        asm_s[s, 0] = jnp.take_along_axis(lead, back, axis=1)
        asm_s[s, 1] = trail

        @pl.when(has_before)
        def _():
            shared(s, 0).start()

        @pl.when(has_after)
        def _():
            shared(s, 1).start()

        @pl.when(has_after)
        def _():
            shared(s, 0).wait_recv()
            for c in range(comps):
                ndb[c, NROW - 1 :, :] = ndb[c, NROW - 1 :, :] + asm_r[s, 0, c : c + 1, :]

        @pl.when(has_before)
        def _():
            shared(s, 1).wait_recv()
            order = jnp.broadcast_to(perm[...], (NROW, LANES))
            got = jnp.take_along_axis(asm_r[s, 1], order, axis=1)
            for c in range(comps):
                ndb[c, 0:1, :] = ndb[c, 0:1, :] + got[c : c + 1]

        @pl.when(has_before)
        def _():
            shared(s, 0).wait_send()

        @pl.when(has_after)
        def _():
            shared(s, 1).wait_send()

    def collect(table):
        def tiles(g, carry_in):
            for j in range(4):
                rows = pl.ds(g * 32 + j * NROW, NROW)
                low, high = nlo[rows, :], nhi[rows, :]
                masks = [high == hi for hi in range(NROW)]
                for c in range(3):
                    out = jnp.zeros((NROW, LANES), F32)
                    for hi in range(NROW):
                        line = jnp.broadcast_to(ndb[6 + c, hi : hi + 1, :], (NROW, LANES))
                        out = jnp.where(masks[hi], jnp.take_along_axis(line, low, axis=1), out)
                    vals[c, rows, :] = out
            return carry_in

        for c in range(3):
            ndb[6 + c] = table[c]
        lax.fori_loop(0, 4, tiles, 0)
        return jnp.concatenate([vals[0], vals[1], vals[2]], axis=1)

    def times(x, table):
        h, l = split2(x)
        return dot(h, table[0]) + dot(l, table[0]) + dot(h, table[1])

    planes(4, 0, PX)

    wait_rows(0)
    arrived = rcv2[:, 0, :]
    h, l = split2(arrived)
    k8 = rcv2[:, 1, :] * (1.0 + 0.5 * jnp.tanh(dot(h, mean8) + dot(l, mean8)))
    k8b[...] = k8
    force = times(arrived, kf)
    for c in range(3):
        part = slice(c * LANES, (c + 1) * LANES)
        vals[c] = force[:, part]
        vals[3 + c] = k8 * dvec[0:1, part]
    spread(6)
    assemble(0, 6)
    forces = [ndb[c] for c in range(3)]
    diagonal = [SPRING + ndb[3 + c] for c in range(3)]
    guess = [RELAX * f / d for f, d in zip(forces, diagonal)]
    pushed = times(collect(guess), ks)
    for c in range(3):
        vals[c] = k8b[...] * pushed[:, c * LANES : (c + 1) * LANES]
    spread(3)
    assemble(1, 3)
    moved = []
    for c in range(3):
        applied = SPRING * guess[c] + ndb[c]
        moved.append(guess[c] + RELAX * (forces[c] - applied) / diagonal[c])
        for hi in range(NROW):
            disp_out[c : c + 1, hi * LANES : (hi + 1) * LANES] = moved[c][hi : hi + 1]
    strain = times(collect(moved), kt)
    snd1[...] = strain.reshape(count, 1, LANES)
    send_rows(1)
    moments_later()
    finish_halo(4)
    wait_rows(1)

    h, l = split2(rcv1[...].reshape(count, LANES).T)
    mine = dot(h, tbuf[...]) + dot(l, tbuf[...])
    for r in range(NROW):
        own = jnp.where(here(r), mine[:, r * LANES : (r + 1) * LANES], 0.0)
        h, l = split2(jnp.concatenate([own[:64], own[64:]], axis=1))
        along = jnp.where(band[:32], dot(wp, h) + dot(wp, l), 0.0)
        h, l = split2(along)
        fine = dot(h, wz[...], NT) + dot(l, wz[...], NT)
        a, bh = r // 2, r % 2
        for i in range(BE):
            share = (i + 0.5) / BE
            ex[BE * a + i, bh * 16 : (bh + 1) * 16, :] = (1.0 - share) * fine[:16] + share * fine[16:]

    def add_excess(i, c):
        vb[4, i] = vb[4, i] - (DT * GAIN) * ex[i] * (vb[3, i] - STRETCH_REV)
        return c

    lax.fori_loop(0, PX, add_excess, 0)
    start_halo(5)
    cross(1, 0, 3, 1, 4)
    planes(5, 0, PX, with_excess=True)
    finish_halo(5)
    ghost_a_rows(1)
    start_halo(6)
    planes(6, 0, PX, with_excess=True)
    ghost_a(1)
    finish_halo(6)
    start_halo(7)

    planes(7, 0, PX, with_excess=True, closing=True)
    ghost_b(1)
    for n in range(7):
        finish_sends(n)
    ghost_sent()
    for s in range(2):
        wait_sent(s)
    finish_halo(7)
    finish_sends(7)


def put_out(pot, states, disp, pot_out, states_out, disp_out, sem):
    copies = [
        pltpu.make_async_copy(src, dst, sem.at[i])
        for i, (src, dst) in enumerate(((states, states_out), (pot, pot_out), (disp, disp_out)))
    ]
    for copy in copies:
        copy.start()
    for copy in copies:
        copy.wait()


def in_hbm(x):
    return pltpu.with_memory_space_constraint(x, pltpu.HBM)


def per_device(
    n_wide,
    n_four,
    voltage,
    states,
    half_volt,
    gate_slope,
    retention,
    conduct,
    reversal,
    tension_weights,
    routes,
    base_stiff,
    elem_nodes,
    share_perm,
    stiffness,
    force_map,
    strain_map,
):
    count = n_wide * n_four
    vmem = pl.BlockSpec(memory_space=pltpu.VMEM)
    hbm = pl.BlockSpec(memory_space=pltpu.HBM)
    scratch = [
        pltpu.SMEM((6, 1, NK), F32),
        pltpu.VMEM((10, NK, NROW, LANES), F32),
        pltpu.VMEM((PX, PY, PZ), F32),
        pltpu.VMEM((NROW, LANES), jnp.int32),
        pltpu.VMEM((NROW, LANES), F32),
        pltpu.VMEM((8, count * MOST), jnp.int32),
        pltpu.VMEM((1, LANES), jnp.int32),
        pltpu.VMEM((24, 24), F32),
        pltpu.VMEM((8, 24), F32),
        pltpu.VMEM((8, 24), F32),
        pltpu.VMEM((NK, PX, PY, PZ), F32),
        pltpu.VMEM((7, PX, PY, PZ), F32),
        pltpu.VMEM((8, 2, PY, PZ), F32),
        pltpu.VMEM((8, 2, PX, PZ), F32),
        pltpu.VMEM((8, 2, PX, PZ), F32),
        pltpu.VMEM((PX, PY, PZ), F32),
        pltpu.VMEM((PX, PY, PZ), F32),
        pltpu.VMEM((count, 1024), BF16),
        pltpu.VMEM((NROW, LANES), jnp.int32),
        pltpu.VMEM((LANES, 1024), BF16),
        pltpu.VMEM((LANES, 1024), BF16),
        pltpu.VMEM((8, LANES, 2048), BF16),
        pltpu.VMEM((96, 2048), BF16),
        pltpu.VMEM((2, 6, count, LANES), F32),
        pltpu.VMEM((count, LANES), jnp.int32),
        pltpu.VMEM((count, LANES), jnp.int32),
        pltpu.VMEM((2, LANES, 384), BF16),
        pltpu.VMEM((2, 384, 384), BF16),
        pltpu.VMEM((2, 384, LANES), BF16),
        pltpu.VMEM((8, 384), F32),
        pltpu.VMEM((LANES, 256), BF16),
        pltpu.VMEM((count, LANES), F32),
        pltpu.VMEM((256, LANES), F32),
        pltpu.VMEM((6, count, LANES), F32),
        pltpu.VMEM((9, NROW, LANES), F32),
        pltpu.VMEM((2, 2, NROW, LANES), F32),
        pltpu.VMEM((2, 2, NROW, LANES), F32),
        pltpu.VMEM((count, 2, LANES), F32),
        pltpu.VMEM((count, 2, LANES), F32),
        pltpu.VMEM((count, 1, LANES), F32),
        pltpu.VMEM((count, 1, LANES), F32),
        pltpu.SemaphoreType.DMA((GROUPS,)),
        pltpu.SemaphoreType.DMA((14,)),
        pltpu.SemaphoreType.DMA((8, 4)),
        pltpu.SemaphoreType.DMA((8, 4)),
        pltpu.SemaphoreType.DMA((2,)),
        pltpu.SemaphoreType.DMA((2,)),
        pltpu.SemaphoreType.DMA((2, 2)),
        pltpu.SemaphoreType.DMA((2, 2)),
        pltpu.SemaphoreType.REGULAR((4,)),
        pltpu.VMEM((NK, 2, PY, PZ), F32),
        pltpu.SemaphoreType.DMA(()),
        pltpu.VMEM((2, 6, PY, PZ), F32),
        pltpu.VMEM((2, 6, PY, PZ), F32),
        pltpu.VMEM((2, 2, PY, PZ), F32),
        pltpu.VMEM((2, PY, PZ), F32),
        pltpu.VMEM((3, PY, PZ), F32),
        pltpu.VMEM((6, 2, 1, LANES), F32),
        pltpu.VMEM((6, 4, 1, LANES), F32),
        pltpu.SemaphoreType.DMA((2, 5)),
        pltpu.SemaphoreType.DMA((2, 5)),
        pltpu.SemaphoreType.DMA((6, 2)),
        pltpu.SemaphoreType.DMA((6, 2)),
    ]
    made = pl.pallas_call(
        functools.partial(kernel, n_wide, n_four),
        out_shape=(
            jax.ShapeDtypeStruct((PX, PY, PZ), F32),
            jax.ShapeDtypeStruct((NK, PX, PY, PZ), F32),
            jax.ShapeDtypeStruct((3, NROW * LANES), F32),
        ),
        in_specs=[[hbm] * 6] + [hbm] * 9,
        out_specs=(vmem, vmem, vmem),
        scratch_shapes=scratch,
        compiler_params=pltpu.CompilerParams(
            collective_id=0, has_side_effects=True, vmem_limit_bytes=40 << 20
        ),
    )(
        [
            in_hbm(x.reshape(1, NK))
            for x in (half_volt, gate_slope, retention, conduct, reversal, tension_weights)
        ],
        in_hbm(voltage),
        in_hbm(states),
        in_hbm(routes.reshape(NROW, LANES)),
        in_hbm(base_stiff.reshape(NROW, LANES)),
        in_hbm(elem_nodes),
        in_hbm(share_perm),
        in_hbm(stiffness),
        in_hbm(force_map.T),
        in_hbm(strain_map),
    )
    return pl.pallas_call(
        put_out,
        out_shape=[jax.ShapeDtypeStruct(x.shape, x.dtype) for x in made],
        in_specs=[vmem] * 3,
        out_specs=[hbm] * 3,
        scratch_shapes=[pltpu.SemaphoreType.DMA((3,))],
        compiler_params=pltpu.CompilerParams(vmem_limit_bytes=1 << 20),
    )(*made)


def solution(mesh):
    placed = (
        P("wide", "four", None),
        P(None, "wide", "four", None),
        P(),
        P(),
        P(),
        P(),
        P(),
        P(),
        P(("wide", "four"), None),
        P(("wide", "four")),
        P(None, ("wide", "four")),
        P(("wide", "four"), None),
        P(),
        P(),
        P(),
    )
    return jax.shard_map(
        functools.partial(per_device, mesh.shape["wide"], mesh.shape["four"]),
        mesh=mesh,
        in_specs=placed,
        out_specs=(
            P("wide", "four", None),
            P(None, "wide", "four", None),
            P(None, ("wide", "four")),
        ),
        check_vma=False,
    )
```

```python
import functools

import jax
import jax.numpy as jnp
from jax import lax
from jax.experimental import pallas as pl
from jax.experimental.pallas import tpu as pltpu
from jax.sharding import PartitionSpec as P

BE = 4
NK = 20
PX, PY, PZ = 16, 32, 128
NROW = 8
LANES = 128
MOST = 16
F32, BF16 = jnp.float32, jnp.bfloat16
DT = 0.1
DX, DY, DZ = 1.5, 1.0, 0.6
GAIN, STRETCH_REV = 2.0, 0.5
SPRING, RELAX = 1.0, 0.7
GROUPS = 4
TWO = 2
SKIPPED = (1, 2, 6, 7)
BASES = (0, 5)
GP = PX // GROUPS
MESH = pl.DeviceIdType.MESH
NN = (((1,), (0,)), ((), ()))
NT = (((1,), (1,)), ((), ()))


def dot(a, b, dims=NN):
    return lax.dot_general(a, b, dims, preferred_element_type=F32)


def split2(x):
    high = x.astype(BF16)
    return high, (x - high.astype(F32)).astype(BF16)


def iota(shape, dim):
    return lax.broadcasted_iota(jnp.int32, shape, dim)


def corner_of(j):
    return 4 * ((j // 2) % 2) + 2 * (j % 2) + j // 4


def corner_weight(i, side):
    place = (i.astype(F32) + 0.5) * (1.0 / BE)
    return jnp.where(side == 1, place, 1.0 - place)


def kernel(
    n_wide,
    n_four,
    raw_in,
    volt_in,
    states_in,
    routes_in,
    base_in,
    nodes_in,
    perm_in,
    stiff_in,
    fmap_in,
    smap_in,
    pot_out,
    states_out,
    disp_out,
    raw,
    par,
    volt,
    routes,
    base,
    nodes,
    perm,
    stiff,
    fmap,
    smap,
    ust,
    vb,
    xh,
    yh,
    yf,
    ex,
    tens,
    tbuf,
    posb,
    lhi,
    llo,
    onehot,
    abuf,
    vsp,
    nlo,
    nhi,
    kf,
    ks,
    kt,
    dvec,
    wz,
    k8b,
    txb,
    vals,
    ndb,
    asm_s,
    asm_r,
    snd2,
    rcv2,
    snd1,
    rcv1,
    dma_in,
    dma_small,
    hs,
    hr,
    a2s,
    a2r,
    ass,
    asr,
    rounds,
    graw,
    dma_raw,
    mom_s,
    mom_r,
    gpl,
    gex,
    gkeep,
    grow_s,
    grow_r,
    os,
    orv,
    gs,
    gr,
):
    count = n_wide * n_four
    wide = lax.axis_index("wide")
    four = lax.axis_index("four")
    me = wide * n_four + four
    barrier = pltpu.get_barrier_semaphore()

    ring = (wide // 16, (wide // 4) % 4, wide % 4, four)
    extent = (2, 4, 4, 4)

    def place(y, z, x, f):
        return {"wide": y * 16 + z * 4 + x, "four": f}

    def along(axis):
        for step in range(1, extent[axis]):
            spot = list(ring)
            spot[axis] = (spot[axis] + step) % extent[axis]
            yield place(*spot)

    def others(act):
        def some(g, c):
            a, b = g // 4, g % 4
            z = (ring[1] + 2 + 3 * a + 3 * ((a * a - a) // 2)) % 4
            x = (ring[2] + 2 + 3 * b + 3 * ((b * b - b) // 2)) % 4
            for dy in (1, 0):
                w = ((ring[0] + dy) % 2) * 16 + z * 4 + x
                for df in (2, 3, 1, 0):
                    f = (four + df) % 4

                    def go(w=w, f=f):
                        act(w * n_four + f, {"wide": w, "four": f})

                    if dy == 0 and df == 0:
                        pl.when(g < 15)(go)
                    else:
                        go()
            return c

        lax.fori_loop(0, 16, some, 0)

    def greet(device):
        pl.semaphore_signal(barrier, inc=1, device_id=device, device_id_type=MESH)

    for axis in range(4):
        for device in along(axis):
            greet(device)
    at_x_end, at_x_start = wide % 4 == 3, wide % 4 == 0
    extra = (
        (at_x_end & (wide < n_wide - 1), {"wide": wide + 1, "four": four}),
        (at_x_start & (wide > 0), {"wide": wide - 1, "four": four}),
        ((four == n_four - 1) & (wide < n_wide - 1), {"wide": wide + 1, "four": 0 * four}),
        ((four == 0) & (wide > 0), {"wide": wide - 1, "four": 0 * four + n_four - 1}),
    )
    for cond, device in extra:
        pl.when(cond)(functools.partial(greet, device))
    small = [
        pltpu.make_async_copy(src, dst, dma_small.at[i])
        for i, (src, dst) in enumerate(
            [(raw_in[j], raw.at[j]) for j in range(6)]
            + [
                (routes_in, routes),
                (base_in, base),
                (volt_in, volt),
                (nodes_in, nodes),
                (perm_in, perm),
                (stiff_in, stiff),
                (fmap_in, fmap),
                (smap_in, smap),
            ]
        )
    ]
    for copy in small[:9]:
        copy.start()

    def load_group(g):
        part = pl.ds(g * GP, GP)
        return pltpu.make_async_copy(states_in.at[:, part], ust.at[:, part], dma_in.at[g])

    for g in range(GROUPS):
        load_group(g).start()
    for copy in small[9:]:
        copy.start()
    pl.semaphore_wait(barrier, 10 + sum(cond.astype(jnp.int32) for cond, _ in extra))

    def meet(axis):
        for device in along(axis):
            pl.semaphore_signal(rounds.at[axis], inc=1, device_id=device, device_id_type=MESH)

    def met(axis):
        pl.semaphore_wait(rounds.at[axis], extent[axis] - 1)

    meet(0)
    has = (wide > 0, wide < n_wide - 1, four > 0, four < n_four - 1)
    opposite = (1, 0, 3, 2)
    peers = ((wide - 1, four), (wide + 1, four), (wide, four - 1), (wide, four + 1))

    def field(n):
        return volt if n == 0 else vb.at[n - 1]

    def after(n):
        return pot_out if n == 7 else vb.at[n]

    half = n_wide // 2
    slow_low, slow_high = wide == half - 1, wide == half
    slow = slow_low | slow_high
    across = {"wide": jnp.where(slow_low, half, half - 1), "four": four}
    edge = jnp.where(slow_low, PX - 1, 0)
    second = jnp.where(slow_low, PX - 2, 1)
    third = jnp.where(slow_low, PX - 3, 2)
    shut = (slow_high, slow_low, False, False)

    def talks(n, d):
        return has[d] & ~shut[d] if n in SKIPPED and d < 2 else has[d]

    def over(p, i):
        src, dst = (
            (field(BASES[p]).at[second], gpl.at[p, 0]),
            (field(BASES[p]).at[third], gpl.at[p, 1]),
            (mom_s.at[p], mom_r.at[p]),
            (ex.at[edge], gex.at[0]),
            (ex.at[second], gex.at[1]),
        )[i]
        return pltpu.make_async_remote_copy(
            src_ref=src,
            dst_ref=dst,
            send_sem=os.at[p, i],
            recv_sem=orv.at[p, i],
            device_id=across,
            device_id_type=MESH,
        )

    def rows_copy(m, d):
        return pltpu.make_async_remote_copy(
            src_ref=grow_s.at[m, d],
            dst_ref=grow_r.at[m, 1 - d],
            send_sem=gs.at[m, d],
            recv_sem=gr.at[m, d],
            device_id=peers[2 + d],
            device_id_type=MESH,
        )

    def halo(n, d):
        v = field(n)
        src = (v.at[0], v.at[PX - 1], yf.at[n, 0], yf.at[n, 1])[d]
        dst = (xh.at[n, 1], xh.at[n, 0], yh.at[n, 1], yh.at[n, 0])[d]
        return pltpu.make_async_remote_copy(
            src_ref=src,
            dst_ref=dst,
            send_sem=hs.at[n, d],
            recv_sem=hr.at[n, d],
            device_id=peers[d],
            device_id_type=MESH,
        )

    def start_halo(n):
        v = field(n)
        yf[n, 0] = v[:, 0, :]
        yf[n, 1] = v[:, PY - 1, :]
        for d in range(4):

            @pl.when(talks(n, d))
            def _():
                halo(n, d).start()

    def finish_halo(n):
        v, w = field(n), after(n)

        for d in range(4):

            @pl.when(talks(n, opposite[d]))
            def _():
                halo(n, d).wait_recv()

            @pl.when(has[opposite[d]])
            def _():
                if d == 0:
                    w[PX - 1] = w[PX - 1] + (DT * DX) * (xh[n, 1] - v[PX - 1])
                elif d == 1:
                    w[0] = w[0] + (DT * DX) * (xh[n, 0] - v[0])
                elif d == 2:
                    w[:, PY - 1, :] = w[:, PY - 1, :] + (DT * DY) * (yh[n, 1] - v[:, PY - 1, :])
                else:
                    w[:, 0, :] = w[:, 0, :] + (DT * DY) * (yh[n, 0] - v[:, 0, :])

    def finish_sends(n):
        for d in range(4):

            @pl.when(talks(n, d))
            def _():
                halo(n, d).wait_send()

    shape = (TWO, PY // NROW, NROW, LANES)
    lane = iota((PY, PZ), 1)

    def planes(n, first, last, with_excess=False, opening=False, carry=False, tension=False, closing=False):
        v_ref, w_ref = field(n), after(n)

        def body(g, c):
            i = g * TWO
            v = v_ref[pl.ds(i, TWO)].reshape(shape)
            total_a = jnp.broadcast_to(par[9, 0], shape)
            total_b = jnp.broadcast_to(par[9, 1], shape)
            if tension:
                total_t = tens[pl.ds(i, TWO)].reshape(shape)
            else:
                total_t = jnp.broadcast_to(par[9, 2], shape)
            for k in range(NK):
                t = jnp.tanh(v * par[0, k] + par[1, k])
                if tension:
                    total_t = total_t + t * par[11, k]
                    continue
                old = ust[k, pl.ds(i, TWO)].reshape(shape)
                if opening:
                    u = old * par[5, k] + (t * par[3, k] + par[6, k])
                else:
                    u = old * par[2, k] + t * par[3, k]
                if closing:
                    states_out[k, pl.ds(i, TWO)] = (u * par[7, k] + 0.5).reshape(TWO, PY, PZ)
                else:
                    ust[k, pl.ds(i, TWO)] = u.reshape(TWO, PY, PZ)
                total_a = total_a + u
                total_b = total_b + u * par[4, k]
                if carry:
                    total_t = total_t + u * par[10, k]
            if carry or tension:
                tens[pl.ds(i, TWO)] = total_t.reshape(TWO, PY, PZ)
            if tension:
                return c
            current = (v * total_a - total_b).reshape(TWO, PY, PZ)
            for h in range(TWO):
                j = i + h
                v = v_ref[j]
                flow = current[h]
                if with_excess:
                    flow = flow + GAIN * ex[j] * (v - STRETCH_REV)
                near_x = v_ref[jnp.maximum(j - 1, 0)] + v_ref[jnp.minimum(j + 1, PX - 1)]
                near_y = jnp.concatenate([v[:1], v[:-1]], 0) + jnp.concatenate([v[1:], v[-1:]], 0)
                near_z = jnp.where(lane == 0, v, pltpu.roll(v, 1, 1)) + jnp.where(
                    lane == PZ - 1, v, pltpu.roll(v, PZ - 1, 1)
                )
                lap = DX * near_x + DY * near_y + DZ * near_z - (2.0 * (DX + DY + DZ)) * v
                w_ref[j] = v + DT * (lap - flow)
            return c

        lax.fori_loop(first // TWO, last // TWO, body, 0)

    def ghost_plane(n):
        return jnp.where(slow_low, xh[n, 1], xh[n, 0])

    def gate_sums(plane, later=False):
        v = plane.reshape(shape[1:])
        a0 = jnp.broadcast_to(par[9, 0], shape[1:])
        b0 = jnp.broadcast_to(par[9, 1], shape[1:])
        a1 = b1 = jnp.zeros(shape[1:], F32)
        for k in range(NK):
            t = jnp.tanh(v * par[0, k] + par[1, k]) * par[3, k]
            a0, b0 = a0 + t, b0 + t * par[4, k]
            if later:
                t = t * par[2, k]
                a1, b1 = a1 + t, b1 + t * par[4, k]
        return [x.reshape(PY, PZ) for x in (a0, b0, a1, b1)]

    def moments(p, kept):
        for which, powers in ((0, 2), (1, 1)):
            sums = [jnp.zeros(shape[1:], F32) for _ in range(4)]
            for k in range(NK):
                u = kept(k, which).reshape(shape[1:])
                sums[0], sums[1] = sums[0] + u, sums[1] + u * par[4, k]
                if powers == 2:
                    u = u * par[2, k]
                    sums[2], sums[3] = sums[2] + u, sums[3] + u * par[4, k]
            for j in range(2 * powers):
                mom_s[p, 4 * which + j] = sums[j].reshape(PY, PZ)

    def on_slow(act):
        pl.when(slow)(act)

    def cross(p, *items):
        @on_slow
        def _():
            for i in items:
                over(p, i).start()

    first_two = pltpu.make_async_copy(
        states_in.at[:, pl.ds(jnp.where(slow_low, PX - 2, 0), 2)], graw, dma_raw
    )

    def moments_opening():
        @on_slow
        def _():
            first_two.wait()
            spot = (jnp.where(slow_low, 1, 0), jnp.where(slow_low, 0, 1))

            def kept(k, which):
                x = graw[k, spot[which]].reshape(shape[1:])
                return x * par[5, k] + par[6, k]

            moments(0, kept)
            over(0, 2).start()

    def moments_later():
        @on_slow
        def _():
            moments(1, lambda k, which: ust[k, (edge, second)[which]].reshape(shape[1:]) * par[2, k])
            over(1, 2).start()

    def ghost_rows(m, plane):
        grow_s[m, 0] = plane[0:1]
        grow_s[m, 1] = plane[PY - 1 :]
        for d in range(2):
            pl.when(has[2 + d])(lambda d=d: rows_copy(m, d).start())

    def ghost_fresh(m, v, near_x, flow):
        grow_r[m, 2] = v[0:1]
        grow_r[m, 3] = v[PY - 1 :]
        for d in range(2):

            @pl.when(has[2 + 1 - d])
            def _():
                rows_copy(m, d).wait_recv()
                grow_r[m, 2 + 1 - d] = grow_r[m, 1 - d]

        below, above = grow_r[m, 2], grow_r[m, 3]
        near_y = jnp.concatenate([below, v[:-1]], 0) + jnp.concatenate([v[1:], above], 0)
        near_z = jnp.where(lane == 0, v, pltpu.roll(v, 1, 1)) + jnp.where(
            lane == PZ - 1, v, pltpu.roll(v, PZ - 1, 1)
        )
        lap = DX * near_x + DY * near_y + DZ * near_z - (2.0 * (DX + DY + DZ)) * v
        return v + DT * (lap - flow)

    def ghost_put(n, plane):
        @pl.when(slow_low)
        def _():
            xh[n, 1] = plane

        @pl.when(slow_high)
        def _():
            xh[n, 0] = plane

    def ghost_flow(p, which, v, total_a, total_b):
        flow = v * total_a - total_b
        return flow + GAIN * gex[which] * (v - STRETCH_REV) if p else flow

    def ghost_a_rows(p):
        @on_slow
        def _():
            ghost_rows(3 * p, ghost_plane(BASES[p]))
            over(p, 0).wait_recv()
            ghost_rows(3 * p + 1, gpl[p, 0])

    def ghost_a(p):
        @on_slow
        def _():
            n = BASES[p]
            near, far = ghost_plane(n), gpl[p, 0]
            a0, b0, a1, b1 = gate_sums(near, True)
            over(p, 2).wait_recv()
            if p:
                over(p, 3).wait_recv()
            flow = ghost_flow(p, 0, near, a0 + mom_r[p, 0], b0 + mom_r[p, 1])
            gkeep[0] = a1 + mom_r[p, 2]
            gkeep[1] = b1 + mom_r[p, 3]
            fresh = ghost_fresh(3 * p, near, field(n)[edge] + far, flow)
            ghost_put(n + 1, fresh)
            ghost_rows(3 * p + 2, fresh)
            a0, b0, _, _ = gate_sums(far)
            over(p, 1).wait_recv()
            if p:
                over(p, 4).wait_recv()
            flow = ghost_flow(p, 1, far, a0 + mom_r[p, 4], b0 + mom_r[p, 5])
            gkeep[2] = ghost_fresh(3 * p + 1, far, near + gpl[p, 1], flow)

    def ghost_b(p):
        @on_slow
        def _():
            n = BASES[p] + 1
            v = ghost_plane(n)
            a0, b0, _, _ = gate_sums(v)
            flow = ghost_flow(p, 0, v, a0 + gkeep[0], b0 + gkeep[1])
            ghost_put(n + 1, ghost_fresh(3 * p + 2, v, field(n)[edge] + gkeep[2], flow))

    def ghost_sent():
        @on_slow
        def _():
            for p in range(2):
                for i in range(5 if p else 3):
                    over(p, i).wait_send()
                for m in range(3):
                    for d in range(2):
                        pl.when(has[2 + d])(lambda m=3 * p + m, d=d: rows_copy(m, d).wait_send())

    sent, got = (snd2, snd1), (rcv2, rcv1)

    def send_rows(s):
        def one(t, device):
            pltpu.make_async_remote_copy(
                src_ref=sent[s].at[t],
                dst_ref=got[s].at[me],
                send_sem=a2s.at[s],
                recv_sem=a2r.at[s],
                device_id=device,
                device_id_type=MESH,
            ).start()

        others(one)
        got[s][me] = sent[s][me]

    def wait_rows(s):
        part = got[s].at[pl.ds(0, count - 1)]
        pltpu.make_async_copy(part, part, a2r.at[s]).wait()

    def wait_sent(s):
        part = sent[s].at[pl.ds(0, count - 1)]
        pltpu.make_async_copy(part, part, a2s.at[s]).wait()

    on_slow(lambda: first_two.start())
    small[8].wait()
    start_halo(0)
    cross(0, 0, 1)
    for copy in small[:8]:
        copy.wait()
    def spread_scalar(x):
        return jnp.full((NROW, LANES), x, F32)

    sums = [jnp.zeros((NROW, LANES), F32) for _ in range(3)]
    for k in range(NK):
        half, slope, keep, cond, rev, weight = [spread_scalar(raw[j, 0, k]) for j in range(6)]
        inv_slope, inv_cond = 0.5 / slope, 1.0 / cond
        entries = (
            inv_slope,
            -half * inv_slope,
            keep,
            0.5 * cond * (1.0 - keep),
            rev,
            keep * cond,
            -0.5 * keep * cond,
            inv_cond,
            weight * inv_cond,
        )
        for j, entry in enumerate(entries):
            par[j, k] = entry
        par[10, k] = weight * inv_cond * keep
        par[11, k] = 0.5 * weight * (1.0 - keep)
        sums = [sums[0] + 0.5 * cond, sums[1] + 0.5 * cond * rev, sums[2] + 0.5 * weight]
    for j in range(3):
        par[9, j] = sums[j]

    moments_opening()
    for g in range(GROUPS):
        load_group(g).wait()
        planes(0, g * GP, (g + 1) * GP, opening=True)

    tri = jnp.where((iota((LANES, 256), 0) < iota((LANES, 256), 1)), 1.0, 0.0).astype(BF16)
    carry = jnp.zeros((count, LANES), F32)
    for r in range(NROW):
        hot = jnp.broadcast_to(routes[r : r + 1, :], (count, LANES)) == iota((count, LANES), 0)
        hot_f = jnp.where(hot, 1.0, 0.0)
        hot_b = hot_f.astype(BF16)
        tbuf[:, r * LANES : (r + 1) * LANES] = hot_b
        run = dot(hot_b, tri)
        before = run[:, :LANES] + carry
        carry = carry + run[:, LANES:]
        posb[r : r + 1, :] = jnp.sum(before * hot_f, axis=0, keepdims=True).astype(jnp.int32)

    slot_row = lax.rem(iota((LANES, LANES), 0), MOST)

    def here(r):
        return jnp.broadcast_to(posb[r : r + 1, :], (LANES, LANES)) == slot_row

    def placed():
        return dot(tbuf[...], lhi[...], NT) + dot(tbuf[...], llo[...], NT)

    for r in range(NROW):
        row = jnp.broadcast_to(base[r : r + 1, :], (LANES, LANES))
        h, l = split2(jnp.where(here(r), row, 0.0))
        lhi[:, r * LANES : (r + 1) * LANES] = h
        llo[:, r * LANES : (r + 1) * LANES] = l
    snd2[:, 1, :] = placed()


    met(0)
    meet(1)
    finish_halo(0)
    ghost_a_rows(0)
    start_halo(1)
    planes(1, 0, PX)
    met(1)
    meet(2)

    ghost_a(0)
    finish_halo(1)
    start_halo(2)
    planes(2, 0, PX, carry=True)
    met(2)
    meet(3)

    zi, zj = iota((LANES, 256), 0), iota((LANES, 256), 1)
    wz[...] = jnp.where(
        zi // BE == lax.rem(zj, 32), corner_weight(lax.rem(zi, BE), zj // LANES), 0.0
    ).astype(BF16)
    pi, pj = iota((32, 64), 0), iota((32, 64), 1)
    wp = jnp.where(pi // 16 == pj // 32, corner_weight(lax.rem(pi, BE), (pj // 16) % 2), 0.0).astype(BF16)
    ti, tj = iota((64, 32), 0), iota((64, 32), 1)
    wpt = jnp.where(tj // 16 == ti // 32, corner_weight(lax.rem(tj, BE), (ti // 16) % 2), 0.0).astype(BF16)
    band = (iota((256, 256), 0) % 16) // BE == (iota((256, 256), 1) // 32) % BE
    ghost_b(0)
    finish_halo(2)
    start_halo(3)
    planes(3, 0, PX, tension=True)

    for r in range(NROW):
        a, bh = r // 2, r % 2
        for x in range(2):
            acc = None
            for i in range(BE):
                share = (i + 0.5) / BE
                term = tens[BE * a + i, bh * 16 : (bh + 1) * 16, :] * (
                    (share if x else 1.0 - share) / (BE / 2.0) ** 3
                )
                acc = term if acc is None else acc + term
            txb[r * 32 + x * 16 : r * 32 + (x + 1) * 16, :] = acc
    h, l = split2(txb[...])
    along = jnp.where(band, dot(h, wz[...]) + dot(l, wz[...]), 0.0)
    for r in range(NROW):
        h, l = split2(along[r * 32 : (r + 1) * 32])
        both = dot(wpt, h) + dot(wpt, l)
        full = jnp.concatenate([both[:, :LANES], both[:, LANES:]], axis=0)
        h, l = split2(jnp.where(here(r), full, 0.0))
        lhi[:, r * LANES : (r + 1) * LANES] = h
        llo[:, r * LANES : (r + 1) * LANES] = l
    snd2[:, 0, :] = placed()
    met(3)
    send_rows(0)

    planes(3, 0, PX)
    finish_halo(3)
    start_halo(4)

    for copy in small[9:]:
        copy.wait()
    row8, block = iota((NROW, LANES), 0), iota((NROW, LANES), 1) // MOST
    for t in range(count // NROW):
        x = nodes[:, t * LANES : (t + 1) * LANES]
        for bit in (1, 2, 4):
            up = pltpu.roll(pltpu.roll(x, NROW - bit, 0), MOST * bit, 1)
            down = pltpu.roll(pltpu.roll(x, bit, 0), LANES - MOST * bit, 1)
            row_bit, block_bit = (row8 // bit) % 2, (block // bit) % 2
            x = jnp.where(row_bit < block_bit, up, jnp.where(row_bit > block_bit, down, x))
        nlo[t * NROW : (t + 1) * NROW, :] = lax.rem(x, LANES)
        nhi[t * NROW : (t + 1) * NROW, :] = x // LANES

    def hot_chunk(ch, c):
        for j in range(16):
            row = nlo[pl.ds(ch * 16 + j, 1), :]
            hit = jnp.broadcast_to(row, (LANES, LANES)) == iota((LANES, LANES), 0)
            onehot[ch, :, j * LANES : (j + 1) * LANES] = jnp.where(hit, 1.0, 0.0).astype(BF16)
        return c

    lax.fori_loop(0, 8, hot_chunk, 0)
    rd = jnp.where(iota((24, 384), 0) == iota((24, 384), 1) // MOST, 1.0, 0.0).astype(BF16)
    rdt = jnp.where(iota((384, 24), 1) == iota((384, 24), 0) // MOST, 1.0, 0.0).astype(BF16)
    rj = jnp.where(iota((LANES, 8), 1) == corner_of(iota((LANES, 8), 0) // MOST), 1.0, 0.0).astype(BF16)
    rjt = jnp.where(iota((8, LANES), 0) == corner_of(iota((8, LANES), 1) // MOST), 1.0, 0.0).astype(BF16)

    def kron(left, part, right, rows, cols, dims=NT):
        full = dot(dot(left, part, dims).astype(BF16), right)
        same = lax.rem(iota((rows, cols), 0), MOST) == lax.rem(iota((rows, cols), 1), MOST)
        return jnp.where(same, full, 0.0).astype(BF16)

    for s, part in enumerate(split2(fmap[...])):
        kf[s] = kron(rj, part, rd, LANES, 384, NN)
    for s, part in enumerate(split2(stiff[...])):
        ks[s] = kron(rdt, part, rd, 384, 384)
    for s, part in enumerate(split2(smap[...])):
        kt[s] = kron(rdt, part, rjt, 384, LANES)
    eye = jnp.where(iota((24, 24), 0) == iota((24, 24), 1), stiff[...], 0.0)
    dh, dl = split2(jnp.broadcast_to(jnp.sum(eye, axis=0, keepdims=True), (8, 24)))
    dvec[...] = dot(dh, rd) + dot(dl, rd)
    mean8 = jnp.where(
        lax.rem(iota((LANES, LANES), 0), MOST) == lax.rem(iota((LANES, LANES), 1), MOST), 0.125, 0.0
    ).astype(BF16)
    pair = jnp.where(
        jnp.broadcast_to(perm[...], (LANES, LANES)) == iota((LANES, LANES), 0), 1.0, 0.0
    ).astype(BF16)
    back = dot(iota((8, LANES), 1).astype(F32).astype(BF16), pair, NT).astype(jnp.int32)


    def spread(comps):
        rows = 2 * comps * NROW
        for c in range(comps):
            h, l = split2(vals[c])
            vsp[0, c] = h.astype(F32)
            vsp[1, c] = l.astype(F32)

        def chunk(ch, acc):
            for j in range(16):
                p = ch * 16 + j
                hit = jnp.broadcast_to(nhi[pl.ds(p, 1), :], (NROW, LANES)) == iota((NROW, LANES), 0)
                column = []
                for s in range(2):
                    for c in range(comps):
                        row = jnp.broadcast_to(vsp[s, c, pl.ds(p, 1), :], (NROW, LANES))
                        column.append(jnp.where(hit, row, 0.0))
                abuf[0:rows, j * LANES : (j + 1) * LANES] = jnp.concatenate(column, axis=0).astype(BF16)
            return acc + dot(abuf[0:rows, :], onehot[ch], NT)

        acc = lax.fori_loop(0, 8, chunk, jnp.zeros((rows, LANES), F32))
        both = acc[: rows // 2] + acc[rows // 2 :]
        for c in range(comps):
            ndb[c] = both[c * NROW : (c + 1) * NROW]

    def shared(s, to):
        peer = me - 1 if to == 0 else me + 1
        return pltpu.make_async_remote_copy(
            src_ref=asm_s.at[s, to],
            dst_ref=asm_r.at[s, to],
            send_sem=ass.at[s, to],
            recv_sem=asr.at[s, to],
            device_id=(peer // n_four, lax.rem(peer, n_four)),
            device_id_type=MESH,
        )

    has_before, has_after = me > 0, me < count - 1

    def assemble(s, comps):
        lead = jnp.concatenate([ndb[c, 0:1, :] for c in range(comps)] + [jnp.zeros((NROW - comps, LANES), F32)], axis=0)
        trail = jnp.concatenate(
            [ndb[c, NROW - 1 :, :] for c in range(comps)] + [jnp.zeros((NROW - comps, LANES), F32)], axis=0
        )
        asm_s[s, 0] = jnp.take_along_axis(lead, back, axis=1)
        asm_s[s, 1] = trail

        @pl.when(has_before)
        def _():
            shared(s, 0).start()

        @pl.when(has_after)
        def _():
            shared(s, 1).start()

        @pl.when(has_after)
        def _():
            shared(s, 0).wait_recv()
            for c in range(comps):
                ndb[c, NROW - 1 :, :] = ndb[c, NROW - 1 :, :] + asm_r[s, 0, c : c + 1, :]

        @pl.when(has_before)
        def _():
            shared(s, 1).wait_recv()
            order = jnp.broadcast_to(perm[...], (NROW, LANES))
            got = jnp.take_along_axis(asm_r[s, 1], order, axis=1)
            for c in range(comps):
                ndb[c, 0:1, :] = ndb[c, 0:1, :] + got[c : c + 1]

        @pl.when(has_before)
        def _():
            shared(s, 0).wait_send()

        @pl.when(has_after)
        def _():
            shared(s, 1).wait_send()

    def collect(table):
        def tiles(g, carry_in):
            for j in range(4):
                rows = pl.ds(g * 32 + j * NROW, NROW)
                low, high = nlo[rows, :], nhi[rows, :]
                masks = [high == hi for hi in range(NROW)]
                for c in range(3):
                    out = jnp.zeros((NROW, LANES), F32)
                    for hi in range(NROW):
                        line = jnp.broadcast_to(ndb[6 + c, hi : hi + 1, :], (NROW, LANES))
                        out = jnp.where(masks[hi], jnp.take_along_axis(line, low, axis=1), out)
                    vals[c, rows, :] = out
            return carry_in

        for c in range(3):
            ndb[6 + c] = table[c]
        lax.fori_loop(0, 4, tiles, 0)
        return jnp.concatenate([vals[0], vals[1], vals[2]], axis=1)

    def times(x, table):
        h, l = split2(x)
        return dot(h, table[0]) + dot(l, table[0]) + dot(h, table[1])


    wait_rows(0)
    arrived = rcv2[:, 0, :]
    h, l = split2(arrived)
    k8 = rcv2[:, 1, :] * (1.0 + 0.5 * jnp.tanh(dot(h, mean8) + dot(l, mean8)))
    k8b[...] = k8
    force = times(arrived, kf)
    for c in range(3):
        part = slice(c * LANES, (c + 1) * LANES)
        vals[c] = force[:, part]
        vals[3 + c] = k8 * dvec[0:1, part]
    spread(6)
    assemble(0, 6)
    forces = [ndb[c] for c in range(3)]
    diagonal = [SPRING + ndb[3 + c] for c in range(3)]
    guess = [RELAX * f / d for f, d in zip(forces, diagonal)]
    pushed = times(collect(guess), ks)
    for c in range(3):
        vals[c] = k8b[...] * pushed[:, c * LANES : (c + 1) * LANES]
    spread(3)
    assemble(1, 3)
    moved = []
    for c in range(3):
        applied = SPRING * guess[c] + ndb[c]
        moved.append(guess[c] + RELAX * (forces[c] - applied) / diagonal[c])
        for hi in range(NROW):
            disp_out[c : c + 1, hi * LANES : (hi + 1) * LANES] = moved[c][hi : hi + 1]
    strain = times(collect(moved), kt)
    snd1[...] = strain.reshape(count, 1, LANES)
    send_rows(1)
    planes(4, 0, PX)
    moments_later()
    finish_halo(4)
    wait_rows(1)

    h, l = split2(rcv1[...].reshape(count, LANES).T)
    mine = dot(h, tbuf[...]) + dot(l, tbuf[...])
    for r in range(NROW):
        own = jnp.where(here(r), mine[:, r * LANES : (r + 1) * LANES], 0.0)
        h, l = split2(jnp.concatenate([own[:64], own[64:]], axis=1))
        along = jnp.where(band[:32], dot(wp, h) + dot(wp, l), 0.0)
        h, l = split2(along)
        fine = dot(h, wz[...], NT) + dot(l, wz[...], NT)
        a, bh = r // 2, r % 2
        for i in range(BE):
            share = (i + 0.5) / BE
            ex[BE * a + i, bh * 16 : (bh + 1) * 16, :] = (1.0 - share) * fine[:16] + share * fine[16:]

    def add_excess(i, c):
        vb[4, i] = vb[4, i] - (DT * GAIN) * ex[i] * (vb[3, i] - STRETCH_REV)
        return c

    lax.fori_loop(0, PX, add_excess, 0)
    start_halo(5)
    cross(1, 0, 3, 1, 4)
    planes(5, 0, PX, with_excess=True)
    finish_halo(5)
    ghost_a_rows(1)
    start_halo(6)
    planes(6, 0, PX, with_excess=True)
    ghost_a(1)
    finish_halo(6)
    start_halo(7)

    planes(7, 0, PX, with_excess=True, closing=True)
    ghost_b(1)
    for n in range(7):
        finish_sends(n)
    ghost_sent()
    for s in range(2):
        wait_sent(s)
    finish_halo(7)
    finish_sends(7)


def put_out(pot, states, disp, pot_out, states_out, disp_out, sem):
    copies = [
        pltpu.make_async_copy(src, dst, sem.at[i])
        for i, (src, dst) in enumerate(((states, states_out), (pot, pot_out), (disp, disp_out)))
    ]
    for copy in copies:
        copy.start()
    for copy in copies:
        copy.wait()


def in_hbm(x):
    return pltpu.with_memory_space_constraint(x, pltpu.HBM)


def per_device(
    n_wide,
    n_four,
    voltage,
    states,
    half_volt,
    gate_slope,
    retention,
    conduct,
    reversal,
    tension_weights,
    routes,
    base_stiff,
    elem_nodes,
    share_perm,
    stiffness,
    force_map,
    strain_map,
):
    count = n_wide * n_four
    vmem = pl.BlockSpec(memory_space=pltpu.VMEM)
    hbm = pl.BlockSpec(memory_space=pltpu.HBM)
    scratch = [
        pltpu.SMEM((6, 1, NK), F32),
        pltpu.VMEM((12, NK, NROW, LANES), F32),
        pltpu.VMEM((PX, PY, PZ), F32),
        pltpu.VMEM((NROW, LANES), jnp.int32),
        pltpu.VMEM((NROW, LANES), F32),
        pltpu.VMEM((8, count * MOST), jnp.int32),
        pltpu.VMEM((1, LANES), jnp.int32),
        pltpu.VMEM((24, 24), F32),
        pltpu.VMEM((8, 24), F32),
        pltpu.VMEM((8, 24), F32),
        pltpu.VMEM((NK, PX, PY, PZ), F32),
        pltpu.VMEM((7, PX, PY, PZ), F32),
        pltpu.VMEM((8, 2, PY, PZ), F32),
        pltpu.VMEM((8, 2, PX, PZ), F32),
        pltpu.VMEM((8, 2, PX, PZ), F32),
        pltpu.VMEM((PX, PY, PZ), F32),
        pltpu.VMEM((PX, PY, PZ), F32),
        pltpu.VMEM((count, 1024), BF16),
        pltpu.VMEM((NROW, LANES), jnp.int32),
        pltpu.VMEM((LANES, 1024), BF16),
        pltpu.VMEM((LANES, 1024), BF16),
        pltpu.VMEM((8, LANES, 2048), BF16),
        pltpu.VMEM((96, 2048), BF16),
        pltpu.VMEM((2, 6, count, LANES), F32),
        pltpu.VMEM((count, LANES), jnp.int32),
        pltpu.VMEM((count, LANES), jnp.int32),
        pltpu.VMEM((2, LANES, 384), BF16),
        pltpu.VMEM((2, 384, 384), BF16),
        pltpu.VMEM((2, 384, LANES), BF16),
        pltpu.VMEM((8, 384), F32),
        pltpu.VMEM((LANES, 256), BF16),
        pltpu.VMEM((count, LANES), F32),
        pltpu.VMEM((256, LANES), F32),
        pltpu.VMEM((6, count, LANES), F32),
        pltpu.VMEM((9, NROW, LANES), F32),
        pltpu.VMEM((2, 2, NROW, LANES), F32),
        pltpu.VMEM((2, 2, NROW, LANES), F32),
        pltpu.VMEM((count, 2, LANES), F32),
        pltpu.VMEM((count, 2, LANES), F32),
        pltpu.VMEM((count, 1, LANES), F32),
        pltpu.VMEM((count, 1, LANES), F32),
        pltpu.SemaphoreType.DMA((GROUPS,)),
        pltpu.SemaphoreType.DMA((14,)),
        pltpu.SemaphoreType.DMA((8, 4)),
        pltpu.SemaphoreType.DMA((8, 4)),
        pltpu.SemaphoreType.DMA((2,)),
        pltpu.SemaphoreType.DMA((2,)),
        pltpu.SemaphoreType.DMA((2, 2)),
        pltpu.SemaphoreType.DMA((2, 2)),
        pltpu.SemaphoreType.REGULAR((4,)),
        pltpu.VMEM((NK, 2, PY, PZ), F32),
        pltpu.SemaphoreType.DMA(()),
        pltpu.VMEM((2, 6, PY, PZ), F32),
        pltpu.VMEM((2, 6, PY, PZ), F32),
        pltpu.VMEM((2, 2, PY, PZ), F32),
        pltpu.VMEM((2, PY, PZ), F32),
        pltpu.VMEM((3, PY, PZ), F32),
        pltpu.VMEM((6, 2, 1, LANES), F32),
        pltpu.VMEM((6, 4, 1, LANES), F32),
        pltpu.SemaphoreType.DMA((2, 5)),
        pltpu.SemaphoreType.DMA((2, 5)),
        pltpu.SemaphoreType.DMA((6, 2)),
        pltpu.SemaphoreType.DMA((6, 2)),
    ]
    made = pl.pallas_call(
        functools.partial(kernel, n_wide, n_four),
        out_shape=(
            jax.ShapeDtypeStruct((PX, PY, PZ), F32),
            jax.ShapeDtypeStruct((NK, PX, PY, PZ), F32),
            jax.ShapeDtypeStruct((3, NROW * LANES), F32),
        ),
        in_specs=[[hbm] * 6] + [hbm] * 9,
        out_specs=(vmem, vmem, vmem),
        scratch_shapes=scratch,
        compiler_params=pltpu.CompilerParams(
            collective_id=0, has_side_effects=True, vmem_limit_bytes=40 << 20
        ),
    )(
        [
            in_hbm(x.reshape(1, NK))
            for x in (half_volt, gate_slope, retention, conduct, reversal, tension_weights)
        ],
        in_hbm(voltage),
        in_hbm(states),
        in_hbm(routes.reshape(NROW, LANES)),
        in_hbm(base_stiff.reshape(NROW, LANES)),
        in_hbm(elem_nodes),
        in_hbm(share_perm),
        in_hbm(stiffness),
        in_hbm(force_map.T),
        in_hbm(strain_map),
    )
    return pl.pallas_call(
        put_out,
        out_shape=[jax.ShapeDtypeStruct(x.shape, x.dtype) for x in made],
        in_specs=[vmem] * 3,
        out_specs=[hbm] * 3,
        scratch_shapes=[pltpu.SemaphoreType.DMA((3,))],
        compiler_params=pltpu.CompilerParams(vmem_limit_bytes=1 << 20),
    )(*made)


def solution(mesh):
    placed = (
        P("wide", "four", None),
        P(None, "wide", "four", None),
        P(),
        P(),
        P(),
        P(),
        P(),
        P(),
        P(("wide", "four"), None),
        P(("wide", "four")),
        P(None, ("wide", "four")),
        P(("wide", "four"), None),
        P(),
        P(),
        P(),
    )
    return jax.shard_map(
        functools.partial(per_device, mesh.shape["wide"], mesh.shape["four"]),
        mesh=mesh,
        in_specs=placed,
        out_specs=(
            P("wide", "four", None),
            P(None, "wide", "four", None),
            P(None, ("wide", "four")),
        ),
        check_vma=False,
    )
```
